256 devices in a mesh: rows: 128 (over x, z, y), cols: 2 (over core).
Axes of the slice: x: 4, y: 4, z: 8, core: 2. Of those that a mesh axis runs over, the one named last changes fastest.
Arguments:
- embeddings: bfloat16 [262144, 384], P('rows')
- test_matrix: bfloat16 [262144, 64], P('rows'), may hold values from -6 to 6
- pair_list: int32 [1024, 2], P(('rows', 'cols')), may hold values from -1 to 255, as said below
Outputs:
- orthonormal_basis: float32 [262144, 64], P(('rows', 'cols'))
- upper_factor: float32 [64, 64], replicated
The draws below stay inside these ranges and needn't reach their ends.
Inputs may be any that keep to these rules, and one draw needn't show every extreme that they name: `pair_list`: device (r, c) holds 4 entries. Its live entries come first: pairs (i, j) with r * 2 <= i < (r + 1) * 2 and i <= j < min((r + 3) * 2, 256); each pair appears at most once over all devices; its other entries are -1 in both places. The device with c = 0 holds at least one live pair, the two devices of one r hold at most 4 together, and device (0, 0) holds exactly 4.
All inputs are finite; a program needn't handle non-finite values.
Results may differ from the reference program's by a relative error of at most 0.0053.
Values may be sent and summed in bfloat16 or wider, within the bound.
No kernel may reach another device: no remote copies, remote signals or barrier semaphores. Data moves between devices by JAX's collectives and lax.ppermute only.
A program may use at most 64 MiB of HBM per device.

```python
import jax
import jax.numpy as jnp
import numpy as np
from jax import lax

E = 384
K = 64
BLK = 1024
BLK_DEV = 2
NB = 256
ROWS_ALL = 262144
PAIRS_DEV = 4


def draw_embeddings(key, part):
    rows_total = NB * BLK
    group_key, member_key, noise_key, center_key = jax.random.split(key, 4)
    row_index = jnp.arange(rows_total, dtype=jnp.int32)
    block_index = row_index // BLK
    group_shift = jax.random.randint(group_key, (rows_total,), 0, 3)
    group_index = (block_index + group_shift) // 3
    member = jax.random.randint(member_key, (rows_total,), 0, BLK)
    cluster = group_index * BLK + member

    def center_of(cluster_id):
        return jax.random.normal(jax.random.fold_in(center_key, cluster_id), (E,), jnp.float32)
    centers = jax.vmap(center_of)(cluster)
    noise = 0.35 * jax.random.normal(noise_key, (rows_total, E), jnp.float32)
    return (centers + noise).astype(jnp.bfloat16)


def draw_pair_list(key, part):
    device_rows = NB // BLK_DEV
    first_offsets = []
    second_offsets = []
    for first_local in range(BLK_DEV):
        for second_local in range(first_local, 3 * BLK_DEV):
            first_offsets.append(first_local)
            second_offsets.append(second_local)
    first_table = jnp.array(np.array(first_offsets, np.int32))
    second_table = jnp.array(np.array(second_offsets, np.int32))
    candidates = len(first_offsets)
    score_key, first_key, second_key = jax.random.split(key, 3)
    base_block = jnp.arange(device_rows, dtype=jnp.int32)[:, None] * BLK_DEV
    usable = base_block + second_table[None, :] < NB
    usable_count = jnp.sum(usable.astype(jnp.int32), axis=1)
    scores = jax.random.randint(score_key, (device_rows, candidates), 0, 2 ** 20) * 256 + jnp.arange(candidates, dtype=jnp.int32)[None, :]
    scores = jnp.where(usable, scores, scores + 2 ** 29)
    ranked = jnp.argsort(scores, axis=1)
    first_most = jnp.minimum(PAIRS_DEV, usable_count)
    first_count = jax.random.randint(first_key, (device_rows,), 1, first_most + 1)
    first_count = first_count.at[0].set(PAIRS_DEV)
    second_count = jax.random.randint(second_key, (device_rows,), 0, first_most - first_count + 1)
    slot_index = jnp.arange(PAIRS_DEV, dtype=jnp.int32)[None, :]
    first_picked = ranked[:, :PAIRS_DEV]
    second_picked = jnp.take_along_axis(ranked, jnp.minimum(first_count[:, None] + slot_index, candidates - 1), axis=1)

    def to_pairs(picked, active):
        first_ids = base_block + first_table[picked]
        second_ids = base_block + second_table[picked]
        pair_rows = jnp.stack([first_ids, second_ids], axis=-1)
        return jnp.where(active[..., None], pair_rows, -1)
    first_pairs = to_pairs(first_picked, slot_index < first_count[:, None])
    second_pairs = to_pairs(second_picked, slot_index < second_count[:, None])
    return jnp.stack([first_pairs, second_pairs], axis=1).reshape(device_rows * 2 * PAIRS_DEV, 2).astype(jnp.int32)


def level_of(stream_key, extent, cuts, least, high):
    gain = 1.0
    for axis_at, blocks in cuts:
        draws = jax.random.uniform(jax.random.fold_in(jax.random.fold_in(stream_key, 6), axis_at), (blocks,), jnp.float32, least / len(cuts), high / len(cuts))
        gain = gain * jnp.repeat(jnp.exp(draws), extent[axis_at] // blocks).reshape((-1,) + (1,) * (len(extent) - 1 - axis_at))
    return gain


def gaussian(own_key, extent, spread, reach, pieces=(), kind=jnp.bfloat16):
    result = spread * jax.random.normal(own_key, extent, jnp.float32)
    if pieces:
        result = result * level_of(own_key, extent, pieces, -0.22, 0.18)
    return jnp.clip(result, -reach, reach).astype(kind)


def setup_inputs(seed: int = 0) -> dict:
    streams_of = jax.random.split(jax.random.key(seed), 4)
    return {
        "embeddings": draw_embeddings(jax.random.fold_in(streams_of[3], 71), 0),
        "test_matrix": gaussian(streams_of[1], (ROWS_ALL, K), 1.0, 6.0, ((0, 128),)),
        "pair_list": draw_pair_list(jax.random.fold_in(streams_of[3], 71), 0),
    }


SHARPNESS = 6.0
EPSILON = 1e-06

def unit_rows(embeddings):
    widened = embeddings.astype(jnp.float32)
    inverse = lax.rsqrt(lax.optimization_barrier(jnp.sum(widened * widened, axis=1, keepdims=True)) + EPSILON)
    return (widened * inverse).astype(jnp.bfloat16)

def affinity(left_rows, right_rows):
    scores = lax.dot_general(left_rows.astype(jnp.float32), right_rows.astype(jnp.float32), (((1,), (1,)), ((), ())), preferred_element_type=jnp.float32)
    return jnp.exp(SHARPNESS * (scores - 1.0)).astype(jnp.bfloat16)

def mirror_product(affinity_tile, vectors):
    return lax.dot_general(affinity_tile.astype(jnp.float32), vectors.astype(jnp.float32), (((0,), (0,)), ((), ())), preferred_element_type=jnp.float32)

def block_at(stacked, index):
    return lax.dynamic_index_in_dim(stacked, index, 0, keepdims=False)

def apply_pairs(normed, vectors, pair_list):

    def pair_step(accumulated, entry):

        def compute(current):
            first_block = entry[0]
            second_block = entry[1]
            affinity_tile = affinity(block_at(normed, first_block), block_at(normed, second_block))
            forward = jnp.dot(affinity_tile.astype(jnp.float32), block_at(vectors, second_block).astype(jnp.float32), preferred_element_type=jnp.float32)
            backward = mirror_product(affinity_tile, block_at(vectors, first_block))
            mirror_weight = (first_block != second_block).astype(jnp.float32)
            current = current.at[first_block].add(forward)
            return current.at[second_block].add(mirror_weight * backward)
        return (lax.cond(entry[0] >= 0, compute, lambda unchanged: unchanged, accumulated), None)
    initial = jnp.zeros((normed.shape[0], normed.shape[1], vectors.shape[2]), jnp.float32)
    accumulated, _ = lax.scan(pair_step, initial, pair_list.astype(jnp.int32))
    return accumulated.reshape(-1, vectors.shape[2])

def orthonormal(sketch_rows):
    gram_matrix = lax.dot_general(sketch_rows.astype(jnp.float32), sketch_rows.astype(jnp.float32), (((0,), (0,)), ((), ())), precision=lax.Precision.HIGHEST, preferred_element_type=jnp.float32) / ROWS_ALL
    lower_factor = jnp.linalg.cholesky(gram_matrix)
    solved = lax.linalg.triangular_solve(lower_factor, sketch_rows, left_side=False, lower=True, transpose_a=True)
    return (solved, lower_factor.T)

def reference(embeddings, test_matrix, pair_list):
    normed = unit_rows(embeddings).reshape(NB, BLK, E)
    sketch_rows = apply_pairs(normed, test_matrix.reshape(NB, BLK, K), pair_list)
    panel_rows, _ = orthonormal(sketch_rows)
    image_rows = apply_pairs(normed, panel_rows.astype(jnp.bfloat16).reshape(NB, BLK, K), pair_list)
    return orthonormal(image_rows)
```

```python
import functools

import jax
import jax.numpy as jnp
from jax import lax
from jax.experimental import pallas as pl
from jax.experimental.pallas import tpu as pltpu
from jax.sharding import PartitionSpec as P

BLK = 1024
HALF = 512
SHARPNESS = 6.0
EPSILON = 1e-06
LOG2E = 1.4426950408889634
HIGHEST = lax.Precision.HIGHEST
VMEM = pl.BlockSpec(memory_space=pltpu.VMEM)
SMEM = pl.BlockSpec(memory_space=pltpu.SMEM)
NT = (((1,), (1,)), ((), ()))
NN = (((1,), (0,)), ((), ()))
ACROSS, PLANES, RING = 4, 8, 4


def call(kernel, outs, flops, moved, exps=0):
    return functools.partial(
        pl.pallas_call,
        kernel,
        out_shape=outs,
        out_specs=jax.tree.map(lambda _: VMEM, outs),
        compiler_params=pltpu.CompilerParams(vmem_limit_bytes=48 * 1024 * 1024),
        cost_estimate=pl.CostEstimate(flops=flops, bytes_accessed=moved, transcendentals=exps),
    )


def shape(dims, dtype=jnp.float32):
    return jax.ShapeDtypeStruct(dims, dtype)


def dot(left, right, dims, precision=None):
    return lax.dot_general(
        left, right, dims, precision=precision, preferred_element_type=jnp.float32
    )


def unit_kernel(relative, core_ref, rows_ref, unit_ref):
    core = core_ref[0]
    side = core if relative == 0 else 1 - core
    for block in range(2):
        start = pl.multiple_of(block * BLK + side * HALF, HALF)
        widened = rows_ref[pl.ds(start, HALF), :].astype(jnp.float32)
        inverse = lax.rsqrt(jnp.sum(widened * widened, axis=1, keepdims=True) + EPSILON)
        unit_ref[block] = (widened * inverse).astype(jnp.bfloat16)


def affinity_tile(left, right):
    scores = dot(left, right, NT)
    return jnp.exp2((SHARPNESS * LOG2E) * scores - (SHARPNESS * LOG2E)).astype(jnp.bfloat16)


def fold(product):
    if product.shape[0] == 128:
        return product[:64] + product[64:]
    return product


def make_tiles(left, rights, tile_ref, slot):
    for side in range(2):
        for at in range(0, HALF, 256):
            tile_ref[slot, side, :, at : at + 256] = affinity_tile(
                left, rights[side][at : at + 256]
            )


def use_tiles(tile_ref, slot, ahead, behind, forward_ref, forward_at, mirror_ref, mirror_at, mirror):
    total = fold(dot(ahead[0], tile_ref[slot, 0], NT)) + fold(dot(ahead[1], tile_ref[slot, 1], NT))
    forward_ref[forward_at] += total

    def put_mirror():
        for side in range(2):
            mirror_ref[side, mirror_at] += fold(dot(behind, tile_ref[slot, side], NN))

    if mirror is None:
        put_mirror()
    else:
        pl.when(mirror)(put_mirror)


def local_kernel(make, flags_ref, *refs):
    if make:
        unit0, unit1, vec0, vec1, tile_ref, forward_ref, mirror_ref = refs
    else:
        tile_ref, vec0, vec1, forward_ref, mirror_ref = refs
    forward_ref[...] = jnp.zeros_like(forward_ref)
    mirror_ref[...] = jnp.zeros_like(mirror_ref)

    @pl.loop(0, 3)
    def _(slot):
        first, second = slot // 2, (slot + 1) // 2

        @pl.when(flags_ref[slot] > 0)
        def _():
            if make:
                make_tiles(unit0[first], (unit0.at[second], unit1.at[second]), tile_ref, slot)
            use_tiles(
                tile_ref, slot, (vec0[second], vec1[second]), vec0[first],
                forward_ref, first, mirror_ref, second, slot == 1,
            )


def near_kernel(make, flags_ref, *refs):
    if make:
        (unit0, unit_prev, next0, next1, vec0, vec_prev, vnext0, vnext1, started,
         tile_ref, forward_ref, before_ref, mirror_ref) = refs
    else:
        (tile_ref, vec0, vec_prev, vnext0, vnext1, started,
         forward_ref, before_ref, mirror_ref) = refs
    forward_ref[...] = started[...]
    before_ref[...] = jnp.zeros_like(before_ref)
    mirror_ref[...] = jnp.zeros_like(mirror_ref)
    for kind in range(2):

        @pl.loop(0, 4)
        def _(index):
            first, second = index // 2, index % 2
            slot = kind * 4 + index

            @pl.when(flags_ref[3 + slot] > 0)
            def _():
                if make:
                    left = (unit0, unit_prev)[kind][first]
                    make_tiles(left, (next0.at[second], next1.at[second]), tile_ref, slot)
                use_tiles(
                    tile_ref, slot, (vnext0[second], vnext1[second]), (vec0, vec_prev)[kind][first],
                    (forward_ref, before_ref)[kind], first, mirror_ref, second, None,
                )


def total_kernel(forward, mirror_mine, mirror_other, from_next, from_prev, sum_ref, pair_ref=None):
    for block in range(2):
        value = (
            forward[block] + mirror_mine[0, block] + mirror_other[block]
            + from_next[block] + from_prev[block]
        )
        sum_ref[block] = value
        if pair_ref is not None:
            high = value.astype(jnp.bfloat16)
            pair_ref[block, :64] = high
            pair_ref[block, 64:] = (value - high.astype(jnp.float32)).astype(jnp.bfloat16)


def gram_of(value_ref, scale):
    gram = dot(value_ref[0], value_ref[0], NT, HIGHEST) + dot(value_ref[1], value_ref[1], NT, HIGHEST)
    gram = gram * scale
    return jnp.concatenate([gram[:32], gram[32:]], axis=1)


def gram_kernel(scale, value_ref, gram_ref):
    gram_ref[...] = gram_of(value_ref, scale)


def second_gram_kernel(scale, core_ref, first_ref, value_ref, keep_ref, give_ref, swap_ref):
    second = gram_of(value_ref, scale)
    first = first_ref[...]
    lead = core_ref[0] == 0
    keep_ref[...] = jnp.where(lead, first, second)
    give_ref[...] = jnp.where(lead, second, first)
    swap_ref[...] = value_ref[1 - core_ref[0]]


def eliminate(packed):
    lanes = lax.broadcasted_iota(jnp.int32, (8, 64), 1)
    subs = lax.broadcasted_iota(jnp.int32, (8, 64), 0)
    sub1 = lax.broadcasted_iota(jnp.int32, (8, 1), 0)
    states = []
    for matrix in packed:
        whole = jnp.concatenate([matrix[:, :64], matrix[:, 64:]], axis=0)
        states.append([
            jnp.concatenate(
                [whole[8 * b : 8 * b + 8], (lanes == subs + 8 * b).astype(jnp.float32)], axis=1
            )
            for b in range(8)
        ])
    for k in range(64):
        at, sub = k // 8, k % 8
        for state in states:
            row = state[at][sub : sub + 1, :]
            scaled = row / state[at][sub : sub + 1, k : k + 1]
            for b in range(at, 8):
                column = state[b][:, k : k + 1]
                if b == at:
                    column = jnp.where(sub1 > sub, column, 0.0)
                state[b] = state[b] - column * scaled
    uppers, inverses = [], []
    for state in states:
        rows = []
        for b in range(8):
            diagonal = jnp.sum(
                jnp.where(lanes == subs + 8 * b, state[b][:, :64], 0.0), axis=1, keepdims=True
            )
            rows.append(state[b] * lax.rsqrt(diagonal))
        whole = jnp.concatenate(rows, axis=0)
        uppers.append(whole[:, :64])
        inverses.append(whole[:, 64:])
    return uppers, inverses


def finish_kernel(core_ref, mine_ref, other_ref, value_ref, got_ref, basis_ref, factor_ref):
    core = core_ref[0]
    lead = core == 0
    mine, other = mine_ref[...], other_ref[...]
    first, second = jnp.where(lead, mine, other), jnp.where(lead, other, mine)
    uppers, inverses = eliminate([first, second])
    factor = dot(uppers[1], inverses[0], NT, HIGHEST)
    wide = lax.broadcasted_iota(jnp.int32, (64, 64), 1)
    tall = lax.broadcasted_iota(jnp.int32, (64, 64), 0)
    factor_ref[...] = jnp.where(wide >= tall, factor, 0.0)
    low = jnp.where(wide <= tall, inverses[1], 0.0)
    here = pl.multiple_of(core * HALF, HALF)
    there = pl.multiple_of((1 - core) * HALF, HALF)
    basis_ref[:, pl.ds(here, HALF)] = dot(low, value_ref[core], NN, HIGHEST)
    basis_ref[:, pl.ds(there, HALF)] = dot(low, got_ref[...], NN, HIGHEST)


def step_rows(value, steps):
    count = lax.axis_size("rows")
    return lax.ppermute(value, "rows", [(r, (r + steps) % count) for r in range(count)])


def swap(value):
    return lax.ppermute(value, "cols", [(0, 1), (1, 0)])


def live_flags(pair_list, base):
    own = jnp.concatenate([pair_list, swap(pair_list)], axis=0)
    before = step_rows(own, 1)

    def any_of(entries, pairs):
        table = jnp.array(pairs, jnp.int32) + base
        hit = (entries[None, :, :] == table[:, None, :]).all(axis=2)
        live = entries[None, :, 0] >= 0
        return jnp.any(hit & live, axis=1)

    ours = [(0, 0), (0, 1), (1, 1), (0, 2), (0, 3), (1, 2), (1, 3)]
    across = [(-2, 2), (-2, 3), (-1, 2), (-1, 3)]
    return jnp.concatenate([any_of(own, ours), any_of(before, across)]).astype(jnp.int32)


def spread(forward, before, mirror_own, mirror_next):
    from_next = step_rows(before, -1)
    other_own = swap(mirror_own[1])
    other_next = swap(mirror_next[1])
    from_prev = step_rows(mirror_next[0] + other_next, 1)
    return forward, mirror_own, other_own, from_next, from_prev


def sum_over_chips(value):
    count = lax.axis_size("rows")
    planes = [[(x * PLANES + z) * RING + y for x in range(ACROSS) for y in range(RING)] for z in range(PLANES)]
    lines = [[(x * PLANES + z) * RING + y for z in range(PLANES)] for x in range(ACROSS) for y in range(RING)]
    for groups in (planes, lines):
        size = len(groups[0])
        copies = jnp.broadcast_to(value[None], (size,) + value.shape)
        value = lax.all_to_all(copies, "rows", 0, 0, axis_index_groups=groups, tiled=True).sum(0)
    return value


def local(embeddings, test_matrix, pair_list):
    rows_dev = embeddings.shape[0]
    columns = test_matrix.shape[1]
    bf16, f32 = jnp.bfloat16, jnp.float32
    core = lax.axis_index("cols").astype(jnp.int32)
    core_ref = core.reshape(1)
    base = (lax.axis_index("rows") * 2).astype(jnp.int32)
    scale = 1.0 / (rows_dev * lax.axis_size("rows"))

    def unit(relative):
        return call(
            functools.partial(unit_kernel, relative), shape((2, HALF, 384), bf16), 2**20, 2**21
        )(in_specs=[SMEM, VMEM])(core_ref, embeddings)

    unit0 = unit(0)
    unit_prev = step_rows(unit0, 1)
    next0 = step_rows(unit0, -1)
    flags = live_flags(pair_list, base)
    turned = test_matrix.T.reshape(columns, 2, 2, HALF).transpose(2, 1, 0, 3)
    vec0 = lax.dynamic_index_in_dim(turned, core, 0, keepdims=False)
    vec1 = lax.dynamic_index_in_dim(turned, 1 - core, 0, keepdims=False)
    vec_prev = step_rows(vec0, 1)
    vnext0 = step_rows(vec0, -1)
    vnext1 = swap(vnext0)
    unit1 = unit(1)
    next1 = swap(next0)

    sum_shape, mirror_shape = shape((2, 64, HALF)), shape((2, 2, 64, HALF))
    tiles_own, forward, mirror_own = call(
        functools.partial(local_kernel, True),
        (shape((3, 2, HALF, HALF), bf16), sum_shape, mirror_shape),
        2 * 10**9, 4 * 10**6, 10**6,
    )(in_specs=[SMEM] + [VMEM] * 4)(flags, unit0, unit1, vec0, vec1)
    tiles_near, forward, before, mirror_next = call(
        functools.partial(near_kernel, True),
        (shape((8, 2, HALF, HALF), bf16), sum_shape, sum_shape, mirror_shape),
        4 * 10**9, 8 * 10**6, 2 * 10**6,
    )(in_specs=[SMEM] + [VMEM] * 9)(
        flags, unit0, unit_prev, next0, next1, vec0, vec_prev, vnext0, vnext1, forward
    )
    sketch, pair0 = call(total_kernel, (sum_shape, shape((2, 128, HALF), bf16)), 10**6, 2 * 10**6)(
        in_specs=[VMEM] * 5
    )(*spread(forward, before, mirror_own, mirror_next))

    pair_prev = step_rows(pair0, 1)
    pnext0 = step_rows(pair0, -1)
    pair1 = swap(pair0)
    pnext1 = swap(pnext0)
    gram_shape = shape((32, 128))
    first_gram = call(functools.partial(gram_kernel, scale), gram_shape, 10**8, 10**6)(
        in_specs=[VMEM]
    )(sketch)
    forward, mirror_own = call(
        functools.partial(local_kernel, False), (sum_shape, mirror_shape), 10**9, 3 * 10**6
    )(in_specs=[SMEM] + [VMEM] * 3)(flags, tiles_own, pair0, pair1)
    forward, before, mirror_next = call(
        functools.partial(near_kernel, False), (sum_shape, sum_shape, mirror_shape), 10**9, 8 * 10**6
    )(in_specs=[SMEM] + [VMEM] * 6)(flags, tiles_near, pair0, pair_prev, pnext0, pnext1, forward)
    image = call(total_kernel, sum_shape, 10**6, 2 * 10**6)(in_specs=[VMEM] * 5)(
        *spread(forward, before, mirror_own, mirror_next)
    )
    keep, give, half = call(
        functools.partial(second_gram_kernel, scale),
        (gram_shape, gram_shape, shape((64, HALF))),
        10**8, 10**6,
    )(in_specs=[SMEM, VMEM, VMEM])(core_ref, first_gram, image)
    got = swap(half)
    mine = sum_over_chips(keep + swap(give))
    other = swap(mine)
    basis, factor = call(finish_kernel, (shape((64, BLK)), shape((64, 64))), 10**8, 10**6)(
        in_specs=[SMEM] + [VMEM] * 4
    )(core_ref, mine, other, image, got)
    return basis.T, factor


def solution(mesh):
    in_specs = (P("rows", None), P("rows", None), P(("rows", "cols"), None))
    out_specs = (P(("rows", "cols"), None), P())
    return jax.shard_map(local, mesh=mesh, in_specs=in_specs, out_specs=out_specs, check_vma=False)
```

```python
import functools

import jax
import jax.numpy as jnp
from jax import lax
from jax.experimental import pallas as pl
from jax.experimental.pallas import tpu as pltpu
from jax.sharding import PartitionSpec as P

BLK = 1024
HALF = 512
SHARPNESS = 6.0
EPSILON = 1e-06
LOG2E = 1.4426950408889634
HIGHEST = lax.Precision.HIGHEST
VMEM = pl.BlockSpec(memory_space=pltpu.VMEM)
HBM = pl.BlockSpec(memory_space=pltpu.HBM)
SMEM = pl.BlockSpec(memory_space=pltpu.SMEM)
NT = (((1,), (1,)), ((), ()))
NN = (((1,), (0,)), ((), ()))
ACROSS, PLANES, RING = 4, 8, 4


def call(kernel, outs, flops, moved, exps=0, room=16):
    return functools.partial(
        pl.pallas_call,
        kernel,
        out_shape=outs,
        out_specs=jax.tree.map(lambda _: VMEM, outs),
        compiler_params=pltpu.CompilerParams(vmem_limit_bytes=room * 1024 * 1024),
        cost_estimate=pl.CostEstimate(flops=flops, bytes_accessed=moved, transcendentals=exps),
    )


def shape(dims, dtype=jnp.float32):
    return jax.ShapeDtypeStruct(dims, dtype)


def dot(left, right, dims, precision=None):
    return lax.dot_general(
        left, right, dims, precision=precision, preferred_element_type=jnp.float32
    )


def packet_kernel(relative, core_ref, rows_ref, columns_ref, packet_ref, raw_ref, vec_ref, sems):
    side = core_ref[0] if relative == 0 else 1 - core_ref[0]
    copies = []
    for block in range(2):
        start = pl.multiple_of(block * BLK + side * HALF, HALF)
        copies.append((
            pltpu.make_async_copy(rows_ref.at[pl.ds(start, HALF), :], raw_ref.at[block], sems.at[block]),
            pltpu.make_async_copy(
                columns_ref.at[:, pl.ds(start, HALF)], vec_ref.at[block], sems.at[2 + block]
            ),
        ))
        for copy in copies[-1]:
            copy.start()
    for block in range(2):
        for copy in copies[block]:
            copy.wait()
        widened = raw_ref[block].astype(jnp.float32)
        inverse = lax.rsqrt(jnp.sum(widened * widened, axis=1, keepdims=True) + EPSILON)
        unit = (widened * inverse).astype(jnp.bfloat16)
        for tile in range(3):
            packet_ref[block, HALF * tile : HALF * (tile + 1)] = unit[:, 128 * tile : 128 * (tile + 1)]
        for tile in range(4):
            packet_ref[block, 1536 + 64 * tile : 1600 + 64 * tile] = vec_ref[
                block, :, 128 * tile : 128 * (tile + 1)
            ]


def unit_rows(packet, start, count):
    return jnp.concatenate(
        [packet[HALF * tile + start : HALF * tile + start + count] for tile in range(3)], axis=1
    )


def vectors(packet):
    return jnp.concatenate([packet[1536 + 64 * tile : 1600 + 64 * tile] for tile in range(4)], axis=1)


def affinity_tile(left, right):
    scores = dot(left, right, NT)
    return jnp.exp2((SHARPNESS * LOG2E) * scores - (SHARPNESS * LOG2E)).astype(jnp.bfloat16)


def fold(product):
    if product.shape[0] == 128:
        return product[:64] + product[64:]
    return product


def make_tiles(left, rights, tile_ref, slot):
    whole = unit_rows(left, 0, HALF)
    for side in range(2):
        for at in range(0, HALF, 256):
            tile_ref[slot, side, :, at : at + 256] = affinity_tile(
                whole, unit_rows(rights[side], at, 256)
            )


def use_tiles(tile_ref, slot, ahead, behind, forward_ref, forward_at, mirror_refs, mirror_at, mirror):
    total = fold(dot(ahead[0], tile_ref[slot, 0], NT)) + fold(dot(ahead[1], tile_ref[slot, 1], NT))
    forward_ref[forward_at] += total

    def put_mirror():
        for side in range(2):
            mirror_refs[side][mirror_at] += fold(dot(behind, tile_ref[slot, side], NN))

    if mirror is None:
        put_mirror()
    else:
        pl.when(mirror)(put_mirror)


def local_kernel(make, flags_ref, *refs):
    if make:
        own0, own1, tile_ref, forward_ref, mirror0, mirror1 = refs
    else:
        tile_ref, own0, own1, forward_ref, mirror0, mirror1 = refs
    for ref in (forward_ref, mirror0, mirror1):
        ref[...] = jnp.zeros_like(ref)
    take = vectors if make else (lambda ref: ref[...])

    @pl.loop(0, 3)
    def _(slot):
        first, second = slot // 2, (slot + 1) // 2

        @pl.when(flags_ref[slot] > 0)
        def _():
            if make:
                make_tiles(own0.at[first], (own0.at[second], own1.at[second]), tile_ref, slot)
            use_tiles(
                tile_ref, slot, (take(own0.at[second]), take(own1.at[second])), take(own0.at[first]),
                forward_ref, first, (mirror0, mirror1), second, slot == 1,
            )


def near_kernel(make, flags_ref, *refs):
    if make:
        own0, prev, next0, next1, started, tile_ref, forward_ref, before_ref, mirror0, mirror1 = refs
    else:
        tile_ref, own0, prev, next0, next1, started, forward_ref, before_ref, mirror0, mirror1 = refs
    forward_ref[...] = started[...]
    for ref in (before_ref, mirror0, mirror1):
        ref[...] = jnp.zeros_like(ref)
    take = vectors if make else (lambda ref: ref[...])
    for kind in range(2):

        @pl.loop(0, 4)
        def _(index):
            first, second = index // 2, index % 2
            slot = kind * 4 + index
            left = (own0, prev)[kind]

            @pl.when(flags_ref[3 + slot] > 0)
            def _():
                if make:
                    make_tiles(left.at[first], (next0.at[second], next1.at[second]), tile_ref, slot)
                use_tiles(
                    tile_ref, slot, (take(next0.at[second]), take(next1.at[second])),
                    take(left.at[first]), (forward_ref, before_ref)[kind], first,
                    (mirror0, mirror1), second, None,
                )


def total_kernel(forward, mirror_mine, mirror_other, from_next, from_prev, sum_ref, pair_ref=None):
    for block in range(2):
        value = (
            forward[block] + mirror_mine[block] + mirror_other[block]
            + from_next[block] + from_prev[block]
        )
        sum_ref[block] = value
        if pair_ref is not None:
            high = value.astype(jnp.bfloat16)
            pair_ref[block, :64] = high
            pair_ref[block, 64:] = (value - high.astype(jnp.float32)).astype(jnp.bfloat16)


def gram_of(value_ref, scale):
    gram = dot(value_ref[0], value_ref[0], NT, HIGHEST) + dot(value_ref[1], value_ref[1], NT, HIGHEST)
    gram = gram * scale
    return jnp.concatenate([gram[:32], gram[32:]], axis=1)


def gram_kernel(scale, value_ref, gram_ref):
    gram_ref[...] = gram_of(value_ref, scale)


def second_gram_kernel(scale, core_ref, first_ref, value_ref, keep_ref, give_ref, swap_ref):
    second = gram_of(value_ref, scale)
    first = first_ref[...]
    lead = core_ref[0] == 0
    keep_ref[...] = jnp.where(lead, first, second)
    give_ref[...] = jnp.where(lead, second, first)
    swap_ref[...] = value_ref[1 - core_ref[0]]


def eliminate(packed):
    lanes = lax.broadcasted_iota(jnp.int32, (8, 64), 1)
    subs = lax.broadcasted_iota(jnp.int32, (8, 64), 0)
    sub1 = lax.broadcasted_iota(jnp.int32, (8, 1), 0)
    states = []
    for matrix in packed:
        whole = jnp.concatenate([matrix[:, :64], matrix[:, 64:]], axis=0)
        states.append([
            jnp.concatenate(
                [whole[8 * b : 8 * b + 8], (lanes == subs + 8 * b).astype(jnp.float32)], axis=1
            )
            for b in range(8)
        ])
    for k in range(64):
        at, sub = k // 8, k % 8
        for state in states:
            row = state[at][sub : sub + 1, :]
            scaled = row / state[at][sub : sub + 1, k : k + 1]
            for b in range(at, 8):
                column = state[b][:, k : k + 1]
                if b == at:
                    column = jnp.where(sub1 > sub, column, 0.0)
                state[b] = state[b] - column * scaled
    uppers, inverses = [], []
    for state in states:
        rows = []
        for b in range(8):
            diagonal = jnp.sum(
                jnp.where(lanes == subs + 8 * b, state[b][:, :64], 0.0), axis=1, keepdims=True
            )
            rows.append(state[b] * lax.rsqrt(diagonal))
        whole = jnp.concatenate(rows, axis=0)
        uppers.append(whole[:, :64])
        inverses.append(whole[:, 64:])
    return uppers, inverses


def finish_kernel(core_ref, mine_ref, other_ref, value_ref, got_ref, basis_ref, factor_ref):
    core = core_ref[0]
    lead = core == 0
    mine, other = mine_ref[...], other_ref[...]
    first, second = jnp.where(lead, mine, other), jnp.where(lead, other, mine)
    uppers, inverses = eliminate([first, second])
    factor = dot(uppers[1], inverses[0], NT, HIGHEST)
    wide = lax.broadcasted_iota(jnp.int32, (64, 64), 1)
    tall = lax.broadcasted_iota(jnp.int32, (64, 64), 0)
    factor_ref[...] = jnp.where(wide >= tall, factor, 0.0)
    low = jnp.where(wide <= tall, inverses[1], 0.0)
    here = pl.multiple_of(core * HALF, HALF)
    there = pl.multiple_of((1 - core) * HALF, HALF)
    basis_ref[:, pl.ds(here, HALF)] = dot(low, value_ref[core], NN, HIGHEST)
    basis_ref[:, pl.ds(there, HALF)] = dot(low, got_ref[...], NN, HIGHEST)


def step_rows(value, steps):
    count = lax.axis_size("rows")
    return lax.ppermute(
        value, "rows", [(r, r + steps) for r in range(count) if 0 <= r + steps < count]
    )


def cross_rows(value):
    count = lax.axis_size("rows")
    return lax.ppermute(
        value,
        ("rows", "cols"),
        [(2 * r + c, 2 * (r + 1) + 1 - c) for r in range(count - 1) for c in range(2)],
    )


def swap(value):
    return lax.ppermute(value, "cols", [(0, 1), (1, 0)])


def live_flags(pair_list, base):
    pairs = jnp.concatenate(
        [pair_list, swap(pair_list), step_rows(pair_list, 1), cross_rows(pair_list)], axis=0
    )
    from_prev = lax.broadcasted_iota(jnp.int32, (16,), 0) >= 8
    codes = (pairs[:, 0] - base) * 8 + (pairs[:, 1] - base) + jnp.where(from_prev, 1000, 0)
    ours = [(0, 0), (0, 1), (1, 1), (0, 2), (0, 3), (1, 2), (1, 3)]
    across = [(-2, 2), (-2, 3), (-1, 2), (-1, 3)]
    wanted = [8 * i + j for i, j in ours] + [1000 + 8 * i + j for i, j in across]
    hit = codes[None, :] == jnp.array(wanted, jnp.int32)[:, None]
    return jnp.any(hit & (pairs[None, :, 0] >= 0), axis=1).astype(jnp.int32)


def spread(forward, before, own0, other_own, next0, next1):
    from_next = step_rows(before, -1)
    from_prev = step_rows(next0 + swap(next1), 1)
    return forward, own0, other_own, from_next, from_prev


def sum_over_chips(value):
    count = lax.axis_size("rows")
    planes = [[(x * PLANES + z) * RING + y for x in range(ACROSS) for y in range(RING)] for z in range(PLANES)]
    lines = [[(x * PLANES + z) * RING + y for z in range(PLANES)] for x in range(ACROSS) for y in range(RING)]
    for groups in (planes, lines):
        size = len(groups[0])
        copies = jnp.broadcast_to(value[None], (size,) + value.shape)
        value = lax.all_to_all(copies, "rows", 0, 0, axis_index_groups=groups, tiled=True).sum(0)
    return value


def local(embeddings, test_matrix, pair_list):
    rows_dev = embeddings.shape[0]
    columns = test_matrix.shape[1]
    bf16, f32 = jnp.bfloat16, jnp.float32
    core = lax.axis_index("cols").astype(jnp.int32)
    core_ref = core.reshape(1)
    base = (lax.axis_index("rows") * 2).astype(jnp.int32)
    scale = 1.0 / (rows_dev * lax.axis_size("rows"))

    test_columns = pltpu.with_memory_space_constraint(test_matrix.T, pltpu.HBM)
    embeddings = pltpu.with_memory_space_constraint(embeddings, pltpu.HBM)

    def packet(relative):
        return call(
            functools.partial(packet_kernel, relative), shape((2, 1792, 128), bf16), 10**4, 10**4,
        )(
            in_specs=[SMEM, HBM, HBM],
            scratch_shapes=[
                pltpu.VMEM((2, HALF, 384), bf16),
                pltpu.VMEM((2, columns, HALF), bf16),
                pltpu.SemaphoreType.DMA((4,)),
            ],
        )(core_ref, embeddings, test_columns)

    own0 = packet(0)
    next0 = step_rows(own0, -1)
    prev = step_rows(own0, 1)
    own1, pair_list = lax.optimization_barrier((packet(1), pair_list))
    flags = live_flags(pair_list, base)

    sum_shape = shape((2, 64, HALF))
    tiles_own, forward, mirror_own, mirror1 = call(
        functools.partial(local_kernel, True),
        (shape((3, 2, HALF, HALF), bf16),) + 3 * (sum_shape,),
        10**4, 10**4,
    )(in_specs=[SMEM] + [VMEM] * 2)(flags, own0, own1)
    mirror1, next0, prev = lax.optimization_barrier((mirror1, next0, prev))
    next1 = swap(next0)
    other_own = swap(mirror1)
    tiles_near, forward, before, mirror0, mirror1 = call(
        functools.partial(near_kernel, True),
        (shape((8, 2, HALF, HALF), bf16),) + 4 * (sum_shape,),
        4 * 10**9, 8 * 10**6, 2 * 10**6,
    )(in_specs=[SMEM] + [VMEM] * 5)(flags, own0, prev, next0, next1, forward)
    sketch, pair0 = call(total_kernel, (sum_shape, shape((2, 128, HALF), bf16)), 10**6, 2 * 10**6)(
        in_specs=[VMEM] * 5
    )(*spread(forward, before, mirror_own, other_own, mirror0, mirror1))

    pnext0 = step_rows(pair0, -1)
    pair_prev = step_rows(pair0, 1)
    pair1 = swap(pair0)
    pnext1 = swap(pnext0)
    gram_shape = shape((32, 128))
    first_gram = call(functools.partial(gram_kernel, scale), gram_shape, 10**8, 10**6)(
        in_specs=[VMEM]
    )(sketch)
    forward, mirror_own, mirror1 = call(
        functools.partial(local_kernel, False), 3 * (sum_shape,), 10**9, 3 * 10**6
    )(in_specs=[SMEM] + [VMEM] * 3)(flags, tiles_own, pair0, pair1)
    other_own = swap(mirror1)
    forward, before, mirror0, mirror1 = call(
        functools.partial(near_kernel, False), 4 * (sum_shape,), 10**9, 8 * 10**6
    )(in_specs=[SMEM] + [VMEM] * 6)(flags, tiles_near, pair0, pair_prev, pnext0, pnext1, forward)
    image = call(total_kernel, sum_shape, 10**6, 2 * 10**6)(in_specs=[VMEM] * 5)(
        *spread(forward, before, mirror_own, other_own, mirror0, mirror1)
    )
    keep, give, half = call(
        functools.partial(second_gram_kernel, scale),
        (gram_shape, gram_shape, shape((64, HALF))),
        10**8, 10**6,
    )(in_specs=[SMEM, VMEM, VMEM])(core_ref, first_gram, image)
    got = swap(half)
    mine = sum_over_chips(keep + swap(give))
    other = swap(mine)
    basis, factor = call(finish_kernel, (shape((64, BLK)), shape((64, 64))), 10**8, 10**6)(
        in_specs=[SMEM] + [VMEM] * 4
    )(core_ref, mine, other, image, got)
    return basis.T, factor


def solution(mesh):
    in_specs = (P("rows", None), P("rows", None), P(("rows", "cols"), None))
    out_specs = (P(("rows", "cols"), None), P())
    return jax.shard_map(local, mesh=mesh, in_specs=in_specs, out_specs=out_specs, check_vma=False)
```

```python
import functools

import jax
import jax.numpy as jnp
from jax import lax
from jax.experimental import pallas as pl
from jax.experimental.pallas import tpu as pltpu
from jax.sharding import PartitionSpec as P

BLK = 1024
HALF = 512
SHARPNESS = 6.0
EPSILON = 1e-06
LOG2E = 1.4426950408889634
HIGHEST = lax.Precision.HIGHEST
VMEM = pl.BlockSpec(memory_space=pltpu.VMEM)
HBM = pl.BlockSpec(memory_space=pltpu.HBM)
SMEM = pl.BlockSpec(memory_space=pltpu.SMEM)
NT = (((1,), (1,)), ((), ()))
NN = (((1,), (0,)), ((), ()))
ACROSS, PLANES, RING = 4, 8, 4


def call(kernel, outs, flops, moved, exps=0, room=16):
    return functools.partial(
        pl.pallas_call,
        kernel,
        out_shape=outs,
        out_specs=jax.tree.map(lambda _: VMEM, outs),
        compiler_params=pltpu.CompilerParams(vmem_limit_bytes=room * 1024 * 1024),
        cost_estimate=pl.CostEstimate(flops=flops, bytes_accessed=moved, transcendentals=exps),
    )


def shape(dims, dtype=jnp.float32):
    return jax.ShapeDtypeStruct(dims, dtype)


def dot(left, right, dims, precision=None):
    return lax.dot_general(
        left, right, dims, precision=precision, preferred_element_type=jnp.float32
    )


def packet_kernel(relative, core_ref, rows_ref, columns_ref, packet_ref, raw_ref, vec_ref, sems):
    side = core_ref[0] if relative == 0 else 1 - core_ref[0]
    copies = []
    for block in range(2):
        start = pl.multiple_of(block * BLK + side * HALF, HALF)
        copies.append((
            pltpu.make_async_copy(rows_ref.at[pl.ds(start, HALF), :], raw_ref.at[block], sems.at[block]),
            pltpu.make_async_copy(
                columns_ref.at[:, pl.ds(start, HALF)], vec_ref.at[block], sems.at[2 + block]
            ),
        ))
        for copy in copies[-1]:
            copy.start()
    for block in range(2):
        for copy in copies[block]:
            copy.wait()
        widened = raw_ref[block].astype(jnp.float32)
        inverse = lax.rsqrt(jnp.sum(widened * widened, axis=1, keepdims=True) + EPSILON)
        unit = (widened * inverse).astype(jnp.bfloat16)
        for tile in range(3):
            packet_ref[block, HALF * tile : HALF * (tile + 1)] = unit[:, 128 * tile : 128 * (tile + 1)]
        for tile in range(4):
            packet_ref[block, 1536 + 64 * tile : 1600 + 64 * tile] = vec_ref[
                block, :, 128 * tile : 128 * (tile + 1)
            ]


def unit_rows(packet, start, count):
    return jnp.concatenate(
        [packet[HALF * tile + start : HALF * tile + start + count] for tile in range(3)], axis=1
    )


def vectors(packet):
    return jnp.concatenate([packet[1536 + 64 * tile : 1600 + 64 * tile] for tile in range(4)], axis=1)


def affinity_tile(left, right):
    scores = dot(left, right, NT)
    return jnp.exp2((SHARPNESS * LOG2E) * scores - (SHARPNESS * LOG2E)).astype(jnp.bfloat16)


def fold(product):
    if product.shape[0] == 128:
        return product[:64] + product[64:]
    return product


def make_tiles(left, rights, tile_ref, slot):
    whole = unit_rows(left, 0, HALF)
    for side in range(2):
        for at in range(0, HALF, 256):
            tile_ref[slot, side, :, at : at + 256] = affinity_tile(
                whole, unit_rows(rights[side], at, 256)
            )


def use_tiles(tile_ref, slot, rights, left, done_ref, done_at, part_refs, part_at, partial):
    total = fold(dot(rights[0], tile_ref[slot, 0], NT)) + fold(dot(rights[1], tile_ref[slot, 1], NT))
    done_ref[done_at] += total

    def put_part():
        for side in range(2):
            part_refs[side][part_at] += fold(dot(left, tile_ref[slot, side], NN))

    if partial is None:
        put_part()
    else:
        pl.when(partial)(put_part)


def one_pair(make, tile_ref, slot, left, rights, done_ref, done_at, part_refs, part_at, partial=None):
    take = vectors if make else (lambda ref: ref[...])
    if make:
        make_tiles(left, rights, tile_ref, slot)
    use_tiles(
        tile_ref, slot, (take(rights[0]), take(rights[1])), take(left),
        done_ref, done_at, part_refs, part_at, partial,
    )


def local_kernel(make, flags_ref, *refs):
    if make:
        own0, own1, tile_ref, done_ref, part0, part1 = refs
    else:
        tile_ref, own0, own1, done_ref, part0, part1 = refs
    for ref in (done_ref, part0, part1):
        ref[...] = jnp.zeros_like(ref)

    @pl.loop(0, 3)
    def _(slot):
        first, second = slot // 2, (slot + 1) // 2

        @pl.when(flags_ref[slot] > 0)
        def _():
            one_pair(
                make, tile_ref, slot, own0.at[first], (own0.at[second], own1.at[second]),
                done_ref, first, (part0, part1), second, slot == 1,
            )


def odd_kernel(make, flags_ref, *refs):
    if make:
        odd0, own0, own1, in0, in1, tile_ref, done_ref, part0, part1 = refs
    else:
        tile_ref, odd0, own0, own1, in0, in1, done_ref, part0, part1 = refs
    done_ref[...] = jnp.zeros_like(done_ref)
    part0[...] = in0[...]
    part1[...] = in1[...]

    @pl.loop(0, 4)
    def _(slot):
        left, right = slot // 2, slot % 2

        @pl.when(flags_ref[7 + slot] > 0)
        def _():
            one_pair(
                make, tile_ref, slot, odd0.at[left], (own0.at[right], own1.at[right]),
                done_ref, left, (part0, part1), right,
            )


def even_kernel(make, flags_ref, far_ref, *refs):
    if make:
        own0, odd0, even0, even1, own_in, odd_in, tile_ref, *refs = refs
    else:
        tile_ref, own0, odd0, even0, even1, own_in, odd_in, *refs = refs
    own_done, odd_done, part0, part1 = refs
    own_done[...] = own_in[...]
    odd_done[...] = odd_in[...]
    for ref in (part0, part1):
        ref[...] = jnp.zeros_like(ref)
    for kind in range(2):
        lefts, done_ref = ((own0, own_done), (odd0, odd_done))[kind]
        flag_ref, flag_at = ((flags_ref, 3), (far_ref, 0))[kind]

        @pl.loop(0, 4)
        def _(index):
            left, right = index // 2, index % 2

            @pl.when(flag_ref[flag_at + index] > 0)
            def _():
                one_pair(
                    make, tile_ref, kind * 4 + index, lefts.at[left],
                    (even0.at[right], even1.at[right]), done_ref, left, (part0, part1), right,
                )


def total_kernel(done, part_mine, part_other, from_odd, from_even, sum_ref, pair_ref=None):
    for block in range(2):
        value = (
            done[block] + part_mine[block] + part_other[block] + from_odd[block] + from_even[block]
        )
        sum_ref[block] = value
        if pair_ref is not None:
            high = value.astype(jnp.bfloat16)
            pair_ref[block, :64] = high
            pair_ref[block, 64:] = (value - high.astype(jnp.float32)).astype(jnp.bfloat16)


def gram_of(value_ref, scale):
    gram = dot(value_ref[0], value_ref[0], NT, HIGHEST) + dot(value_ref[1], value_ref[1], NT, HIGHEST)
    gram = gram * scale
    return jnp.concatenate([gram[:32], gram[32:]], axis=1)


def gram_kernel(scale, value_ref, gram_ref):
    gram_ref[...] = gram_of(value_ref, scale)


def second_gram_kernel(scale, core_ref, first_ref, value_ref, keep_ref, give_ref, swap_ref):
    second = gram_of(value_ref, scale)
    first = first_ref[...]
    lead = core_ref[0] == 0
    keep_ref[...] = jnp.where(lead, first, second)
    give_ref[...] = jnp.where(lead, second, first)
    swap_ref[...] = value_ref[1 - core_ref[0]]


def eliminate(packed):
    lanes = lax.broadcasted_iota(jnp.int32, (8, 64), 1)
    subs = lax.broadcasted_iota(jnp.int32, (8, 64), 0)
    sub1 = lax.broadcasted_iota(jnp.int32, (8, 1), 0)
    states = []
    for matrix in packed:
        whole = jnp.concatenate([matrix[:, :64], matrix[:, 64:]], axis=0)
        states.append([
            jnp.concatenate(
                [whole[8 * b : 8 * b + 8], (lanes == subs + 8 * b).astype(jnp.float32)], axis=1
            )
            for b in range(8)
        ])
    for k in range(64):
        at, sub = k // 8, k % 8
        for state in states:
            row = state[at][sub : sub + 1, :]
            scaled = row / state[at][sub : sub + 1, k : k + 1]
            for b in range(at, 8):
                column = state[b][:, k : k + 1]
                if b == at:
                    column = jnp.where(sub1 > sub, column, 0.0)
                state[b] = state[b] - column * scaled
    uppers, inverses = [], []
    for state in states:
        rows = []
        for b in range(8):
            diagonal = jnp.sum(
                jnp.where(lanes == subs + 8 * b, state[b][:, :64], 0.0), axis=1, keepdims=True
            )
            rows.append(state[b] * lax.rsqrt(diagonal))
        whole = jnp.concatenate(rows, axis=0)
        uppers.append(whole[:, :64])
        inverses.append(whole[:, 64:])
    return uppers, inverses


def finish_kernel(core_ref, mine_ref, other_ref, value_ref, got_ref, basis_ref, factor_ref):
    core = core_ref[0]
    lead = core == 0
    mine, other = mine_ref[...], other_ref[...]
    first, second = jnp.where(lead, mine, other), jnp.where(lead, other, mine)
    uppers, inverses = eliminate([first, second])
    factor = dot(uppers[1], inverses[0], NT, HIGHEST)
    wide = lax.broadcasted_iota(jnp.int32, (64, 64), 1)
    tall = lax.broadcasted_iota(jnp.int32, (64, 64), 0)
    factor_ref[...] = jnp.where(wide >= tall, factor, 0.0)
    low = jnp.where(wide <= tall, inverses[1], 0.0)
    here = pl.multiple_of(core * HALF, HALF)
    there = pl.multiple_of((1 - core) * HALF, HALF)
    basis_ref[:, pl.ds(here, HALF)] = dot(low, value_ref[core], NN, HIGHEST)
    basis_ref[:, pl.ds(there, HALF)] = dot(low, got_ref[...], NN, HIGHEST)


def exchange(value, start):
    links = []
    for r in range(start, lax.axis_size("rows") - 1, 2):
        links += [(r, r + 1), (r + 1, r)]
    return lax.ppermute(value, "rows", links)


def to_even(value):
    return exchange(value, 0)


def to_odd(value):
    return exchange(value, 1)


def swap(value):
    return lax.ppermute(value, "cols", [(0, 1), (1, 0)])


def live_flags(pairs, base, even_codes, odd_codes):
    none = (100, 100)

    def table(entries):
        return jnp.array([64 * i + j for i, j in (none if e is None else e for e in entries)], jnp.int32)

    even_row = lax.axis_index("rows") % 2 == 0
    wanted = jnp.where(even_row, table(even_codes), table(odd_codes))
    codes = (pairs[:, 0] - base) * 64 + (pairs[:, 1] - base)
    hit = (codes[None, :] == wanted[:, None]) & (pairs[None, :, 0] >= 0)
    return jnp.any(hit, axis=1).astype(jnp.int32)


SLOTS = [(0, 0), (0, 1), (1, 0), (1, 1)]


def own_flags_and_list(pair_list, base):
    own = jnp.concatenate([pair_list, swap(pair_list)], axis=0)
    before = lax.ppermute(own, "rows", [(r, r + 1) for r in range(lax.axis_size("rows") - 1)])
    within, idle = [(0, 0), (0, 1), (1, 1)], [None] * 4
    flags = live_flags(
        own, base,
        within + [(left, 2 + right) for left, right in SLOTS] + idle,
        within + idle + [(right, 2 + left) for left, right in SLOTS],
    )
    return flags, before


def flags_of_far(before, base):
    return live_flags(
        before, base,
        [(left - 2, 2 + right) for left, right in SLOTS],
        [(right - 2, 2 + left) for left, right in SLOTS],
    )


def spread(done, own0, own1, out_odd, even0, even1):
    from_odd = to_odd(out_odd)
    from_even = to_even(even0 + swap(even1))
    return done, own0, swap(own1), from_odd, from_even


def sum_over_chips(value):
    count = lax.axis_size("rows")
    planes = [[(x * PLANES + z) * RING + y for x in range(ACROSS) for y in range(RING)] for z in range(PLANES)]
    lines = [[(x * PLANES + z) * RING + y for z in range(PLANES)] for x in range(ACROSS) for y in range(RING)]
    for groups in (planes, lines):
        size = len(groups[0])
        copies = jnp.broadcast_to(value[None], (size,) + value.shape)
        value = lax.all_to_all(copies, "rows", 0, 0, axis_index_groups=groups, tiled=True).sum(0)
    return value


def local(embeddings, test_matrix, pair_list):
    rows_dev = embeddings.shape[0]
    columns = test_matrix.shape[1]
    bf16, f32 = jnp.bfloat16, jnp.float32
    core = lax.axis_index("cols").astype(jnp.int32)
    core_ref = core.reshape(1)
    base = (lax.axis_index("rows") * 2).astype(jnp.int32)
    scale = 1.0 / (rows_dev * lax.axis_size("rows"))

    test_columns = pltpu.with_memory_space_constraint(test_matrix.T, pltpu.HBM)
    embeddings = pltpu.with_memory_space_constraint(embeddings, pltpu.HBM)

    def packet(relative):
        return call(
            functools.partial(packet_kernel, relative), shape((2, 1792, 128), bf16), 10**4, 10**4,
        )(
            in_specs=[SMEM, HBM, HBM],
            scratch_shapes=[
                pltpu.VMEM((2, HALF, 384), bf16),
                pltpu.VMEM((2, columns, HALF), bf16),
                pltpu.SemaphoreType.DMA((4,)),
            ],
        )(core_ref, embeddings, test_columns)

    own0 = packet(0)
    even0 = to_even(own0)
    odd0 = to_odd(own0)
    own1, pair_list = lax.optimization_barrier((packet(1), pair_list))
    flags, before = own_flags_and_list(pair_list, base)

    sum_shape = shape((2, 64, HALF))

    def tiles(count):
        return shape((count, 2, HALF, HALF), bf16)

    tiles_own, done, own_part0, own_part1 = call(
        functools.partial(local_kernel, True), (tiles(3),) + 3 * (sum_shape,), 10**4, 10**4
    )(in_specs=[SMEM] + [VMEM] * 2)(flags, own0, own1)
    done, even0, odd0, before = lax.optimization_barrier((done, even0, odd0, before))
    even1 = swap(even0)
    far_flags = flags_of_far(before, base)
    tiles_odd, out_odd, own_part0, own_part1 = call(
        functools.partial(odd_kernel, True), (tiles(4),) + 3 * (sum_shape,), 10**4, 10**4
    )(in_specs=[SMEM] + [VMEM] * 5)(flags, odd0, own0, own1, own_part0, own_part1)
    tiles_even, done, out_odd, even_part0, even_part1 = call(
        functools.partial(even_kernel, True), (tiles(8),) + 4 * (sum_shape,), 10**9, 10**6
    )(in_specs=[SMEM] * 2 + [VMEM] * 6)(flags, far_flags, own0, odd0, even0, even1, done, out_odd)
    sketch, pair0 = call(total_kernel, (sum_shape, shape((2, 128, HALF), bf16)), 10**6, 2 * 10**6)(
        in_specs=[VMEM] * 5
    )(*spread(done, own_part0, own_part1, out_odd, even_part0, even_part1))

    even0 = to_even(pair0)
    odd0 = to_odd(pair0)
    pair1 = swap(pair0)
    gram_shape = shape((32, 128))
    first_gram = call(functools.partial(gram_kernel, scale), gram_shape, 10**8, 10**6)(
        in_specs=[VMEM]
    )(sketch)
    done, own_part0, own_part1 = call(
        functools.partial(local_kernel, False), 3 * (sum_shape,), 10**4, 10**4
    )(in_specs=[SMEM] + [VMEM] * 3)(flags, tiles_own, pair0, pair1)
    done, even0, odd0 = lax.optimization_barrier((done, even0, odd0))
    even1 = swap(even0)
    out_odd, own_part0, own_part1 = call(
        functools.partial(odd_kernel, False), 3 * (sum_shape,), 10**4, 10**4
    )(in_specs=[SMEM] + [VMEM] * 6)(flags, tiles_odd, odd0, pair0, pair1, own_part0, own_part1)
    done, out_odd, even_part0, even_part1 = call(
        functools.partial(even_kernel, False), 4 * (sum_shape,), 10**9, 10**6
    )(in_specs=[SMEM] * 2 + [VMEM] * 7)(
        flags, far_flags, tiles_even, pair0, odd0, even0, even1, done, out_odd
    )
    image = call(total_kernel, sum_shape, 10**6, 2 * 10**6)(in_specs=[VMEM] * 5)(
        *spread(done, own_part0, own_part1, out_odd, even_part0, even_part1)
    )
    keep, give, half = call(
        functools.partial(second_gram_kernel, scale),
        (gram_shape, gram_shape, shape((64, HALF))),
        10**8, 10**6,
    )(in_specs=[SMEM, VMEM, VMEM])(core_ref, first_gram, image)
    got = swap(half)
    mine = sum_over_chips(keep + swap(give))
    other = swap(mine)
    basis, factor = call(finish_kernel, (shape((64, BLK)), shape((64, 64))), 10**8, 10**6)(
        in_specs=[SMEM] + [VMEM] * 4
    )(core_ref, mine, other, image, got)
    return basis.T, factor


def solution(mesh):
    in_specs = (P("rows", None), P("rows", None), P(("rows", "cols"), None))
    out_specs = (P(("rows", "cols"), None), P())
    return jax.shard_map(local, mesh=mesh, in_specs=in_specs, out_specs=out_specs, check_vma=False)
```

```python
import functools

import jax
import jax.numpy as jnp
from jax import lax
from jax.experimental import pallas as pl
from jax.experimental.pallas import tpu as pltpu
from jax.sharding import PartitionSpec as P

BLK = 1024
HALF = 512
SHARPNESS = 6.0
EPSILON = 1e-06
LOG2E = 1.4426950408889634
HIGHEST = lax.Precision.HIGHEST
VMEM = pl.BlockSpec(memory_space=pltpu.VMEM)
HBM = pl.BlockSpec(memory_space=pltpu.HBM)
SMEM = pl.BlockSpec(memory_space=pltpu.SMEM)
NT = (((1,), (1,)), ((), ()))
NN = (((1,), (0,)), ((), ()))
ACROSS, PLANES, RING = 4, 8, 4


def call(kernel, outs, flops, moved, exps=0, room=16):
    return functools.partial(
        pl.pallas_call,
        kernel,
        out_shape=outs,
        out_specs=jax.tree.map(lambda _: VMEM, outs),
        compiler_params=pltpu.CompilerParams(vmem_limit_bytes=room * 1024 * 1024),
        cost_estimate=pl.CostEstimate(flops=flops, bytes_accessed=moved, transcendentals=exps),
    )


def shape(dims, dtype=jnp.float32):
    return jax.ShapeDtypeStruct(dims, dtype)


def dot(left, right, dims, precision=None):
    return lax.dot_general(
        left, right, dims, precision=precision, preferred_element_type=jnp.float32
    )


def packet_kernel(relative, core_ref, rows_ref, columns_ref, packet_ref, raw_ref, vec_ref, sems):
    side = core_ref[0] if relative == 0 else 1 - core_ref[0]
    copies = []
    for block in range(2):
        start = pl.multiple_of(block * BLK + side * HALF, HALF)
        copies.append((
            pltpu.make_async_copy(rows_ref.at[pl.ds(start, HALF), :], raw_ref.at[block], sems.at[block]),
            pltpu.make_async_copy(
                columns_ref.at[:, pl.ds(start, HALF)], vec_ref.at[block], sems.at[2 + block]
            ),
        ))
        for copy in copies[-1]:
            copy.start()
    for block in range(2):
        for copy in copies[block]:
            copy.wait()
        widened = raw_ref[block].astype(jnp.float32)
        inverse = lax.rsqrt(jnp.sum(widened * widened, axis=1, keepdims=True) + EPSILON)
        unit = (widened * inverse).astype(jnp.bfloat16)
        for tile in range(3):
            packet_ref[block, HALF * tile : HALF * (tile + 1)] = unit[:, 128 * tile : 128 * (tile + 1)]
        for tile in range(4):
            packet_ref[block, 1536 + 64 * tile : 1600 + 64 * tile] = vec_ref[
                block, :, 128 * tile : 128 * (tile + 1)
            ]


def unit_rows(packet, start, count):
    return jnp.concatenate(
        [packet[HALF * tile + start : HALF * tile + start + count] for tile in range(3)], axis=1
    )


def vectors(packet):
    return jnp.concatenate([packet[1536 + 64 * tile : 1600 + 64 * tile] for tile in range(4)], axis=1)


def affinity_tile(left, right):
    scores = dot(left, right, NT)
    return jnp.exp2((SHARPNESS * LOG2E) * scores - (SHARPNESS * LOG2E)).astype(jnp.bfloat16)


def fold(product):
    if product.shape[0] == 128:
        return product[:64] + product[64:]
    return product


def make_tiles(left, rights, tile_ref, slot):
    whole = unit_rows(left, 0, HALF)
    for side in range(2):
        for at in range(0, HALF, 256):
            tile_ref[slot, side, :, at : at + 256] = affinity_tile(
                whole, unit_rows(rights[side], at, 256)
            )


def use_tiles(tile_ref, slot, rights, left, done_ref, done_at, part_refs, part_at, partial):
    total = fold(dot(rights[0], tile_ref[slot, 0], NT)) + fold(dot(rights[1], tile_ref[slot, 1], NT))
    done_ref[done_at] += total

    def put_part():
        for side in range(2):
            part_refs[side][part_at] += fold(dot(left, tile_ref[slot, side], NN))

    if partial is None:
        put_part()
    else:
        pl.when(partial)(put_part)


def one_pair(make, tile_ref, slot, left, rights, done_ref, done_at, part_refs, part_at, partial=None):
    take = vectors if make else (lambda ref: ref[...])
    if make:
        make_tiles(left, rights, tile_ref, slot)
    use_tiles(
        tile_ref, slot, (take(rights[0]), take(rights[1])), take(left),
        done_ref, done_at, part_refs, part_at, partial,
    )


def local_kernel(make, flags_ref, *refs):
    if make:
        own0, own1, tile_ref, done_ref, part0, part1 = refs
    else:
        tile_ref, own0, own1, done_ref, part0, part1 = refs
    for ref in (done_ref, part0, part1):
        ref[...] = jnp.zeros_like(ref)

    @pl.loop(0, 3)
    def _(slot):
        first, second = slot // 2, (slot + 1) // 2

        @pl.when(flags_ref[slot] > 0)
        def _():
            one_pair(
                make, tile_ref, slot, own0.at[first], (own0.at[second], own1.at[second]),
                done_ref, first, (part0, part1), second, slot == 1,
            )


def early_kernel(make, flags_ref, *refs):
    if make:
        own0, even0, even1, started, tile_ref, done_ref, part0, part1 = refs
    else:
        tile_ref, own0, even0, even1, started, done_ref, part0, part1 = refs
    done_ref[...] = started[...]
    for ref in (part0, part1):
        ref[...] = jnp.zeros_like(ref)

    @pl.loop(0, 4)
    def _(slot):
        left, right = slot // 2, slot % 2

        @pl.when(flags_ref[3 + slot] > 0)
        def _():
            one_pair(
                make, tile_ref, slot, own0.at[left], (even0.at[right], even1.at[right]),
                done_ref, left, (part0, part1), right,
            )


def late_kernel(make, flags_ref, far_ref, *refs):
    if make:
        odd0, own0, own1, even0, even1, *ins = refs[:9]
        tile_ref, done_ref, *parts = refs[9:]
    else:
        tile_ref, odd0, own0, own1, even0, even1, *ins = refs[:10]
        done_ref, *parts = refs[10:]
    done_ref[...] = jnp.zeros_like(done_ref)
    for ref, value in zip(parts, ins):
        ref[...] = value[...]
    for kind in range(2):
        rights = ((own0, own1), (even0, even1))[kind]
        part_refs = (parts[:2], parts[2:])[kind]
        flag_ref, flag_at = ((flags_ref, 7), (far_ref, 0))[kind]

        @pl.loop(0, 4)
        def _(index):
            left, right = index // 2, index % 2

            @pl.when(flag_ref[flag_at + index] > 0)
            def _():
                one_pair(
                    make, tile_ref, kind * 4 + index, odd0.at[left],
                    (rights[0].at[right], rights[1].at[right]), done_ref, left, part_refs, right,
                )


def total_kernel(done, part_mine, part_other, from_odd, from_even, sum_ref, pair_ref=None):
    for block in range(2):
        value = (
            done[block] + part_mine[block] + part_other[block] + from_odd[block] + from_even[block]
        )
        sum_ref[block] = value
        if pair_ref is not None:
            high = value.astype(jnp.bfloat16)
            pair_ref[block, :64] = high
            pair_ref[block, 64:] = (value - high.astype(jnp.float32)).astype(jnp.bfloat16)


def gram_of(value_ref, scale):
    gram = dot(value_ref[0], value_ref[0], NT, HIGHEST) + dot(value_ref[1], value_ref[1], NT, HIGHEST)
    gram = gram * scale
    return jnp.concatenate([gram[:32], gram[32:]], axis=1)


def gram_kernel(scale, value_ref, gram_ref):
    gram_ref[...] = gram_of(value_ref, scale)


def second_gram_kernel(scale, core_ref, first_ref, value_ref, keep_ref, give_ref, swap_ref):
    second = gram_of(value_ref, scale)
    first = first_ref[...]
    lead = core_ref[0] == 0
    keep_ref[...] = jnp.where(lead, first, second)
    give_ref[...] = jnp.where(lead, second, first)
    swap_ref[...] = value_ref[1 - core_ref[0]]


def eliminate(packed):
    lanes = lax.broadcasted_iota(jnp.int32, (8, 64), 1)
    subs = lax.broadcasted_iota(jnp.int32, (8, 64), 0)
    sub1 = lax.broadcasted_iota(jnp.int32, (8, 1), 0)
    states = []
    for matrix in packed:
        whole = jnp.concatenate([matrix[:, :64], matrix[:, 64:]], axis=0)
        states.append([
            jnp.concatenate(
                [whole[8 * b : 8 * b + 8], (lanes == subs + 8 * b).astype(jnp.float32)], axis=1
            )
            for b in range(8)
        ])
    for k in range(64):
        at, sub = k // 8, k % 8
        for state in states:
            row = state[at][sub : sub + 1, :]
            scaled = row / state[at][sub : sub + 1, k : k + 1]
            for b in range(at, 8):
                column = state[b][:, k : k + 1]
                if b == at:
                    column = jnp.where(sub1 > sub, column, 0.0)
                state[b] = state[b] - column * scaled
    uppers, inverses = [], []
    for state in states:
        rows = []
        for b in range(8):
            diagonal = jnp.sum(
                jnp.where(lanes == subs + 8 * b, state[b][:, :64], 0.0), axis=1, keepdims=True
            )
            rows.append(state[b] * lax.rsqrt(diagonal))
        whole = jnp.concatenate(rows, axis=0)
        uppers.append(whole[:, :64])
        inverses.append(whole[:, 64:])
    return uppers, inverses


def finish_kernel(core_ref, mine_ref, other_ref, value_ref, got_ref, basis_ref, factor_ref):
    core = core_ref[0]
    lead = core == 0
    mine, other = mine_ref[...], other_ref[...]
    first, second = jnp.where(lead, mine, other), jnp.where(lead, other, mine)
    uppers, inverses = eliminate([first, second])
    factor = dot(uppers[1], inverses[0], NT, HIGHEST)
    wide = lax.broadcasted_iota(jnp.int32, (64, 64), 1)
    tall = lax.broadcasted_iota(jnp.int32, (64, 64), 0)
    factor_ref[...] = jnp.where(wide >= tall, factor, 0.0)
    low = jnp.where(wide <= tall, inverses[1], 0.0)
    here = pl.multiple_of(core * HALF, HALF)
    there = pl.multiple_of((1 - core) * HALF, HALF)
    basis_ref[:, pl.ds(here, HALF)] = dot(low, value_ref[core], NN, HIGHEST)
    basis_ref[:, pl.ds(there, HALF)] = dot(low, got_ref[...], NN, HIGHEST)


def exchange(value, start):
    links = []
    for r in range(start, lax.axis_size("rows") - 1, 2):
        links += [(r, r + 1), (r + 1, r)]
    return lax.ppermute(value, "rows", links)


def to_even(value):
    return exchange(value, 0)


def to_odd(value):
    return exchange(value, 1)


def swap(value):
    return lax.ppermute(value, "cols", [(0, 1), (1, 0)])


def swap_blocks(value):
    return jnp.stack([swap(value[block]) for block in range(2)])


def live_flags(pairs, base, even_codes, odd_codes):
    none = (100, 100)

    def table(entries):
        return jnp.array([64 * i + j for i, j in (none if e is None else e for e in entries)], jnp.int32)

    even_row = lax.axis_index("rows") % 2 == 0
    wanted = jnp.where(even_row, table(even_codes), table(odd_codes))
    codes = (pairs[:, 0] - base) * 64 + (pairs[:, 1] - base)
    hit = (codes[None, :] == wanted[:, None]) & (pairs[None, :, 0] >= 0)
    return jnp.any(hit, axis=1).astype(jnp.int32)


SLOTS = [(0, 0), (0, 1), (1, 0), (1, 1)]


def own_flags_and_list(pair_list, base):
    own = jnp.concatenate([pair_list, swap(pair_list)], axis=0)
    before = lax.ppermute(own, "rows", [(r, r + 1) for r in range(lax.axis_size("rows") - 1)])
    within, idle = [(0, 0), (0, 1), (1, 1)], [None] * 4
    flags = live_flags(
        own, base,
        within + [(left, 2 + right) for left, right in SLOTS] + idle,
        within + idle + [(right, 2 + left) for left, right in SLOTS],
    )
    return flags, before


def flags_of_far(before, base):
    return live_flags(
        before, base,
        [(left - 2, 2 + right) for left, right in SLOTS],
        [(right - 2, 2 + left) for left, right in SLOTS],
    )


def spread(done, own0, own1, out_odd, even0, even1):
    from_odd = to_odd(out_odd)
    from_even = to_even(even0 + swap(even1))
    return done, own0, swap(own1), from_odd, from_even


def sum_over_chips(value):
    count = lax.axis_size("rows")
    planes = [[(x * PLANES + z) * RING + y for x in range(ACROSS) for y in range(RING)] for z in range(PLANES)]
    lines = [[(x * PLANES + z) * RING + y for z in range(PLANES)] for x in range(ACROSS) for y in range(RING)]
    for groups in (planes, lines):
        size = len(groups[0])
        copies = jnp.broadcast_to(value[None], (size,) + value.shape)
        value = lax.all_to_all(copies, "rows", 0, 0, axis_index_groups=groups, tiled=True).sum(0)
    return value


def local(embeddings, test_matrix, pair_list):
    rows_dev = embeddings.shape[0]
    columns = test_matrix.shape[1]
    bf16, f32 = jnp.bfloat16, jnp.float32
    core = lax.axis_index("cols").astype(jnp.int32)
    core_ref = core.reshape(1)
    base = (lax.axis_index("rows") * 2).astype(jnp.int32)
    scale = 1.0 / (rows_dev * lax.axis_size("rows"))

    test_columns = pltpu.with_memory_space_constraint(test_matrix.T, pltpu.HBM)
    embeddings = pltpu.with_memory_space_constraint(embeddings, pltpu.HBM)

    def packet(relative):
        return call(
            functools.partial(packet_kernel, relative), shape((2, 1792, 128), bf16), 10**4, 10**4,
        )(
            in_specs=[SMEM, HBM, HBM],
            scratch_shapes=[
                pltpu.VMEM((2, HALF, 384), bf16),
                pltpu.VMEM((2, columns, HALF), bf16),
                pltpu.SemaphoreType.DMA((4,)),
            ],
        )(core_ref, embeddings, test_columns)

    own0 = packet(0)
    even0 = to_even(own0)
    odd0 = to_odd(own0)
    own1, pair_list = lax.optimization_barrier((packet(1), pair_list))
    flags, before = own_flags_and_list(pair_list, base)

    sum_shape = shape((2, 64, HALF))

    def tiles(count):
        return shape((count, 2, HALF, HALF), bf16)

    tiles_own, done, own_part0, own_part1 = call(
        functools.partial(local_kernel, True), (tiles(3),) + 3 * (sum_shape,), 10**4, 10**4
    )(in_specs=[SMEM] + [VMEM] * 2)(flags, own0, own1)
    done, even0 = lax.optimization_barrier((done, even0))
    even1 = swap_blocks(even0)
    tiles_early, done, even_part0, even_part1 = call(
        functools.partial(early_kernel, True), (tiles(4),) + 3 * (sum_shape,), 10**4, 10**4
    )(in_specs=[SMEM] + [VMEM] * 4)(flags, own0, even0, even1, done)
    done, odd0, before = lax.optimization_barrier((done, odd0, before))
    far_flags = flags_of_far(before, base)
    tiles_late, out_odd, own_part0, own_part1, even_part0, even_part1 = call(
        functools.partial(late_kernel, True), (tiles(8),) + 5 * (sum_shape,), 10**9, 10**6
    )(in_specs=[SMEM] * 2 + [VMEM] * 9)(
        flags, far_flags, odd0, own0, own1, even0, even1, own_part0, own_part1, even_part0, even_part1
    )
    sketch, pair0 = call(total_kernel, (sum_shape, shape((2, 128, HALF), bf16)), 10**6, 2 * 10**6)(
        in_specs=[VMEM] * 5
    )(*spread(done, own_part0, own_part1, out_odd, even_part0, even_part1))

    even0 = to_even(pair0)
    odd0 = to_odd(pair0)
    gram_shape = shape((32, 128))
    first_gram = call(functools.partial(gram_kernel, scale), gram_shape, 10**4, 10**4)(
        in_specs=[VMEM]
    )(sketch)
    pair1 = swap(pair0)
    done, own_part0, own_part1 = call(
        functools.partial(local_kernel, False), 3 * (sum_shape,), 10**4, 10**4
    )(in_specs=[SMEM] + [VMEM] * 3)(flags, tiles_own, pair0, pair1)
    even1 = swap_blocks(even0)
    done, even_part0, even_part1 = call(
        functools.partial(early_kernel, False), 3 * (sum_shape,), 10**4, 10**4
    )(in_specs=[SMEM] + [VMEM] * 5)(flags, tiles_early, pair0, even0, even1, done)
    done, odd0 = lax.optimization_barrier((done, odd0))
    out_odd, own_part0, own_part1, even_part0, even_part1 = call(
        functools.partial(late_kernel, False), 5 * (sum_shape,), 10**9, 10**6
    )(in_specs=[SMEM] * 2 + [VMEM] * 10)(
        flags, far_flags, tiles_late, odd0, pair0, pair1, even0, even1,
        own_part0, own_part1, even_part0, even_part1,
    )
    image = call(total_kernel, sum_shape, 10**6, 2 * 10**6)(in_specs=[VMEM] * 5)(
        *spread(done, own_part0, own_part1, out_odd, even_part0, even_part1)
    )
    keep, give, half = call(
        functools.partial(second_gram_kernel, scale),
        (gram_shape, gram_shape, shape((64, HALF))),
        10**8, 10**6,
    )(in_specs=[SMEM, VMEM, VMEM])(core_ref, first_gram, image)
    got = swap(half)
    mine = sum_over_chips(keep + swap(give))
    other = swap(mine)
    basis, factor = call(finish_kernel, (shape((64, BLK)), shape((64, 64))), 10**8, 10**6)(
        in_specs=[SMEM] + [VMEM] * 4
    )(core_ref, mine, other, image, got)
    return basis.T, factor


def solution(mesh):
    in_specs = (P("rows", None), P("rows", None), P(("rows", "cols"), None))
    out_specs = (P(("rows", "cols"), None), P())
    return jax.shard_map(local, mesh=mesh, in_specs=in_specs, out_specs=out_specs, check_vma=False)
```

```python
import functools

import jax
import jax.numpy as jnp
from jax import lax
from jax.experimental import pallas as pl
from jax.experimental.pallas import tpu as pltpu
from jax.sharding import PartitionSpec as P

BLK = 1024
HALF = 512
SHARPNESS = 6.0
EPSILON = 1e-06
LOG2E = 1.4426950408889634
HIGHEST = lax.Precision.HIGHEST
VMEM = pl.BlockSpec(memory_space=pltpu.VMEM)
HBM = pl.BlockSpec(memory_space=pltpu.HBM)
SMEM = pl.BlockSpec(memory_space=pltpu.SMEM)
NT = (((1,), (1,)), ((), ()))
NN = (((1,), (0,)), ((), ()))
ACROSS, PLANES, RING = 4, 8, 4


def call(kernel, outs, flops, moved, exps=0, room=16):
    return functools.partial(
        pl.pallas_call,
        kernel,
        out_shape=outs,
        out_specs=jax.tree.map(lambda _: VMEM, outs),
        compiler_params=pltpu.CompilerParams(vmem_limit_bytes=room * 1024 * 1024),
        cost_estimate=pl.CostEstimate(flops=flops, bytes_accessed=moved, transcendentals=exps),
    )


def shape(dims, dtype=jnp.float32):
    return jax.ShapeDtypeStruct(dims, dtype)


def dot(left, right, dims, precision=None):
    return lax.dot_general(
        left, right, dims, precision=precision, preferred_element_type=jnp.float32
    )


def packet_kernel(relative, core_ref, rows_ref, columns_ref, packet_ref, raw_ref, vec_ref, sems):
    side = core_ref[0] if relative == 0 else 1 - core_ref[0]
    copies = []
    for block in range(2):
        start = pl.multiple_of(block * BLK + side * HALF, HALF)
        copies.append((
            pltpu.make_async_copy(rows_ref.at[pl.ds(start, HALF), :], raw_ref.at[block], sems.at[block]),
            pltpu.make_async_copy(
                columns_ref.at[:, pl.ds(start, HALF)], vec_ref.at[block], sems.at[2 + block]
            ),
        ))
        for copy in copies[-1]:
            copy.start()
    for block in range(2):
        for copy in copies[block]:
            copy.wait()
        widened = raw_ref[block].astype(jnp.float32)
        inverse = lax.rsqrt(jnp.sum(widened * widened, axis=1, keepdims=True) + EPSILON)
        unit = (widened * inverse).astype(jnp.bfloat16)
        for tile in range(3):
            packet_ref[block, HALF * tile : HALF * (tile + 1)] = unit[:, 128 * tile : 128 * (tile + 1)]
        for tile in range(4):
            packet_ref[block, 1536 + 64 * tile : 1600 + 64 * tile] = vec_ref[
                block, :, 128 * tile : 128 * (tile + 1)
            ]


def unit_rows(packet, start, count):
    return jnp.concatenate(
        [packet[HALF * tile + start : HALF * tile + start + count] for tile in range(3)], axis=1
    )


def vectors(packet):
    return jnp.concatenate([packet[1536 + 64 * tile : 1600 + 64 * tile] for tile in range(4)], axis=1)


def affinity_tile(left, right):
    scores = dot(left, right, NT)
    return jnp.exp2((SHARPNESS * LOG2E) * scores - (SHARPNESS * LOG2E)).astype(jnp.bfloat16)


def fold(product):
    if product.shape[0] == 128:
        return product[:64] + product[64:]
    return product


def make_tiles(left, rights, tile_ref, slot):
    whole = unit_rows(left, 0, HALF)
    for side in range(2):
        for at in range(0, HALF, 256):
            tile_ref[slot, side, :, at : at + 256] = affinity_tile(
                whole, unit_rows(rights[side], at, 256)
            )


def use_tiles(tile_ref, slot, rights, left, done_ref, done_at, part_refs, part_at, partial):
    total = fold(dot(rights[0], tile_ref[slot, 0], NT)) + fold(dot(rights[1], tile_ref[slot, 1], NT))
    done_ref[done_at] += total

    def put_part():
        for side in range(2):
            part_refs[side][part_at] += fold(dot(left, tile_ref[slot, side], NN))

    if partial is None:
        put_part()
    else:
        pl.when(partial)(put_part)


def one_pair(make, tile_ref, slot, left, rights, done_ref, done_at, part_refs, part_at, partial=None):
    take = vectors if make else (lambda ref: ref[...])
    if make:
        make_tiles(left, rights, tile_ref, slot)
    use_tiles(
        tile_ref, slot, (take(rights[0]), take(rights[1])), take(left),
        done_ref, done_at, part_refs, part_at, partial,
    )


def local_kernel(make, flags_ref, *refs):
    if make:
        own0, own1, tile_ref, done_ref, part0, part1 = refs
    else:
        tile_ref, own0, own1, done_ref, part0, part1 = refs
    for ref in (done_ref, part0, part1):
        ref[...] = jnp.zeros_like(ref)

    @pl.loop(0, 3)
    def _(slot):
        first, second = slot // 2, (slot + 1) // 2

        @pl.when(flags_ref[slot] > 0)
        def _():
            one_pair(
                make, tile_ref, slot, own0.at[first], (own0.at[second], own1.at[second]),
                done_ref, first, (part0, part1), second, slot == 1,
            )


def early_kernel(make, flags_ref, *refs):
    if make:
        own0, even0, even1, started, tile_ref, done_ref, part0, part1 = refs
    else:
        tile_ref, own0, even0, even1, started, done_ref, part0, part1 = refs
    done_ref[...] = started[...]
    for ref in (part0, part1):
        ref[...] = jnp.zeros_like(ref)

    @pl.loop(0, 4)
    def _(slot):
        left, right = slot // 2, slot % 2

        @pl.when(flags_ref[3 + slot] > 0)
        def _():
            one_pair(
                make, tile_ref, slot, own0.at[left], (even0.at[right], even1.at[right]),
                done_ref, left, (part0, part1), right,
            )


def late_kernel(make, flags_ref, list_ref, *refs):
    if make:
        odd0, own0, own1, even0, even1, *ins = refs[:9]
        tile_ref, done_ref, *parts = refs[9:]
    else:
        tile_ref, odd0, own0, own1, even0, even1, *ins = refs[:10]
        done_ref, *parts = refs[10:]
    done_ref[...] = jnp.zeros_like(done_ref)
    for ref, value in zip(parts, ins):
        ref[...] = value[...]
    base, even = flags_ref[11], flags_ref[12] > 0

    def far_is_live(left, right):
        first = base - 2 + jnp.where(even, left, right)
        second = base + 2 + jnp.where(even, right, left)
        hits = [
            (list_ref[0, at] == first) & (list_ref[1, at] == second)
            for at in range(list_ref.shape[1])
        ]
        return functools.reduce(jnp.logical_or, hits)

    for kind in range(2):
        rights = ((own0, own1), (even0, even1))[kind]
        part_refs = (parts[:2], parts[2:])[kind]

        @pl.loop(0, 4)
        def _(index):
            left, right = index // 2, index % 2

            live = far_is_live(left, right) if kind else flags_ref[7 + index] > 0

            @pl.when(live)
            def _():
                one_pair(
                    make, tile_ref, kind * 4 + index, odd0.at[left],
                    (rights[0].at[right], rights[1].at[right]), done_ref, left, part_refs, right,
                )


def total_kernel(done, part_mine, part_other, from_odd, from_even, sum_ref, pair_ref=None):
    for block in range(2):
        value = (
            done[block] + part_mine[block] + part_other[block] + from_odd[block] + from_even[block]
        )
        sum_ref[block] = value
        if pair_ref is not None:
            high = value.astype(jnp.bfloat16)
            pair_ref[block, :64] = high
            pair_ref[block, 64:] = (value - high.astype(jnp.float32)).astype(jnp.bfloat16)


def gram_of(value_ref, scale):
    gram = dot(value_ref[0], value_ref[0], NT, HIGHEST) + dot(value_ref[1], value_ref[1], NT, HIGHEST)
    gram = gram * scale
    return jnp.concatenate([gram[:32], gram[32:]], axis=1)


def gram_kernel(scale, value_ref, gram_ref):
    gram_ref[...] = gram_of(value_ref, scale)


def second_gram_kernel(scale, core_ref, first_ref, value_ref, keep_ref, give_ref, swap_ref):
    second = gram_of(value_ref, scale)
    first = first_ref[...]
    lead = core_ref[0] == 0
    keep_ref[...] = jnp.where(lead, first, second)
    give_ref[...] = jnp.where(lead, second, first)
    swap_ref[...] = value_ref[1 - core_ref[0]]


def eliminate(packed):
    lanes = lax.broadcasted_iota(jnp.int32, (8, 64), 1)
    subs = lax.broadcasted_iota(jnp.int32, (8, 64), 0)
    deep = lax.broadcasted_iota(jnp.int32, (8, 128), 0)
    states = []
    for matrix in packed:
        whole = jnp.concatenate([matrix[:, :64], matrix[:, 64:]], axis=0)
        states.append([
            jnp.concatenate(
                [whole[8 * b : 8 * b + 8], (lanes == subs + 8 * b).astype(jnp.float32)], axis=1
            )
            for b in range(8)
        ])
    scales = [[] for _ in states]
    for at in range(8):
        spreads = [
            {
                b: [jnp.broadcast_to(state[b][:, k : k + 1], (8, 128)) for k in range(8 * at, 8 * at + 8)]
                for b in range(at, 8)
            }
            for state in states
        ]
        pivots = [jnp.zeros((8, 128), jnp.float32) for _ in states]
        for sub in range(8):
            for n, (state, spread_of) in enumerate(zip(states, spreads)):
                pivot = spread_of[at][sub][sub : sub + 1, :]
                inverse = 1.0 / pivot
                pivots[n] = jnp.where(deep == sub, pivot, pivots[n])
                row = state[at][sub : sub + 1, :] * inverse
                ahead = {j: spread_of[at][j][sub : sub + 1, :] * inverse for j in range(sub + 1, 8)}
                for b in range(at, 8):
                    column = spread_of[b][sub]
                    if b == at:
                        column = jnp.where(deep > sub, column, 0.0)
                    for j, value in ahead.items():
                        spread_of[b][j] = spread_of[b][j] - column * value
                    state[b] = state[b] - column * row
        for n, pivot in enumerate(pivots):
            scales[n].append(lax.rsqrt(pivot))
    uppers, inverses = [], []
    for state, scale in zip(states, scales):
        whole = jnp.concatenate([rows * by for rows, by in zip(state, scale)], axis=0)
        uppers.append(whole[:, :64])
        inverses.append(whole[:, 64:])
    return uppers, inverses


def copies_kernel(*refs):
    *value_refs, copies_ref = refs
    total = None
    for ref in value_refs:
        value = ref[...] if len(ref.shape) == 2 else jnp.sum(ref[...], axis=0)
        total = value if total is None else total + value
    for at in range(copies_ref.shape[0]):
        copies_ref[at] = total


def finish_kernel(core_ref, mine_ref, other_ref, value_ref, got_ref, basis_ref, factor_ref):
    core = core_ref[0]
    lead = core == 0
    mine, other = mine_ref[...], other_ref[...]
    first, second = jnp.where(lead, mine, other), jnp.where(lead, other, mine)
    uppers, inverses = eliminate([first, second])
    factor = dot(uppers[1], inverses[0], NT, HIGHEST)
    wide = lax.broadcasted_iota(jnp.int32, (64, 64), 1)
    tall = lax.broadcasted_iota(jnp.int32, (64, 64), 0)
    factor_ref[...] = jnp.where(wide >= tall, factor, 0.0)
    low = jnp.where(wide <= tall, inverses[1], 0.0)
    here = pl.multiple_of(core * HALF, HALF)
    there = pl.multiple_of((1 - core) * HALF, HALF)
    basis_ref[:, pl.ds(here, HALF)] = dot(low, value_ref[core], NN, HIGHEST)
    basis_ref[:, pl.ds(there, HALF)] = dot(low, got_ref[...], NN, HIGHEST)


def exchange(value, start):
    links = []
    for r in range(start, lax.axis_size("rows") - 1, 2):
        links += [(r, r + 1), (r + 1, r)]
    return lax.ppermute(value, "rows", links)


def to_even(value):
    return exchange(value, 0)


def to_odd(value):
    return exchange(value, 1)


def swap(value):
    return lax.ppermute(value, "cols", [(0, 1), (1, 0)])


def swap_blocks(value):
    return jnp.stack([swap(value[block]) for block in range(2)])


SLOTS = [(0, 0), (0, 1), (1, 0), (1, 1)]


def own_flags_and_list(pair_list, base):
    own = jnp.concatenate([pair_list.T, swap(pair_list.T)], axis=1)
    before = lax.ppermute(own, "rows", [(r, r + 1) for r in range(lax.axis_size("rows") - 1)])
    within, idle = [(0, 0), (0, 1), (1, 1)], [(100, 100)] * 4

    def table(entries):
        return jnp.array([64 * i + j for i, j in entries], jnp.int32)

    even = lax.axis_index("rows") % 2 == 0
    wanted = jnp.where(
        even,
        table(within + [(left, 2 + right) for left, right in SLOTS] + idle),
        table(within + idle + [(right, 2 + left) for left, right in SLOTS]),
    )
    codes = (own[0] - base) * 64 + (own[1] - base)
    hit = (codes[None, :] == wanted[:, None]) & (own[0][None, :] >= 0)
    flags = jnp.any(hit, axis=1).astype(jnp.int32)
    return jnp.concatenate([flags, base[None], even.astype(jnp.int32)[None]]), before


def spread(done, own0, own1, out_odd, even0, even1):
    from_odd = to_odd(out_odd)
    from_even = to_even(even0 + swap(even1))
    return done, own0, swap(own1), from_odd, from_even


def sum_over_chips(*values):
    planes = [[(x * PLANES + z) * RING + y for x in range(ACROSS) for y in range(RING)] for z in range(PLANES)]
    lines = [[(x * PLANES + z) * RING + y for z in range(PLANES)] for x in range(ACROSS) for y in range(RING)]
    for groups in (planes, lines):
        copies = call(copies_kernel, shape((len(groups[0]), 32, 128)), 10**5, 10**5)(
            in_specs=[VMEM] * len(values)
        )(*values)
        values = [
            lax.all_to_all(copies, "rows", 0, 0, axis_index_groups=groups, tiled=True)
        ]
    return values[0].sum(0)


def local(embeddings, test_matrix, pair_list):
    rows_dev = embeddings.shape[0]
    columns = test_matrix.shape[1]
    bf16, f32 = jnp.bfloat16, jnp.float32
    core = lax.axis_index("cols").astype(jnp.int32)
    core_ref = core.reshape(1)
    base = (lax.axis_index("rows") * 2).astype(jnp.int32)
    scale = 1.0 / (rows_dev * lax.axis_size("rows"))

    test_columns = pltpu.with_memory_space_constraint(test_matrix.T, pltpu.HBM)
    embeddings = pltpu.with_memory_space_constraint(embeddings, pltpu.HBM)

    def packet(relative):
        return call(
            functools.partial(packet_kernel, relative), shape((2, 1792, 128), bf16), 10**4, 10**4,
        )(
            in_specs=[SMEM, HBM, HBM],
            scratch_shapes=[
                pltpu.VMEM((2, HALF, 384), bf16),
                pltpu.VMEM((2, columns, HALF), bf16),
                pltpu.SemaphoreType.DMA((4,)),
            ],
        )(core_ref, embeddings, test_columns)

    own0 = packet(0)
    even0 = to_even(own0)
    odd0 = to_odd(own0)
    own1, pair_list = lax.optimization_barrier((packet(1), pair_list))
    flags, before = own_flags_and_list(pair_list, base)

    sum_shape = shape((2, 64, HALF))

    def tiles(count):
        return shape((count, 2, HALF, HALF), bf16)

    tiles_own, done, own_part0, own_part1 = call(
        functools.partial(local_kernel, True), (tiles(3),) + 3 * (sum_shape,), 10**4, 10**4
    )(in_specs=[SMEM] + [VMEM] * 2)(flags, own0, own1)
    done, even0 = lax.optimization_barrier((done, even0))
    even1 = swap_blocks(even0)
    tiles_early, done, even_part0, even_part1 = call(
        functools.partial(early_kernel, True), (tiles(4),) + 3 * (sum_shape,), 10**4, 10**4
    )(in_specs=[SMEM] + [VMEM] * 4)(flags, own0, even0, even1, done)
    done, odd0, before = lax.optimization_barrier((done, odd0, before))
    tiles_late, out_odd, own_part0, own_part1, even_part0, even_part1 = call(
        functools.partial(late_kernel, True), (tiles(8),) + 5 * (sum_shape,), 10**9, 10**6
    )(in_specs=[SMEM] * 2 + [VMEM] * 9)(
        flags, before, odd0, own0, own1, even0, even1, own_part0, own_part1, even_part0, even_part1
    )
    sketch, pair0 = call(total_kernel, (sum_shape, shape((2, 128, HALF), bf16)), 10**6, 2 * 10**6)(
        in_specs=[VMEM] * 5
    )(*spread(done, own_part0, own_part1, out_odd, even_part0, even_part1))

    even0 = to_even(pair0)
    odd0 = to_odd(pair0)
    gram_shape = shape((32, 128))
    first_gram = call(functools.partial(gram_kernel, scale), gram_shape, 10**4, 10**4)(
        in_specs=[VMEM]
    )(sketch)
    pair1 = swap(pair0)
    done, own_part0, own_part1 = call(
        functools.partial(local_kernel, False), 3 * (sum_shape,), 10**4, 10**4
    )(in_specs=[SMEM] + [VMEM] * 3)(flags, tiles_own, pair0, pair1)
    even1 = swap_blocks(even0)
    done, even_part0, even_part1 = call(
        functools.partial(early_kernel, False), 3 * (sum_shape,), 10**4, 10**4
    )(in_specs=[SMEM] + [VMEM] * 5)(flags, tiles_early, pair0, even0, even1, done)
    done, odd0 = lax.optimization_barrier((done, odd0))
    out_odd, own_part0, own_part1, even_part0, even_part1 = call(
        functools.partial(late_kernel, False), 5 * (sum_shape,), 10**9, 10**6
    )(in_specs=[SMEM] * 2 + [VMEM] * 10)(
        flags, before, tiles_late, odd0, pair0, pair1, even0, even1,
        own_part0, own_part1, even_part0, even_part1,
    )
    image = call(total_kernel, sum_shape, 10**6, 2 * 10**6)(in_specs=[VMEM] * 5)(
        *spread(done, own_part0, own_part1, out_odd, even_part0, even_part1)
    )
    keep, give, half = call(
        functools.partial(second_gram_kernel, scale),
        (gram_shape, gram_shape, shape((64, HALF))),
        10**8, 10**6,
    )(in_specs=[SMEM, VMEM, VMEM])(core_ref, first_gram, image)
    got = swap(half)
    mine = sum_over_chips(keep, swap(give))
    other = swap(mine)
    basis, factor = call(finish_kernel, (shape((64, BLK)), shape((64, 64))), 10**8, 10**6)(
        in_specs=[SMEM] + [VMEM] * 4
    )(core_ref, mine, other, image, got)
    return basis.T, factor


def solution(mesh):
    in_specs = (P("rows", None), P("rows", None), P(("rows", "cols"), None))
    out_specs = (P(("rows", "cols"), None), P())
    return jax.shard_map(local, mesh=mesh, in_specs=in_specs, out_specs=out_specs, check_vma=False)
```

```python
import functools

import jax
import jax.numpy as jnp
from jax import lax
from jax.experimental import pallas as pl
from jax.experimental.pallas import tpu as pltpu
from jax.sharding import PartitionSpec as P

BLK = 1024
HALF = 512
SHARPNESS = 6.0
EPSILON = 1e-06
LOG2E = 1.4426950408889634
HIGHEST = lax.Precision.HIGHEST
VMEM = pl.BlockSpec(memory_space=pltpu.VMEM)
HBM = pl.BlockSpec(memory_space=pltpu.HBM)
SMEM = pl.BlockSpec(memory_space=pltpu.SMEM)
NT = (((1,), (1,)), ((), ()))
NN = (((1,), (0,)), ((), ()))
ACROSS, PLANES, RING = 4, 8, 4


def call(kernel, outs, flops, moved, exps=0, room=16):
    return functools.partial(
        pl.pallas_call,
        kernel,
        out_shape=outs,
        out_specs=jax.tree.map(lambda _: VMEM, outs),
        compiler_params=pltpu.CompilerParams(vmem_limit_bytes=room * 1024 * 1024),
        cost_estimate=pl.CostEstimate(flops=flops, bytes_accessed=moved, transcendentals=exps),
    )


def shape(dims, dtype=jnp.float32):
    return jax.ShapeDtypeStruct(dims, dtype)


def dot(left, right, dims, precision=None):
    return lax.dot_general(
        left, right, dims, precision=precision, preferred_element_type=jnp.float32
    )


def packet_kernel(relative, core_ref, rows_ref, columns_ref, packet_ref, raw_ref, vec_ref, sems):
    side = core_ref[0] if relative == 0 else 1 - core_ref[0]
    copies = []
    for block in range(2):
        start = pl.multiple_of(block * BLK + side * HALF, HALF)
        copies.append((
            pltpu.make_async_copy(rows_ref.at[pl.ds(start, HALF), :], raw_ref.at[block], sems.at[block]),
            pltpu.make_async_copy(
                columns_ref.at[:, pl.ds(start, HALF)], vec_ref.at[block], sems.at[2 + block]
            ),
        ))
        for copy in copies[-1]:
            copy.start()
    for block in range(2):
        for copy in copies[block]:
            copy.wait()
        widened = raw_ref[block].astype(jnp.float32)
        inverse = lax.rsqrt(jnp.sum(widened * widened, axis=1, keepdims=True) + EPSILON)
        unit = (widened * inverse).astype(jnp.bfloat16)
        for tile in range(3):
            packet_ref[block, HALF * tile : HALF * (tile + 1)] = unit[:, 128 * tile : 128 * (tile + 1)]
        for tile in range(4):
            packet_ref[block, 1536 + 64 * tile : 1600 + 64 * tile] = vec_ref[
                block, :, 128 * tile : 128 * (tile + 1)
            ]


def unit_rows(packet, start, count):
    return jnp.concatenate(
        [packet[HALF * tile + start : HALF * tile + start + count] for tile in range(3)], axis=1
    )


def vectors(packet):
    return jnp.concatenate([packet[1536 + 64 * tile : 1600 + 64 * tile] for tile in range(4)], axis=1)


def affinity_tile(left, right):
    scores = dot(left, right, NT)
    return jnp.exp2((SHARPNESS * LOG2E) * scores - (SHARPNESS * LOG2E)).astype(jnp.bfloat16)


def fold(product):
    if product.shape[0] == 128:
        return product[:64] + product[64:]
    return product


def make_tiles(left, rights, tile_ref, slot):
    whole = unit_rows(left, 0, HALF)
    for side in range(2):
        for at in range(0, HALF, 256):
            tile_ref[slot, side, :, at : at + 256] = affinity_tile(
                whole, unit_rows(rights[side], at, 256)
            )


def use_tiles(tile_ref, slot, rights, left, done_ref, done_at, part_refs, part_at, partial):
    total = fold(dot(rights[0], tile_ref[slot, 0], NT)) + fold(dot(rights[1], tile_ref[slot, 1], NT))
    done_ref[done_at] += total

    def put_part():
        for side in range(2):
            part_refs[side][part_at] += fold(dot(left, tile_ref[slot, side], NN))

    if partial is None:
        put_part()
    else:
        pl.when(partial)(put_part)


def one_pair(make, tile_ref, slot, left, rights, done_ref, done_at, part_refs, part_at, partial=None):
    take = vectors if make else (lambda ref: ref[...])
    if make:
        make_tiles(left, rights, tile_ref, slot)
    use_tiles(
        tile_ref, slot, (take(rights[0]), take(rights[1])), take(left),
        done_ref, done_at, part_refs, part_at, partial,
    )


def local_kernel(make, flags_ref, *refs):
    if make:
        own0, own1, tile_ref, done_ref, part0, part1 = refs
    else:
        tile_ref, own0, own1, done_ref, part0, part1 = refs
    for ref in (done_ref, part0, part1):
        ref[...] = jnp.zeros_like(ref)

    @pl.loop(0, 3)
    def _(slot):
        first, second = slot // 2, (slot + 1) // 2

        @pl.when(flags_ref[slot] > 0)
        def _():
            one_pair(
                make, tile_ref, slot, own0.at[first], (own0.at[second], own1.at[second]),
                done_ref, first, (part0, part1), second, slot == 1,
            )


def early_kernel(make, flags_ref, *refs):
    if make:
        own0, even0, even1, started, tile_ref, done_ref, part0, part1 = refs
    else:
        tile_ref, own0, even0, even1, started, done_ref, part0, part1 = refs
    done_ref[...] = started[...]
    for ref in (part0, part1):
        ref[...] = jnp.zeros_like(ref)

    @pl.loop(0, 4)
    def _(slot):
        left, right = slot // 2, slot % 2

        @pl.when(flags_ref[3 + slot] > 0)
        def _():
            one_pair(
                make, tile_ref, slot, own0.at[left], (even0.at[right], even1.at[right]),
                done_ref, left, (part0, part1), right,
            )


def late_kernel(make, flags_ref, far_ref, *refs):
    if make:
        odd0, own0, own1, even0, even1, *ins = refs[:9]
        tile_ref, done_ref, *parts = refs[9:]
    else:
        tile_ref, odd0, own0, own1, even0, even1, *ins = refs[:10]
        done_ref, *parts = refs[10:]
    done_ref[...] = jnp.zeros_like(done_ref)
    for ref, value in zip(parts, ins):
        ref[...] = value[...]
    for kind in range(2):
        rights = ((own0, own1), (even0, even1))[kind]
        part_refs = (parts[:2], parts[2:])[kind]
        flag_ref, flag_at = ((flags_ref, 7), (far_ref, 0))[kind]

        @pl.loop(0, 4)
        def _(index):
            left, right = index // 2, index % 2

            @pl.when(flag_ref[flag_at + index] > 0)
            def _():
                one_pair(
                    make, tile_ref, kind * 4 + index, odd0.at[left],
                    (rights[0].at[right], rights[1].at[right]), done_ref, left, part_refs, right,
                )


def total_kernel(done, part_mine, part_other, from_odd, from_even, sum_ref, pair_ref=None):
    for block in range(2):
        value = (
            done[block] + part_mine[block] + part_other[block] + from_odd[block] + from_even[block]
        )
        sum_ref[block] = value
        if pair_ref is not None:
            high = value.astype(jnp.bfloat16)
            pair_ref[block, :64] = high
            pair_ref[block, 64:] = (value - high.astype(jnp.float32)).astype(jnp.bfloat16)


def gram_of(value_ref, scale):
    gram = dot(value_ref[0], value_ref[0], NT, HIGHEST) + dot(value_ref[1], value_ref[1], NT, HIGHEST)
    gram = gram * scale
    return jnp.concatenate([gram[:32], gram[32:]], axis=1)


def gram_kernel(scale, value_ref, gram_ref):
    gram_ref[...] = gram_of(value_ref, scale)


def second_gram_kernel(scale, core_ref, first_ref, value_ref, keep_ref, give_ref, swap_ref):
    second = gram_of(value_ref, scale)
    first = first_ref[...]
    lead = core_ref[0] == 0
    keep_ref[...] = jnp.where(lead, first, second)
    give_ref[...] = jnp.where(lead, second, first)
    swap_ref[...] = value_ref[1 - core_ref[0]]


def eliminate(packed):
    lanes = lax.broadcasted_iota(jnp.int32, (8, 64), 1)
    subs = lax.broadcasted_iota(jnp.int32, (8, 64), 0)
    deep = lax.broadcasted_iota(jnp.int32, (8, 128), 0)
    states = []
    for matrix in packed:
        whole = jnp.concatenate([matrix[:, :64], matrix[:, 64:]], axis=0)
        states.append([
            jnp.concatenate(
                [whole[8 * b : 8 * b + 8], (lanes == subs + 8 * b).astype(jnp.float32)], axis=1
            )
            for b in range(8)
        ])
    scales = [[] for _ in states]
    for at in range(8):
        spreads = [
            {
                b: [jnp.broadcast_to(state[b][:, k : k + 1], (8, 128)) for k in range(8 * at, 8 * at + 8)]
                for b in range(at, 8)
            }
            for state in states
        ]
        pivots = [jnp.zeros((8, 128), jnp.float32) for _ in states]
        for sub in range(8):
            for n, (state, spread_of) in enumerate(zip(states, spreads)):
                pivot = spread_of[at][sub][sub : sub + 1, :]
                inverse = 1.0 / pivot
                pivots[n] = jnp.where(deep == sub, pivot, pivots[n])
                row = state[at][sub : sub + 1, :] * inverse
                ahead = {j: spread_of[at][j][sub : sub + 1, :] * inverse for j in range(sub + 1, 8)}
                for b in range(at, 8):
                    column = spread_of[b][sub]
                    if b == at:
                        column = jnp.where(deep > sub, column, 0.0)
                    for j, value in ahead.items():
                        spread_of[b][j] = spread_of[b][j] - column * value
                    state[b] = state[b] - column * row
        for n, pivot in enumerate(pivots):
            scales[n].append(lax.rsqrt(pivot))
    uppers, inverses = [], []
    for state, scale in zip(states, scales):
        whole = jnp.concatenate([rows * by for rows, by in zip(state, scale)], axis=0)
        uppers.append(whole[:, :64])
        inverses.append(whole[:, 64:])
    return uppers, inverses


def copies_kernel(*refs):
    *value_refs, copies_ref = refs
    total = None
    for ref in value_refs:
        value = ref[...] if len(ref.shape) == 2 else jnp.sum(ref[...], axis=0)
        total = value if total is None else total + value
    for at in range(copies_ref.shape[0]):
        copies_ref[at] = total


def finish_kernel(core_ref, mine_ref, other_ref, value_ref, got_ref, basis_ref, factor_ref):
    core = core_ref[0]
    lead = core == 0
    mine, other = mine_ref[...], other_ref[...]
    first, second = jnp.where(lead, mine, other), jnp.where(lead, other, mine)
    uppers, inverses = eliminate([first, second])
    factor = dot(uppers[1], inverses[0], NT, HIGHEST)
    wide = lax.broadcasted_iota(jnp.int32, (64, 64), 1)
    tall = lax.broadcasted_iota(jnp.int32, (64, 64), 0)
    factor_ref[...] = jnp.where(wide >= tall, factor, 0.0)
    low = jnp.where(wide <= tall, inverses[1], 0.0)
    here = pl.multiple_of(core * HALF, HALF)
    there = pl.multiple_of((1 - core) * HALF, HALF)
    basis_ref[:, pl.ds(here, HALF)] = dot(low, value_ref[core], NN, HIGHEST)
    basis_ref[:, pl.ds(there, HALF)] = dot(low, got_ref[...], NN, HIGHEST)


def exchange(value, start):
    links = []
    for r in range(start, lax.axis_size("rows") - 1, 2):
        links += [(r, r + 1), (r + 1, r)]
    return lax.ppermute(value, "rows", links)


def to_even(value):
    return exchange(value, 0)


def to_odd(value):
    return exchange(value, 1)


def swap(value):
    return lax.ppermute(value, "cols", [(0, 1), (1, 0)])


def swap_blocks(value):
    return jnp.stack([swap(value[block]) for block in range(2)])


def live_flags(pairs, base, even_codes, odd_codes):
    none = (100, 100)

    def table(entries):
        return jnp.array([64 * i + j for i, j in (none if e is None else e for e in entries)], jnp.int32)

    even_row = lax.axis_index("rows") % 2 == 0
    wanted = jnp.where(even_row, table(even_codes), table(odd_codes))
    codes = (pairs[:, 0] - base) * 64 + (pairs[:, 1] - base)
    hit = (codes[None, :] == wanted[:, None]) & (pairs[None, :, 0] >= 0)
    return jnp.any(hit, axis=1).astype(jnp.int32)


SLOTS = [(0, 0), (0, 1), (1, 0), (1, 1)]


def own_flags_and_list(pair_list, base):
    own = jnp.concatenate([pair_list, swap(pair_list)], axis=0)
    before = lax.ppermute(own, "rows", [(r, r + 1) for r in range(lax.axis_size("rows") - 1)])
    within, idle = [(0, 0), (0, 1), (1, 1)], [None] * 4
    flags = live_flags(
        own, base,
        within + [(left, 2 + right) for left, right in SLOTS] + idle,
        within + idle + [(right, 2 + left) for left, right in SLOTS],
    )
    return flags, before


def flags_of_far(before, base):
    return live_flags(
        before, base,
        [(left - 2, 2 + right) for left, right in SLOTS],
        [(right - 2, 2 + left) for left, right in SLOTS],
    )


def spread(done, own0, own1, out_odd, even0, even1):
    from_odd = to_odd(out_odd)
    from_even = to_even(even0 + swap(even1))
    return done, own0, swap(own1), from_odd, from_even


def sum_over_chips(*values):
    planes = [[(x * PLANES + z) * RING + y for x in range(ACROSS) for y in range(RING)] for z in range(PLANES)]
    lines = [[(x * PLANES + z) * RING + y for z in range(PLANES)] for x in range(ACROSS) for y in range(RING)]
    for groups in (planes, lines):
        copies = call(copies_kernel, shape((len(groups[0]), 32, 128)), 10**5, 10**5)(
            in_specs=[VMEM] * len(values)
        )(*values)
        values = [
            lax.all_to_all(copies, "rows", 0, 0, axis_index_groups=groups, tiled=True)
        ]
    return values[0].sum(0)


def local(embeddings, test_matrix, pair_list):
    rows_dev = embeddings.shape[0]
    columns = test_matrix.shape[1]
    bf16, f32 = jnp.bfloat16, jnp.float32
    core = lax.axis_index("cols").astype(jnp.int32)
    core_ref = core.reshape(1)
    base = (lax.axis_index("rows") * 2).astype(jnp.int32)
    scale = 1.0 / (rows_dev * lax.axis_size("rows"))

    test_columns = pltpu.with_memory_space_constraint(test_matrix.T, pltpu.HBM)
    embeddings = pltpu.with_memory_space_constraint(embeddings, pltpu.HBM)

    def packet(relative):
        return call(
            functools.partial(packet_kernel, relative), shape((2, 1792, 128), bf16), 10**4, 10**4,
        )(
            in_specs=[SMEM, HBM, HBM],
            scratch_shapes=[
                pltpu.VMEM((2, HALF, 384), bf16),
                pltpu.VMEM((2, columns, HALF), bf16),
                pltpu.SemaphoreType.DMA((4,)),
            ],
        )(core_ref, embeddings, test_columns)

    own0 = packet(0)
    even0 = to_even(own0)
    odd0 = to_odd(own0)
    own1, pair_list = lax.optimization_barrier((packet(1), pair_list))
    flags, before = own_flags_and_list(pair_list, base)

    sum_shape = shape((2, 64, HALF))

    def tiles(count):
        return shape((count, 2, HALF, HALF), bf16)

    tiles_own, done, own_part0, own_part1 = call(
        functools.partial(local_kernel, True), (tiles(3),) + 3 * (sum_shape,), 10**4, 10**4
    )(in_specs=[SMEM] + [VMEM] * 2)(flags, own0, own1)
    done, even0 = lax.optimization_barrier((done, even0))
    even1 = swap_blocks(even0)
    tiles_early, done, even_part0, even_part1 = call(
        functools.partial(early_kernel, True), (tiles(4),) + 3 * (sum_shape,), 10**4, 10**4
    )(in_specs=[SMEM] + [VMEM] * 4)(flags, own0, even0, even1, done)
    done, odd0, before = lax.optimization_barrier((done, odd0, before))
    far_flags = flags_of_far(before, base)
    tiles_late, out_odd, own_part0, own_part1, even_part0, even_part1 = call(
        functools.partial(late_kernel, True), (tiles(8),) + 5 * (sum_shape,), 10**9, 10**6
    )(in_specs=[SMEM] * 2 + [VMEM] * 9)(
        flags, far_flags, odd0, own0, own1, even0, even1, own_part0, own_part1, even_part0, even_part1
    )
    sketch, pair0 = call(total_kernel, (sum_shape, shape((2, 128, HALF), bf16)), 10**6, 2 * 10**6)(
        in_specs=[VMEM] * 5
    )(*spread(done, own_part0, own_part1, out_odd, even_part0, even_part1))

    even0 = to_even(pair0)
    odd0 = to_odd(pair0)
    gram_shape = shape((32, 128))
    first_gram = call(functools.partial(gram_kernel, scale), gram_shape, 10**4, 10**4)(
        in_specs=[VMEM]
    )(sketch)
    pair1 = swap(pair0)
    done, own_part0, own_part1 = call(
        functools.partial(local_kernel, False), 3 * (sum_shape,), 10**4, 10**4
    )(in_specs=[SMEM] + [VMEM] * 3)(flags, tiles_own, pair0, pair1)
    even1 = swap_blocks(even0)
    done, even_part0, even_part1 = call(
        functools.partial(early_kernel, False), 3 * (sum_shape,), 10**4, 10**4
    )(in_specs=[SMEM] + [VMEM] * 5)(flags, tiles_early, pair0, even0, even1, done)
    done, odd0 = lax.optimization_barrier((done, odd0))
    out_odd, own_part0, own_part1, even_part0, even_part1 = call(
        functools.partial(late_kernel, False), 5 * (sum_shape,), 10**9, 10**6
    )(in_specs=[SMEM] * 2 + [VMEM] * 10)(
        flags, far_flags, tiles_late, odd0, pair0, pair1, even0, even1,
        own_part0, own_part1, even_part0, even_part1,
    )
    image = call(total_kernel, sum_shape, 10**6, 2 * 10**6)(in_specs=[VMEM] * 5)(
        *spread(done, own_part0, own_part1, out_odd, even_part0, even_part1)
    )
    keep, give, half = call(
        functools.partial(second_gram_kernel, scale),
        (gram_shape, gram_shape, shape((64, HALF))),
        10**8, 10**6,
    )(in_specs=[SMEM, VMEM, VMEM])(core_ref, first_gram, image)
    got = swap(half)
    mine = sum_over_chips(keep, swap(give))
    other = swap(mine)
    basis, factor = call(finish_kernel, (shape((64, BLK)), shape((64, 64))), 10**8, 10**6)(
        in_specs=[SMEM] + [VMEM] * 4
    )(core_ref, mine, other, image, got)
    return basis.T, factor


def solution(mesh):
    in_specs = (P("rows", None), P("rows", None), P(("rows", "cols"), None))
    out_specs = (P(("rows", "cols"), None), P())
    return jax.shard_map(local, mesh=mesh, in_specs=in_specs, out_specs=out_specs, check_vma=False)
```

```python
import functools

import jax
import jax.numpy as jnp
from jax import lax
from jax.experimental import pallas as pl
from jax.experimental.pallas import tpu as pltpu
from jax.sharding import PartitionSpec as P

BLK = 1024
HALF = 512
QUARTER = 256
SHARPNESS = 6.0
EPSILON = 1e-06
LOG2E = 1.4426950408889634
HIGHEST = lax.Precision.HIGHEST
VMEM = pl.BlockSpec(memory_space=pltpu.VMEM)
HBM = pl.BlockSpec(memory_space=pltpu.HBM)
SMEM = pl.BlockSpec(memory_space=pltpu.SMEM)
NT = (((1,), (1,)), ((), ()))
NN = (((1,), (0,)), ((), ()))
ACROSS, PLANES, RING = 4, 8, 4


def call(kernel, outs, flops, moved, exps=0, room=16):
    return functools.partial(
        pl.pallas_call,
        kernel,
        out_shape=outs,
        out_specs=jax.tree.map(lambda _: VMEM, outs),
        compiler_params=pltpu.CompilerParams(vmem_limit_bytes=room * 1024 * 1024),
        cost_estimate=pl.CostEstimate(flops=flops, bytes_accessed=moved, transcendentals=exps),
    )


def shape(dims, dtype=jnp.float32):
    return jax.ShapeDtypeStruct(dims, dtype)


def dot(left, right, dims, precision=None):
    return lax.dot_general(
        left, right, dims, precision=precision, preferred_element_type=jnp.float32
    )


def packet_kernel(relative, core_ref, rows_ref, columns_ref, packet_ref, raw_ref, vec_ref, sems):
    side = core_ref[0] if relative == 0 else 1 - core_ref[0]
    copies = []
    for block in range(2):
        start = pl.multiple_of(block * BLK + side * HALF, HALF)
        for part in range(2):
            rows = pl.ds(pl.multiple_of(start + part * QUARTER, QUARTER), QUARTER)
            copies.append(
                pltpu.make_async_copy(
                    rows_ref.at[rows, :],
                    raw_ref.at[block, pl.ds(part * QUARTER, QUARTER)],
                    sems.at[2 * block + part],
                )
            )
        copies.append(
            pltpu.make_async_copy(
                columns_ref.at[:, pl.ds(start, HALF)], vec_ref.at[block], sems.at[4 + block]
            )
        )
    for copy in copies:
        copy.start()
    for block in range(2):
        for part in range(2):
            copies[3 * block + part].wait()
            here = slice(part * QUARTER, (part + 1) * QUARTER)
            widened = raw_ref[block, here].astype(jnp.float32)
            inverse = lax.rsqrt(jnp.sum(widened * widened, axis=1, keepdims=True) + EPSILON)
            unit = (widened * inverse).astype(jnp.bfloat16)
            for tile in range(3):
                first = HALF * tile + part * QUARTER
                packet_ref[block, first : first + QUARTER] = unit[:, 128 * tile : 128 * (tile + 1)]
        copies[3 * block + 2].wait()
        for tile in range(4):
            packet_ref[block, 1536 + 64 * tile : 1600 + 64 * tile] = vec_ref[
                block, :, 128 * tile : 128 * (tile + 1)
            ]


def unit_rows(packet, start, count):
    return jnp.concatenate(
        [packet[HALF * tile + start : HALF * tile + start + count] for tile in range(3)], axis=1
    )


def vectors(packet):
    return jnp.concatenate([packet[1536 + 64 * tile : 1600 + 64 * tile] for tile in range(4)], axis=1)


def affinity_tile(left, right):
    scores = dot(left, right, NT)
    return jnp.exp2((SHARPNESS * LOG2E) * scores - (SHARPNESS * LOG2E)).astype(jnp.bfloat16)


def fold(product):
    if product.shape[0] == 128:
        return product[:64] + product[64:]
    return product


def make_tiles(left, rights, tile_ref, slot):
    for side in range(2):
        for at in range(0, HALF, 256):
            right = unit_rows(rights[side], at, 256)
            for row in range(0, HALF, 256):
                tile_ref[slot, side, row : row + 256, at : at + 256] = affinity_tile(
                    unit_rows(left, row, 256), right
                )


def use_tiles(tile_ref, slot, rights, left, done_ref, done_at, part_refs, part_at, partial):
    total = fold(dot(rights[0], tile_ref[slot, 0], NT)) + fold(dot(rights[1], tile_ref[slot, 1], NT))
    done_ref[done_at] += total

    def put_part():
        for side in range(2):
            part_refs[side][part_at] += fold(dot(left, tile_ref[slot, side], NN))

    if partial is None:
        put_part()
    else:
        pl.when(partial)(put_part)


def one_pair(make, tile_ref, slot, left, rights, done_ref, done_at, part_refs, part_at, partial=None):
    take = vectors if make else (lambda ref: ref[...])
    if make:
        make_tiles(left, rights, tile_ref, slot)
    use_tiles(
        tile_ref, slot, (take(rights[0]), take(rights[1])), take(left),
        done_ref, done_at, part_refs, part_at, partial,
    )


def local_kernel(make, flags_ref, *refs):
    if make:
        own0, own1, tile_ref, done_ref, part0, part1 = refs
    else:
        tile_ref, own0, own1, done_ref, part0, part1 = refs
    for ref in (done_ref, part0, part1):
        ref[...] = jnp.zeros_like(ref)

    @pl.loop(0, 3)
    def _(slot):
        first, second = slot // 2, (slot + 1) // 2

        @pl.when(flags_ref[slot] > 0)
        def _():
            one_pair(
                make, tile_ref, slot, own0.at[first], (own0.at[second], own1.at[second]),
                done_ref, first, (part0, part1), second, slot == 1,
            )


def early_kernel(make, flags_ref, *refs):
    if make:
        own0, even0, even1, started, tile_ref, done_ref, part0, part1 = refs
    else:
        tile_ref, own0, even0, even1, started, done_ref, part0, part1 = refs
    done_ref[...] = started[...]
    for ref in (part0, part1):
        ref[...] = jnp.zeros_like(ref)

    @pl.loop(0, 4)
    def _(slot):
        left, right = slot // 2, slot % 2

        @pl.when(flags_ref[3 + slot] > 0)
        def _():
            one_pair(
                make, tile_ref, slot, own0.at[left], (even0.at[right], even1.at[right]),
                done_ref, left, (part0, part1), right,
            )


def late_kernel(make, flags_ref, far_ref, *refs):
    if make:
        odd0, own0, own1, even0, even1, *ins = refs[:9]
        tile_ref, done_ref, own_part, even_part, give_ref = refs[9:]
    else:
        tile_ref, odd0, own0, own1, even0, even1, *ins = refs[:10]
        done_ref, own_part, even_part, give_ref = refs[10:]
    parts = (own_part, give_ref.at[0], even_part, give_ref.at[1])
    done_ref[...] = jnp.zeros_like(done_ref)
    for ref, value in zip(parts, ins):
        ref[...] = value[...]
    for kind in range(2):
        rights = ((own0, own1), (even0, even1))[kind]
        part_refs = (parts[:2], parts[2:])[kind]
        flag_ref, flag_at = ((flags_ref, 7), (far_ref, 0))[kind]

        @pl.loop(0, 4)
        def _(index):
            left, right = index // 2, index % 2

            @pl.when(flag_ref[flag_at + index] > 0)
            def _():
                one_pair(
                    make, tile_ref, kind * 4 + index, odd0.at[left],
                    (rights[0].at[right], rights[1].at[right]), done_ref, left, part_refs, right,
                )


def total_kernel(done, part_mine, parts_other, from_odd, from_even, sum_ref, pair_ref=None):
    for block in range(2):
        value = (
            done[block] + part_mine[block] + parts_other[0, block] + from_odd[block] + from_even[block]
        )
        sum_ref[block] = value
        if pair_ref is not None:
            high = value.astype(jnp.bfloat16)
            pair_ref[block, :64] = high
            pair_ref[block, 64:] = (value - high.astype(jnp.float32)).astype(jnp.bfloat16)


def gram_of(value_ref, scale):
    gram = dot(value_ref[0], value_ref[0], NT, HIGHEST) + dot(value_ref[1], value_ref[1], NT, HIGHEST)
    gram = gram * scale
    return jnp.concatenate([gram[:32], gram[32:]], axis=1)


def gram_kernel(scale, value_ref, gram_ref):
    gram_ref[...] = gram_of(value_ref, scale)


def second_gram_kernel(scale, core_ref, first_ref, value_ref, keep_ref, give_ref, swap_ref):
    second = gram_of(value_ref, scale)
    first = first_ref[...]
    lead = core_ref[0] == 0
    keep_ref[...] = jnp.where(lead, first, second)
    give_ref[...] = jnp.where(lead, second, first)
    swap_ref[...] = value_ref[1 - core_ref[0]]


def eliminate(packed):
    lanes = lax.broadcasted_iota(jnp.int32, (8, 64), 1)
    subs = lax.broadcasted_iota(jnp.int32, (8, 64), 0)
    deep = lax.broadcasted_iota(jnp.int32, (8, 128), 0)
    states = []
    for matrix in packed:
        whole = jnp.concatenate([matrix[:, :64], matrix[:, 64:]], axis=0)
        states.append([
            jnp.concatenate(
                [whole[8 * b : 8 * b + 8], (lanes == subs + 8 * b).astype(jnp.float32)], axis=1
            )
            for b in range(8)
        ])
    scales = [[] for _ in states]
    for at in range(8):
        spreads = [
            {
                b: [jnp.broadcast_to(state[b][:, k : k + 1], (8, 128)) for k in range(8 * at, 8 * at + 8)]
                for b in range(at, 8)
            }
            for state in states
        ]
        pivots = [jnp.zeros((8, 128), jnp.float32) for _ in states]
        for sub in range(8):
            for n, (state, spread_of) in enumerate(zip(states, spreads)):
                pivot = spread_of[at][sub][sub : sub + 1, :]
                inverse = 1.0 / pivot
                pivots[n] = jnp.where(deep == sub, pivot, pivots[n])
                row = state[at][sub : sub + 1, :] * inverse
                ahead = {j: spread_of[at][j][sub : sub + 1, :] * inverse for j in range(sub + 1, 8)}
                for b in range(at, 8):
                    column = spread_of[b][sub]
                    if b == at:
                        column = jnp.where(deep > sub, column, 0.0)
                    for j, value in ahead.items():
                        spread_of[b][j] = spread_of[b][j] - column * value
                    state[b] = state[b] - column * row
        for n, pivot in enumerate(pivots):
            scales[n].append(lax.rsqrt(pivot))
    uppers, inverses = [], []
    for state, scale in zip(states, scales):
        whole = jnp.concatenate([rows * by for rows, by in zip(state, scale)], axis=0)
        uppers.append(whole[:, :64])
        inverses.append(whole[:, 64:])
    return uppers, inverses


def copies_kernel(*refs):
    *value_refs, copies_ref = refs
    total = None
    for ref in value_refs:
        value = ref[...] if len(ref.shape) == 2 else jnp.sum(ref[...], axis=0)
        total = value if total is None else total + value
    for at in range(copies_ref.shape[0]):
        copies_ref[at] = total


def finish_kernel(core_ref, mine_ref, other_ref, value_ref, got_ref, basis_ref, factor_ref):
    core = core_ref[0]
    lead = core == 0
    mine, other = mine_ref[...], other_ref[...]
    first, second = jnp.where(lead, mine, other), jnp.where(lead, other, mine)
    uppers, inverses = eliminate([first, second])
    factor = dot(uppers[1], inverses[0], NT, HIGHEST)
    wide = lax.broadcasted_iota(jnp.int32, (64, 64), 1)
    tall = lax.broadcasted_iota(jnp.int32, (64, 64), 0)
    factor_ref[...] = jnp.where(wide >= tall, factor, 0.0)
    low = jnp.where(wide <= tall, inverses[1], 0.0)
    here = pl.multiple_of(core * HALF, HALF)
    there = pl.multiple_of((1 - core) * HALF, HALF)
    basis_ref[:, pl.ds(here, HALF)] = dot(low, value_ref[core], NN, HIGHEST)
    basis_ref[:, pl.ds(there, HALF)] = dot(low, got_ref[...], NN, HIGHEST)


def exchange(value, start):
    links = []
    for r in range(start, lax.axis_size("rows") - 1, 2):
        links += [(r, r + 1), (r + 1, r)]
    return lax.ppermute(value, "rows", links)


def to_even(value):
    return exchange(value, 0)


def to_odd(value):
    return exchange(value, 1)


def swap(value):
    return lax.ppermute(value, "cols", [(0, 1), (1, 0)])


def swap_blocks(value):
    return jnp.stack([swap(value[block]) for block in range(2)])


def live_flags(pairs, base, even_codes, odd_codes):
    none = (100, 100)

    def table(entries):
        return jnp.array([64 * i + j for i, j in (none if e is None else e for e in entries)], jnp.int32)

    even_row = lax.axis_index("rows") % 2 == 0
    wanted = jnp.where(even_row, table(even_codes), table(odd_codes))
    codes = (pairs[:, 0] - base) * 64 + (pairs[:, 1] - base)
    hit = (codes[None, :] == wanted[:, None]) & (pairs[None, :, 0] >= 0)
    return jnp.any(hit, axis=1).astype(jnp.int32)


SLOTS = [(0, 0), (0, 1), (1, 0), (1, 1)]


def own_flags_and_list(pair_list, base):
    own = jnp.concatenate([pair_list, swap(pair_list)], axis=0)
    before = lax.ppermute(own, "rows", [(r, r + 1) for r in range(lax.axis_size("rows") - 1)])
    within, idle = [(0, 0), (0, 1), (1, 1)], [None] * 4
    flags = live_flags(
        own, base,
        within + [(left, 2 + right) for left, right in SLOTS] + idle,
        within + idle + [(right, 2 + left) for left, right in SLOTS],
    )
    return flags, before


def flags_of_far(before, base):
    return live_flags(
        before, base,
        [(left - 2, 2 + right) for left, right in SLOTS],
        [(right - 2, 2 + left) for left, right in SLOTS],
    )


def spread(done, own0, out_odd, even0, give):
    from_odd = to_odd(out_odd)
    got = swap(give)
    from_even = to_even(even0 + got[1])
    return done, own0, got, from_odd, from_even


def sum_over_chips(*values):
    planes = [[(x * PLANES + z) * RING + y for x in range(ACROSS) for y in range(RING)] for z in range(PLANES)]
    lines = [[(x * PLANES + z) * RING + y for z in range(PLANES)] for x in range(ACROSS) for y in range(RING)]
    for groups in (planes, lines):
        copies = call(copies_kernel, shape((len(groups[0]), 32, 128)), 10**5, 10**5)(
            in_specs=[VMEM] * len(values)
        )(*values)
        values = [
            lax.all_to_all(copies, "rows", 0, 0, axis_index_groups=groups, tiled=True)
        ]
    return values[0].sum(0)


def local(embeddings, test_matrix, pair_list):
    rows_dev = embeddings.shape[0]
    columns = test_matrix.shape[1]
    bf16, f32 = jnp.bfloat16, jnp.float32
    core = lax.axis_index("cols").astype(jnp.int32)
    core_ref = core.reshape(1)
    base = (lax.axis_index("rows") * 2).astype(jnp.int32)
    scale = 1.0 / (rows_dev * lax.axis_size("rows"))

    test_columns = pltpu.with_memory_space_constraint(test_matrix.T, pltpu.HBM)
    embeddings = pltpu.with_memory_space_constraint(embeddings, pltpu.HBM)

    def packet(relative):
        return call(
            functools.partial(packet_kernel, relative), shape((2, 1792, 128), bf16), 10**4, 10**4,
        )(
            in_specs=[SMEM, HBM, HBM],
            scratch_shapes=[
                pltpu.VMEM((2, HALF, 384), bf16),
                pltpu.VMEM((2, columns, HALF), bf16),
                pltpu.SemaphoreType.DMA((6,)),
            ],
        )(core_ref, embeddings, test_columns)

    own0 = packet(0)
    even0 = to_even(own0)
    odd0 = to_odd(own0)
    own1, pair_list = lax.optimization_barrier((packet(1), pair_list))
    flags, before = own_flags_and_list(pair_list, base)

    sum_shape = shape((2, 64, HALF))

    def tiles(count):
        return shape((count, 2, HALF, HALF), bf16)

    tiles_own, done, own_part0, own_part1 = call(
        functools.partial(local_kernel, True), (tiles(3),) + 3 * (sum_shape,), 10**4, 10**4
    )(in_specs=[SMEM] + [VMEM] * 2)(flags, own0, own1)
    done, even0 = lax.optimization_barrier((done, even0))
    even1 = swap_blocks(even0)
    tiles_early, done, even_part0, even_part1 = call(
        functools.partial(early_kernel, True), (tiles(4),) + 3 * (sum_shape,), 10**4, 10**4
    )(in_specs=[SMEM] + [VMEM] * 4)(flags, own0, even0, even1, done)
    done, odd0, before = lax.optimization_barrier((done, odd0, before))
    far_flags = flags_of_far(before, base)
    give_shape = shape((2, 2, 64, HALF))
    tiles_late, out_odd, own_part0, even_part0, give = call(
        functools.partial(late_kernel, True), (tiles(8),) + 3 * (sum_shape,) + (give_shape,), 10**9, 10**6
    )(in_specs=[SMEM] * 2 + [VMEM] * 9)(
        flags, far_flags, odd0, own0, own1, even0, even1, own_part0, own_part1, even_part0, even_part1
    )
    sketch, pair0 = call(total_kernel, (sum_shape, shape((2, 128, HALF), bf16)), 10**6, 2 * 10**6)(
        in_specs=[VMEM] * 5
    )(*spread(done, own_part0, out_odd, even_part0, give))

    even0 = to_even(pair0)
    odd0 = to_odd(pair0)
    gram_shape = shape((32, 128))
    first_gram = call(functools.partial(gram_kernel, scale), gram_shape, 10**4, 10**4)(
        in_specs=[VMEM]
    )(sketch)
    pair1 = swap(pair0)
    done, own_part0, own_part1 = call(
        functools.partial(local_kernel, False), 3 * (sum_shape,), 10**4, 10**4
    )(in_specs=[SMEM] + [VMEM] * 3)(flags, tiles_own, pair0, pair1)
    even1 = swap_blocks(even0)
    done, even_part0, even_part1 = call(
        functools.partial(early_kernel, False), 3 * (sum_shape,), 10**4, 10**4
    )(in_specs=[SMEM] + [VMEM] * 5)(flags, tiles_early, pair0, even0, even1, done)
    done, odd0 = lax.optimization_barrier((done, odd0))
    out_odd, own_part0, even_part0, give = call(
        functools.partial(late_kernel, False), 3 * (sum_shape,) + (give_shape,), 10**9, 10**6
    )(in_specs=[SMEM] * 2 + [VMEM] * 10)(
        flags, far_flags, tiles_late, odd0, pair0, pair1, even0, even1,
        own_part0, own_part1, even_part0, even_part1,
    )
    image = call(total_kernel, sum_shape, 10**6, 2 * 10**6)(in_specs=[VMEM] * 5)(
        *spread(done, own_part0, out_odd, even_part0, give)
    )
    keep, gram_give, half = call(
        functools.partial(second_gram_kernel, scale),
        (gram_shape, gram_shape, shape((64, HALF))),
        10**8, 10**6,
    )(in_specs=[SMEM, VMEM, VMEM])(core_ref, first_gram, image)
    got = swap(half)
    mine = sum_over_chips(keep, swap(gram_give))
    other = swap(mine)
    basis, factor = call(finish_kernel, (shape((64, BLK)), shape((64, 64))), 10**8, 10**6)(
        in_specs=[SMEM] + [VMEM] * 4
    )(core_ref, mine, other, image, got)
    return basis.T, factor


def solution(mesh):
    in_specs = (P("rows", None), P("rows", None), P(("rows", "cols"), None))
    out_specs = (P(("rows", "cols"), None), P())
    return jax.shard_map(local, mesh=mesh, in_specs=in_specs, out_specs=out_specs, check_vma=False)
```

```python
import functools

import jax
import jax.numpy as jnp
from jax import lax
from jax.experimental import pallas as pl
from jax.experimental.pallas import tpu as pltpu
from jax.sharding import PartitionSpec as P

BLK = 1024
HALF = 512
QUARTER = 256
SHARPNESS = 6.0
EPSILON = 1e-06
LOG2E = 1.4426950408889634
HIGHEST = lax.Precision.HIGHEST
VMEM = pl.BlockSpec(memory_space=pltpu.VMEM)
HBM = pl.BlockSpec(memory_space=pltpu.HBM)
SMEM = pl.BlockSpec(memory_space=pltpu.SMEM)
NT = (((1,), (1,)), ((), ()))
NN = (((1,), (0,)), ((), ()))
ACROSS, PLANES, RING = 4, 8, 4


def call(kernel, outs, flops, moved, exps=0, room=16):
    return functools.partial(
        pl.pallas_call,
        kernel,
        out_shape=outs,
        out_specs=jax.tree.map(lambda _: VMEM, outs),
        compiler_params=pltpu.CompilerParams(vmem_limit_bytes=room * 1024 * 1024),
        cost_estimate=pl.CostEstimate(flops=flops, bytes_accessed=moved, transcendentals=exps),
    )


def shape(dims, dtype=jnp.float32):
    return jax.ShapeDtypeStruct(dims, dtype)


def dot(left, right, dims, precision=None):
    return lax.dot_general(
        left, right, dims, precision=precision, preferred_element_type=jnp.float32
    )


def packet_kernel(relative, core_ref, rows_ref, columns_ref, packet_ref, raw_ref, vec_ref, sems):
    side = core_ref[0] if relative == 0 else 1 - core_ref[0]
    copies = []
    for block in range(2):
        start = pl.multiple_of(block * BLK + side * HALF, HALF)
        for part in range(2):
            rows = pl.ds(pl.multiple_of(start + part * QUARTER, QUARTER), QUARTER)
            copies.append(
                pltpu.make_async_copy(
                    rows_ref.at[rows, :],
                    raw_ref.at[block, pl.ds(part * QUARTER, QUARTER)],
                    sems.at[2 * block + part],
                )
            )
        copies.append(
            pltpu.make_async_copy(
                columns_ref.at[:, pl.ds(start, HALF)], vec_ref.at[block], sems.at[4 + block]
            )
        )
    for copy in copies:
        copy.start()
    for block in range(2):
        for part in range(2):
            copies[3 * block + part].wait()
            here = slice(part * QUARTER, (part + 1) * QUARTER)
            widened = raw_ref[block, here].astype(jnp.float32)
            inverse = lax.rsqrt(jnp.sum(widened * widened, axis=1, keepdims=True) + EPSILON)
            unit = (widened * inverse).astype(jnp.bfloat16)
            for tile in range(3):
                first = HALF * tile + part * QUARTER
                packet_ref[block, first : first + QUARTER] = unit[:, 128 * tile : 128 * (tile + 1)]
        copies[3 * block + 2].wait()
        for tile in range(4):
            packet_ref[block, 1536 + 64 * tile : 1600 + 64 * tile] = vec_ref[
                block, :, 128 * tile : 128 * (tile + 1)
            ]


def unit_rows(packet, start, count):
    return jnp.concatenate(
        [packet[HALF * tile + start : HALF * tile + start + count] for tile in range(3)], axis=1
    )


def vectors(packet):
    return jnp.concatenate([packet[1536 + 64 * tile : 1600 + 64 * tile] for tile in range(4)], axis=1)


def affinity_tile(left, right):
    scores = dot(left, right, NT)
    return jnp.exp2((SHARPNESS * LOG2E) * scores - (SHARPNESS * LOG2E)).astype(jnp.bfloat16)


def fold(product):
    if product.shape[0] == 128:
        return product[:64] + product[64:]
    return product


def make_tiles(left, rights, tile_ref, slot):
    for side in range(2):
        for at in range(0, HALF, 256):
            right = unit_rows(rights[side], at, 256)
            for row in range(0, HALF, 256):
                tile_ref[slot, side, row : row + 256, at : at + 256] = affinity_tile(
                    unit_rows(left, row, 256), right
                )


def use_tiles(tile_ref, slot, rights, left, done_ref, done_at, part_refs, part_at, partial):
    total = fold(dot(rights[0], tile_ref[slot, 0], NT)) + fold(dot(rights[1], tile_ref[slot, 1], NT))
    done_ref[done_at] += total

    def put_part():
        for side in range(2):
            part_refs[side][part_at] += fold(dot(left, tile_ref[slot, side], NN))

    if partial is None:
        put_part()
    else:
        pl.when(partial)(put_part)


def one_pair(make, tile_ref, slot, left, rights, done_ref, done_at, part_refs, part_at, partial=None):
    take = vectors if make else (lambda ref: ref[...])
    if make:
        make_tiles(left, rights, tile_ref, slot)
    use_tiles(
        tile_ref, slot, (take(rights[0]), take(rights[1])), take(left),
        done_ref, done_at, part_refs, part_at, partial,
    )


def local_kernel(make, flags_ref, *refs):
    if make:
        own0, own1, tile_ref, done_ref, part0, part1 = refs
    else:
        tile_ref, own0, own1, done_ref, part0, part1 = refs
    for ref in (done_ref, part0, part1):
        ref[...] = jnp.zeros_like(ref)

    @pl.loop(0, 3)
    def _(slot):
        first, second = slot // 2, (slot + 1) // 2

        @pl.when(flags_ref[slot] > 0)
        def _():
            one_pair(
                make, tile_ref, slot, own0.at[first], (own0.at[second], own1.at[second]),
                done_ref, first, (part0, part1), second, slot == 1,
            )


def early_kernel(make, flags_ref, *refs):
    if make:
        own0, even0, even1, started, tile_ref, done_ref, part0, part1 = refs
    else:
        tile_ref, own0, even0, even1, started, done_ref, part0, part1 = refs
    done_ref[...] = started[...]
    for ref in (part0, part1):
        ref[...] = jnp.zeros_like(ref)

    @pl.loop(0, 4)
    def _(slot):
        left, right = slot // 2, slot % 2

        @pl.when(flags_ref[3 + slot] > 0)
        def _():
            one_pair(
                make, tile_ref, slot, own0.at[left], (even0.at[right], even1.at[right]),
                done_ref, left, (part0, part1), right,
            )


def late_kernel(make, flags_ref, far_ref, *refs):
    if make:
        odd0, own0, own1, even0, even1, *ins = refs[:9]
        tile_ref, done_ref, own_part, even_part, give_ref = refs[9:]
    else:
        tile_ref, odd0, own0, own1, even0, even1, *ins = refs[:10]
        done_ref, own_part, even_part, give_ref = refs[10:]
    parts = (own_part, give_ref.at[0], even_part, give_ref.at[1])
    done_ref[...] = jnp.zeros_like(done_ref)
    for ref, value in zip(parts, ins):
        ref[...] = value[...]
    for kind in range(2):
        rights = ((own0, own1), (even0, even1))[kind]
        part_refs = (parts[:2], parts[2:])[kind]
        flag_ref, flag_at = ((flags_ref, 7), (far_ref, 0))[kind]

        @pl.loop(0, 4)
        def _(index):
            left, right = index // 2, index % 2

            @pl.when(flag_ref[flag_at + index] > 0)
            def _():
                one_pair(
                    make, tile_ref, kind * 4 + index, odd0.at[left],
                    (rights[0].at[right], rights[1].at[right]), done_ref, left, part_refs, right,
                )


def put_pair(pair_ref, block, value):
    high = value.astype(jnp.bfloat16)
    pair_ref[block, :64] = high
    pair_ref[block, 64:] = (value - high.astype(jnp.float32)).astype(jnp.bfloat16)


def partial_kernel(done, part_mine, parts_other, from_even, sum_ref):
    for block in range(2):
        sum_ref[block] = done[block] + part_mine[block] + parts_other[0, block] + from_even[block]


def pair_kernel(partial, ours, pair_ref):
    for block in range(2):
        put_pair(pair_ref, block, partial[block] + ours[block])


def total_kernel(partial, from_odd, sum_ref, pair_ref=None):
    for block in range(2):
        value = partial[block] + from_odd[block]
        sum_ref[block] = value
        if pair_ref is not None:
            put_pair(pair_ref, block, value)


def gram_of(value_ref, scale):
    gram = dot(value_ref[0], value_ref[0], NT, HIGHEST) + dot(value_ref[1], value_ref[1], NT, HIGHEST)
    gram = gram * scale
    return jnp.concatenate([gram[:32], gram[32:]], axis=1)


def gram_kernel(scale, value_ref, gram_ref):
    gram_ref[...] = gram_of(value_ref, scale)


def second_gram_kernel(scale, core_ref, first_ref, value_ref, keep_ref, give_ref, swap_ref):
    second = gram_of(value_ref, scale)
    first = first_ref[...]
    lead = core_ref[0] == 0
    keep_ref[...] = jnp.where(lead, first, second)
    give_ref[...] = jnp.where(lead, second, first)
    swap_ref[...] = value_ref[1 - core_ref[0]]


def eliminate(packed):
    lanes = lax.broadcasted_iota(jnp.int32, (8, 64), 1)
    subs = lax.broadcasted_iota(jnp.int32, (8, 64), 0)
    deep = lax.broadcasted_iota(jnp.int32, (8, 128), 0)
    states = []
    for matrix in packed:
        whole = jnp.concatenate([matrix[:, :64], matrix[:, 64:]], axis=0)
        states.append([
            jnp.concatenate(
                [whole[8 * b : 8 * b + 8], (lanes == subs + 8 * b).astype(jnp.float32)], axis=1
            )
            for b in range(8)
        ])
    scales = [[] for _ in states]
    for at in range(8):
        spreads = [
            {
                b: [jnp.broadcast_to(state[b][:, k : k + 1], (8, 128)) for k in range(8 * at, 8 * at + 8)]
                for b in range(at, 8)
            }
            for state in states
        ]
        pivots = [jnp.zeros((8, 128), jnp.float32) for _ in states]
        for sub in range(8):
            for n, (state, spread_of) in enumerate(zip(states, spreads)):
                pivot = spread_of[at][sub][sub : sub + 1, :]
                inverse = 1.0 / pivot
                pivots[n] = jnp.where(deep == sub, pivot, pivots[n])
                row = state[at][sub : sub + 1, :] * inverse
                ahead = {j: spread_of[at][j][sub : sub + 1, :] * inverse for j in range(sub + 1, 8)}
                for b in range(at, 8):
                    column = spread_of[b][sub]
                    if b == at:
                        column = jnp.where(deep > sub, column, 0.0)
                    for j, value in ahead.items():
                        spread_of[b][j] = spread_of[b][j] - column * value
                    state[b] = state[b] - column * row
        for n, pivot in enumerate(pivots):
            scales[n].append(lax.rsqrt(pivot))
    uppers, inverses = [], []
    for state, scale in zip(states, scales):
        whole = jnp.concatenate([rows * by for rows, by in zip(state, scale)], axis=0)
        uppers.append(whole[:, :64])
        inverses.append(whole[:, 64:])
    return uppers, inverses


def copies_kernel(*refs):
    *value_refs, copies_ref = refs
    total = None
    for ref in value_refs:
        value = ref[...] if len(ref.shape) == 2 else jnp.sum(ref[...], axis=0)
        total = value if total is None else total + value
    for at in range(copies_ref.shape[0]):
        copies_ref[at] = total


def finish_kernel(core_ref, mine_ref, other_ref, value_ref, got_ref, basis_ref, factor_ref):
    core = core_ref[0]
    lead = core == 0
    mine, other = mine_ref[...], other_ref[...]
    first, second = jnp.where(lead, mine, other), jnp.where(lead, other, mine)
    uppers, inverses = eliminate([first, second])
    factor = dot(uppers[1], inverses[0], NT, HIGHEST)
    wide = lax.broadcasted_iota(jnp.int32, (64, 64), 1)
    tall = lax.broadcasted_iota(jnp.int32, (64, 64), 0)
    factor_ref[...] = jnp.where(wide >= tall, factor, 0.0)
    low = jnp.where(wide <= tall, inverses[1], 0.0)
    here = pl.multiple_of(core * HALF, HALF)
    there = pl.multiple_of((1 - core) * HALF, HALF)
    basis_ref[:, pl.ds(here, HALF)] = dot(low, value_ref[core], NN, HIGHEST)
    basis_ref[:, pl.ds(there, HALF)] = dot(low, got_ref[...], NN, HIGHEST)


def exchange(value, start):
    links = []
    for r in range(start, lax.axis_size("rows") - 1, 2):
        links += [(r, r + 1), (r + 1, r)]
    return lax.ppermute(value, "rows", links)


def to_even(value):
    return exchange(value, 0)


def to_odd(value):
    return exchange(value, 1)


def swap(value):
    return lax.ppermute(value, "cols", [(0, 1), (1, 0)])


def swap_blocks(value):
    return jnp.stack([swap(value[block]) for block in range(2)])


def live_flags(pairs, base, even_codes, odd_codes):
    none = (100, 100)

    def table(entries):
        return jnp.array([64 * i + j for i, j in (none if e is None else e for e in entries)], jnp.int32)

    even_row = lax.axis_index("rows") % 2 == 0
    wanted = jnp.where(even_row, table(even_codes), table(odd_codes))
    codes = (pairs[:, 0] - base) * 64 + (pairs[:, 1] - base)
    hit = (codes[None, :] == wanted[:, None]) & (pairs[None, :, 0] >= 0)
    return jnp.any(hit, axis=1).astype(jnp.int32)


SLOTS = [(0, 0), (0, 1), (1, 0), (1, 1)]


def own_flags_and_list(pair_list, base):
    own = jnp.concatenate([pair_list, swap(pair_list)], axis=0)
    before = lax.ppermute(own, "rows", [(r, r + 1) for r in range(lax.axis_size("rows") - 1)])
    within, idle = [(0, 0), (0, 1), (1, 1)], [None] * 4
    flags = live_flags(
        own, base,
        within + [(left, 2 + right) for left, right in SLOTS] + idle,
        within + idle + [(right, 2 + left) for left, right in SLOTS],
    )
    return flags, before


def flags_of_far(before, base):
    return live_flags(
        before, base,
        [(left - 2, 2 + right) for left, right in SLOTS],
        [(right - 2, 2 + left) for left, right in SLOTS],
    )


def spread(done, own0, out_odd, even0, give):
    from_odd = to_odd(out_odd)
    got = swap(give)
    from_even = to_even(even0 + got[1])
    partial = call(partial_kernel, shape((2, 64, HALF)), 10**4, 10**4)(in_specs=[VMEM] * 4)(
        done, own0, got, from_even
    )
    return partial, from_odd


def sum_over_chips(*values):
    planes = [[(x * PLANES + z) * RING + y for x in range(ACROSS) for y in range(RING)] for z in range(PLANES)]
    lines = [[(x * PLANES + z) * RING + y for z in range(PLANES)] for x in range(ACROSS) for y in range(RING)]
    for groups in (planes, lines):
        copies = call(copies_kernel, shape((len(groups[0]), 32, 128)), 10**5, 10**5)(
            in_specs=[VMEM] * len(values)
        )(*values)
        values = [
            lax.all_to_all(copies, "rows", 0, 0, axis_index_groups=groups, tiled=True)
        ]
    return values[0].sum(0)


def local(embeddings, test_matrix, pair_list):
    rows_dev = embeddings.shape[0]
    columns = test_matrix.shape[1]
    bf16, f32 = jnp.bfloat16, jnp.float32
    core = lax.axis_index("cols").astype(jnp.int32)
    core_ref = core.reshape(1)
    base = (lax.axis_index("rows") * 2).astype(jnp.int32)
    scale = 1.0 / (rows_dev * lax.axis_size("rows"))

    test_columns = pltpu.with_memory_space_constraint(test_matrix.T, pltpu.HBM)
    embeddings = pltpu.with_memory_space_constraint(embeddings, pltpu.HBM)

    def packet(relative):
        return call(
            functools.partial(packet_kernel, relative), shape((2, 1792, 128), bf16), 10**4, 10**4,
        )(
            in_specs=[SMEM, HBM, HBM],
            scratch_shapes=[
                pltpu.VMEM((2, HALF, 384), bf16),
                pltpu.VMEM((2, columns, HALF), bf16),
                pltpu.SemaphoreType.DMA((6,)),
            ],
        )(core_ref, embeddings, test_columns)

    own0 = packet(0)
    even0 = to_even(own0)
    odd0 = to_odd(own0)
    own1, pair_list = lax.optimization_barrier((packet(1), pair_list))
    flags, before = own_flags_and_list(pair_list, base)

    sum_shape = shape((2, 64, HALF))

    def tiles(count):
        return shape((count, 2, HALF, HALF), bf16)

    tiles_own, done, own_part0, own_part1 = call(
        functools.partial(local_kernel, True), (tiles(3),) + 3 * (sum_shape,), 10**4, 10**4
    )(in_specs=[SMEM] + [VMEM] * 2)(flags, own0, own1)
    done, even0 = lax.optimization_barrier((done, even0))
    even1 = swap_blocks(even0)
    tiles_early, done, even_part0, even_part1 = call(
        functools.partial(early_kernel, True), (tiles(4),) + 3 * (sum_shape,), 10**4, 10**4
    )(in_specs=[SMEM] + [VMEM] * 4)(flags, own0, even0, even1, done)
    done, odd0, before = lax.optimization_barrier((done, odd0, before))
    far_flags = flags_of_far(before, base)
    give_shape = shape((2, 2, 64, HALF))
    tiles_late, out_odd, own_part0, even_part0, give = call(
        functools.partial(late_kernel, True), (tiles(8),) + 3 * (sum_shape,) + (give_shape,), 10**9, 10**6
    )(in_specs=[SMEM] * 2 + [VMEM] * 9)(
        flags, far_flags, odd0, own0, own1, even0, even1, own_part0, own_part1, even_part0, even_part1
    )
    partial, from_odd = spread(done, own_part0, out_odd, even_part0, give)
    odd_partial, odd_ours = to_odd(partial), out_odd
    sketch, pair0 = call(total_kernel, (sum_shape, shape((2, 128, HALF), bf16)), 10**4, 10**4)(
        in_specs=[VMEM] * 2
    )(partial, from_odd)
    even0 = to_even(pair0)
    gram_shape = shape((32, 128))
    first_gram = call(functools.partial(gram_kernel, scale), gram_shape, 10**4, 10**4)(
        in_specs=[VMEM]
    )(sketch)
    odd0 = call(pair_kernel, shape((2, 128, HALF), bf16), 10**4, 10**4)(in_specs=[VMEM] * 2)(
        odd_partial, odd_ours
    )
    pair1, odd0 = lax.optimization_barrier((swap(pair0), odd0))
    done, own_part0, own_part1 = call(
        functools.partial(local_kernel, False), 3 * (sum_shape,), 10**11, 10**4
    )(in_specs=[SMEM] + [VMEM] * 3)(flags, tiles_own, pair0, pair1)
    done, even0 = lax.optimization_barrier((done, even0))
    even1 = swap_blocks(even0)
    done, even_part0, even_part1 = call(
        functools.partial(early_kernel, False), 3 * (sum_shape,), 10**4, 10**4
    )(in_specs=[SMEM] + [VMEM] * 5)(flags, tiles_early, pair0, even0, even1, done)
    out_odd, own_part0, even_part0, give = call(
        functools.partial(late_kernel, False), 3 * (sum_shape,) + (give_shape,), 10**9, 10**6
    )(in_specs=[SMEM] * 2 + [VMEM] * 10)(
        flags, far_flags, tiles_late, odd0, pair0, pair1, even0, even1,
        own_part0, own_part1, even_part0, even_part1,
    )
    image = call(total_kernel, sum_shape, 10**4, 10**4)(in_specs=[VMEM] * 2)(
        *spread(done, own_part0, out_odd, even_part0, give)
    )
    keep, gram_give, half = call(
        functools.partial(second_gram_kernel, scale),
        (gram_shape, gram_shape, shape((64, HALF))),
        10**8, 10**6,
    )(in_specs=[SMEM, VMEM, VMEM])(core_ref, first_gram, image)
    got = swap(half)
    mine = sum_over_chips(keep, swap(gram_give))
    other = swap(mine)
    basis, factor = call(finish_kernel, (shape((64, BLK)), shape((64, 64))), 10**8, 10**6)(
        in_specs=[SMEM] + [VMEM] * 4
    )(core_ref, mine, other, image, got)
    return basis.T, factor


def solution(mesh):
    in_specs = (P("rows", None), P("rows", None), P(("rows", "cols"), None))
    out_specs = (P(("rows", "cols"), None), P())
    return jax.shard_map(local, mesh=mesh, in_specs=in_specs, out_specs=out_specs, check_vma=False)
```

```python
import functools

import jax
import jax.numpy as jnp
from jax import lax
from jax.experimental import pallas as pl
from jax.experimental.pallas import tpu as pltpu
from jax.sharding import PartitionSpec as P

BLK = 1024
HALF = 512
QUARTER = 256
SHARPNESS = 6.0
EPSILON = 1e-06
LOG2E = 1.4426950408889634
HIGHEST = lax.Precision.HIGHEST
VMEM = pl.BlockSpec(memory_space=pltpu.VMEM)
HBM = pl.BlockSpec(memory_space=pltpu.HBM)
SMEM = pl.BlockSpec(memory_space=pltpu.SMEM)
NT = (((1,), (1,)), ((), ()))
NN = (((1,), (0,)), ((), ()))
ACROSS, PLANES, RING = 4, 8, 4


def call(kernel, outs, flops, moved, exps=0, room=16):
    return functools.partial(
        pl.pallas_call,
        kernel,
        out_shape=outs,
        out_specs=jax.tree.map(lambda _: VMEM, outs),
        compiler_params=pltpu.CompilerParams(vmem_limit_bytes=room * 1024 * 1024),
        cost_estimate=pl.CostEstimate(flops=flops, bytes_accessed=moved, transcendentals=exps),
    )


def shape(dims, dtype=jnp.float32):
    return jax.ShapeDtypeStruct(dims, dtype)


def dot(left, right, dims, precision=None):
    return lax.dot_general(
        left, right, dims, precision=precision, preferred_element_type=jnp.float32
    )


def packet_kernel(relative, core_ref, rows_ref, columns_ref, packet_ref, raw_ref, vec_ref, sems):
    side = core_ref[0] if relative == 0 else 1 - core_ref[0]
    copies = []
    for block in range(2):
        start = pl.multiple_of(block * BLK + side * HALF, HALF)
        for part in range(2):
            rows = pl.ds(pl.multiple_of(start + part * QUARTER, QUARTER), QUARTER)
            copies.append(
                pltpu.make_async_copy(
                    rows_ref.at[rows, :],
                    raw_ref.at[block, pl.ds(part * QUARTER, QUARTER)],
                    sems.at[2 * block + part],
                )
            )
        copies.append(
            pltpu.make_async_copy(
                columns_ref.at[:, pl.ds(start, HALF)], vec_ref.at[block], sems.at[4 + block]
            )
        )
    for copy in copies:
        copy.start()
    for block in range(2):
        for part in range(2):
            copies[3 * block + part].wait()
            here = slice(part * QUARTER, (part + 1) * QUARTER)
            widened = raw_ref[block, here].astype(jnp.float32)
            inverse = lax.rsqrt(jnp.sum(widened * widened, axis=1, keepdims=True) + EPSILON)
            unit = (widened * inverse).astype(jnp.bfloat16)
            for tile in range(3):
                first = HALF * tile + part * QUARTER
                packet_ref[block, first : first + QUARTER] = unit[:, 128 * tile : 128 * (tile + 1)]
        copies[3 * block + 2].wait()
        for tile in range(4):
            packet_ref[block, 1536 + 64 * tile : 1600 + 64 * tile] = vec_ref[
                block, :, 128 * tile : 128 * (tile + 1)
            ]


def unit_rows(packet, start, count):
    return jnp.concatenate(
        [packet[HALF * tile + start : HALF * tile + start + count] for tile in range(3)], axis=1
    )


def vectors(packet):
    return jnp.concatenate([packet[1536 + 64 * tile : 1600 + 64 * tile] for tile in range(4)], axis=1)


def affinity_tile(left, right):
    scores = dot(left, right, NT)
    return jnp.exp2((SHARPNESS * LOG2E) * scores - (SHARPNESS * LOG2E)).astype(jnp.bfloat16)


def fold(product):
    if product.shape[0] == 128:
        return product[:64] + product[64:]
    return product


def make_tiles(left, rights, tile_ref, slot):
    for side in range(2):
        for at in range(0, HALF, 256):
            right = unit_rows(rights[side], at, 256)
            for row in range(0, HALF, 256):
                tile_ref[slot, side, row : row + 256, at : at + 256] = affinity_tile(
                    unit_rows(left, row, 256), right
                )


def use_tiles(tile_ref, slot, rights, left, done_ref, done_at, part_refs, part_at, partial):
    total = fold(dot(rights[0], tile_ref[slot, 0], NT)) + fold(dot(rights[1], tile_ref[slot, 1], NT))
    done_ref[done_at] += total

    def put_part():
        for side in range(2):
            part_refs[side][part_at] += fold(dot(left, tile_ref[slot, side], NN))

    if partial is None:
        put_part()
    else:
        pl.when(partial)(put_part)


def one_pair(make, tile_ref, slot, left, rights, done_ref, done_at, part_refs, part_at, partial=None):
    take = vectors if make else (lambda ref: ref[...])
    if make:
        make_tiles(left, rights, tile_ref, slot)
    use_tiles(
        tile_ref, slot, (take(rights[0]), take(rights[1])), take(left),
        done_ref, done_at, part_refs, part_at, partial,
    )


def local_kernel(make, flags_ref, *refs):
    if make:
        own0, own1, tile_ref, done_ref, part0, part1 = refs
    else:
        tile_ref, own0, own1, done_ref, part0, part1 = refs
    for ref in (done_ref, part0, part1):
        ref[...] = jnp.zeros_like(ref)

    @pl.loop(0, 3)
    def _(slot):
        first, second = slot // 2, (slot + 1) // 2

        @pl.when(flags_ref[slot] > 0)
        def _():
            one_pair(
                make, tile_ref, slot, own0.at[first], (own0.at[second], own1.at[second]),
                done_ref, first, (part0, part1), second, slot == 1,
            )


def early_kernel(make, flags_ref, *refs):
    if make:
        own0, even0, even1, started, tile_ref, done_ref, part0, part1 = refs
    else:
        tile_ref, own0, even0, even1, started, done_ref, part0, part1 = refs
    done_ref[...] = started[...]
    for ref in (part0, part1):
        ref[...] = jnp.zeros_like(ref)

    @pl.loop(0, 4)
    def _(slot):
        left, right = slot // 2, slot % 2

        @pl.when(flags_ref[3 + slot] > 0)
        def _():
            one_pair(
                make, tile_ref, slot, own0.at[left], (even0.at[right], even1.at[right]),
                done_ref, left, (part0, part1), right,
            )


def late_kernel(make, flags_ref, far_ref, *refs):
    if make:
        odd0, own0, own1, even0, even1, *ins = refs[:9]
        tile_ref, done_ref, *parts = refs[9:]
    else:
        tile_ref, odd0, own0, own1, even0, even1, *ins = refs[:10]
        done_ref, *parts = refs[10:]
    done_ref[...] = jnp.zeros_like(done_ref)
    for ref, value in zip(parts, ins):
        ref[...] = value[...]
    for kind in range(2):
        rights = ((own0, own1), (even0, even1))[kind]
        part_refs = (parts[:2], parts[2:])[kind]
        flag_ref, flag_at = ((flags_ref, 7), (far_ref, 0))[kind]

        @pl.loop(0, 4)
        def _(index):
            left, right = index // 2, index % 2

            @pl.when(flag_ref[flag_at + index] > 0)
            def _():
                one_pair(
                    make, tile_ref, kind * 4 + index, odd0.at[left],
                    (rights[0].at[right], rights[1].at[right]), done_ref, left, part_refs, right,
                )


def put_pair(pair_ref, block, value):
    high = value.astype(jnp.bfloat16)
    pair_ref[block, :64] = high
    pair_ref[block, 64:] = (value - high.astype(jnp.float32)).astype(jnp.bfloat16)


def sum_kernel(*refs):
    *value_refs, sum_ref = refs
    for block in range(2):
        total = value_refs[0][block]
        for ref in value_refs[1:]:
            total = total + ref[block]
        sum_ref[block] = total


def pair_kernel(partial, ours, pair_ref):
    for block in range(2):
        put_pair(pair_ref, block, partial[block] + ours[block])


def total_kernel(partial, from_odd, sum_ref, pair_ref):
    for block in range(2):
        value = partial[block] + from_odd[block]
        sum_ref[block] = value
        put_pair(pair_ref, block, value)


def gram_of(value_ref, scale):
    gram = dot(value_ref[0], value_ref[0], NT, HIGHEST) + dot(value_ref[1], value_ref[1], NT, HIGHEST)
    gram = gram * scale
    return jnp.concatenate([gram[:32], gram[32:]], axis=1)


def gram_kernel(scale, value_ref, gram_ref):
    gram_ref[...] = gram_of(value_ref, scale)


def second_gram_kernel(scale, core_ref, first_ref, value_ref, keep_ref, give_ref, swap_ref):
    second = gram_of(value_ref, scale)
    first = first_ref[...]
    lead = core_ref[0] == 0
    keep_ref[...] = jnp.where(lead, first, second)
    give_ref[...] = jnp.where(lead, second, first)
    swap_ref[...] = value_ref[1 - core_ref[0]]


def eliminate(packed):
    lanes = lax.broadcasted_iota(jnp.int32, (8, 64), 1)
    subs = lax.broadcasted_iota(jnp.int32, (8, 64), 0)
    deep = lax.broadcasted_iota(jnp.int32, (8, 128), 0)
    states = []
    for matrix in packed:
        whole = jnp.concatenate([matrix[:, :64], matrix[:, 64:]], axis=0)
        states.append([
            jnp.concatenate(
                [whole[8 * b : 8 * b + 8], (lanes == subs + 8 * b).astype(jnp.float32)], axis=1
            )
            for b in range(8)
        ])
    scales = [[] for _ in states]
    for at in range(8):
        spreads = [
            {
                b: [jnp.broadcast_to(state[b][:, k : k + 1], (8, 128)) for k in range(8 * at, 8 * at + 8)]
                for b in range(at, 8)
            }
            for state in states
        ]
        pivots = [jnp.zeros((8, 128), jnp.float32) for _ in states]
        for sub in range(8):
            for n, (state, spread_of) in enumerate(zip(states, spreads)):
                pivot = spread_of[at][sub][sub : sub + 1, :]
                inverse = 1.0 / pivot
                pivots[n] = jnp.where(deep == sub, pivot, pivots[n])
                row = state[at][sub : sub + 1, :] * inverse
                ahead = {j: spread_of[at][j][sub : sub + 1, :] * inverse for j in range(sub + 1, 8)}
                for b in range(at, 8):
                    column = spread_of[b][sub]
                    if b == at:
                        column = jnp.where(deep > sub, column, 0.0)
                    for j, value in ahead.items():
                        spread_of[b][j] = spread_of[b][j] - column * value
                    state[b] = state[b] - column * row
        for n, pivot in enumerate(pivots):
            scales[n].append(lax.rsqrt(pivot))
    uppers, inverses = [], []
    for state, scale in zip(states, scales):
        whole = jnp.concatenate([rows * by for rows, by in zip(state, scale)], axis=0)
        uppers.append(whole[:, :64])
        inverses.append(whole[:, 64:])
    return uppers, inverses


def copies_kernel(*refs):
    *value_refs, copies_ref = refs
    total = None
    for ref in value_refs:
        value = ref[...] if len(ref.shape) == 2 else jnp.sum(ref[...], axis=0)
        total = value if total is None else total + value
    for at in range(copies_ref.shape[0]):
        copies_ref[at] = total


def finish_kernel(core_ref, mine_ref, other_ref, value_ref, got_ref, basis_ref, factor_ref):
    core = core_ref[0]
    lead = core == 0
    mine, other = mine_ref[...], other_ref[...]
    first, second = jnp.where(lead, mine, other), jnp.where(lead, other, mine)
    uppers, inverses = eliminate([first, second])
    factor = dot(uppers[1], inverses[0], NT, HIGHEST)
    wide = lax.broadcasted_iota(jnp.int32, (64, 64), 1)
    tall = lax.broadcasted_iota(jnp.int32, (64, 64), 0)
    factor_ref[...] = jnp.where(wide >= tall, factor, 0.0)
    low = jnp.where(wide <= tall, inverses[1], 0.0)
    here = pl.multiple_of(core * HALF, HALF)
    there = pl.multiple_of((1 - core) * HALF, HALF)
    basis_ref[:, pl.ds(here, HALF)] = dot(low, value_ref[core], NN, HIGHEST)
    basis_ref[:, pl.ds(there, HALF)] = dot(low, got_ref[...], NN, HIGHEST)


def exchange(value, start):
    links = []
    for r in range(start, lax.axis_size("rows") - 1, 2):
        links += [(r, r + 1), (r + 1, r)]
    return lax.ppermute(value, "rows", links)


def to_even(value):
    return exchange(value, 0)


def to_odd(value):
    return exchange(value, 1)


def swap(value):
    return lax.ppermute(value, "cols", [(0, 1), (1, 0)])


def swap_blocks(value):
    return jnp.stack([swap(value[block]) for block in range(2)])


def live_flags(pairs, base, even_codes, odd_codes):
    none = (100, 100)

    def table(entries):
        return jnp.array([64 * i + j for i, j in (none if e is None else e for e in entries)], jnp.int32)

    even_row = lax.axis_index("rows") % 2 == 0
    wanted = jnp.where(even_row, table(even_codes), table(odd_codes))
    codes = (pairs[:, 0] - base) * 64 + (pairs[:, 1] - base)
    hit = (codes[None, :] == wanted[:, None]) & (pairs[None, :, 0] >= 0)
    return jnp.any(hit, axis=1).astype(jnp.int32)


SLOTS = [(0, 0), (0, 1), (1, 0), (1, 1)]


def own_flags_and_list(pair_list, base):
    own = jnp.concatenate([pair_list, swap(pair_list)], axis=0)
    before = lax.ppermute(own, "rows", [(r, r + 1) for r in range(lax.axis_size("rows") - 1)])
    within, idle = [(0, 0), (0, 1), (1, 1)], [None] * 4
    flags = live_flags(
        own, base,
        within + [(left, 2 + right) for left, right in SLOTS] + idle,
        within + idle + [(right, 2 + left) for left, right in SLOTS],
    )
    return flags, before


def flags_of_far(before, base):
    return live_flags(
        before, base,
        [(left - 2, 2 + right) for left, right in SLOTS],
        [(right - 2, 2 + left) for left, right in SLOTS],
    )


def spread(done, own0, own1, out_odd, even0, even1):
    from_odd = to_odd(out_odd)
    from_even = to_even(even0 + swap(even1))
    return done, own0, swap(own1), from_even, from_odd


def sum_over_chips(*values):
    planes = [[(x * PLANES + z) * RING + y for x in range(ACROSS) for y in range(RING)] for z in range(PLANES)]
    lines = [[(x * PLANES + z) * RING + y for z in range(PLANES)] for x in range(ACROSS) for y in range(RING)]
    for groups in (planes, lines):
        copies = call(copies_kernel, shape((len(groups[0]), 32, 128)), 10**5, 10**5)(
            in_specs=[VMEM] * len(values)
        )(*values)
        values = [
            lax.all_to_all(copies, "rows", 0, 0, axis_index_groups=groups, tiled=True)
        ]
    return values[0].sum(0)


def local(embeddings, test_matrix, pair_list):
    rows_dev = embeddings.shape[0]
    columns = test_matrix.shape[1]
    bf16, f32 = jnp.bfloat16, jnp.float32
    core = lax.axis_index("cols").astype(jnp.int32)
    core_ref = core.reshape(1)
    base = (lax.axis_index("rows") * 2).astype(jnp.int32)
    scale = 1.0 / (rows_dev * lax.axis_size("rows"))

    test_columns = pltpu.with_memory_space_constraint(test_matrix.T, pltpu.HBM)
    embeddings = pltpu.with_memory_space_constraint(embeddings, pltpu.HBM)

    def packet(relative):
        return call(
            functools.partial(packet_kernel, relative), shape((2, 1792, 128), bf16), 10**4, 10**4,
        )(
            in_specs=[SMEM, HBM, HBM],
            scratch_shapes=[
                pltpu.VMEM((2, HALF, 384), bf16),
                pltpu.VMEM((2, columns, HALF), bf16),
                pltpu.SemaphoreType.DMA((6,)),
            ],
        )(core_ref, embeddings, test_columns)

    own0 = packet(0)
    even0 = to_even(own0)
    odd0 = to_odd(own0)
    own1, pair_list = lax.optimization_barrier((packet(1), pair_list))
    flags, before = own_flags_and_list(pair_list, base)

    sum_shape = shape((2, 64, HALF))

    def tiles(count):
        return shape((count, 2, HALF, HALF), bf16)

    tiles_own, done, own_part0, own_part1 = call(
        functools.partial(local_kernel, True), (tiles(3),) + 3 * (sum_shape,), 10**4, 10**4
    )(in_specs=[SMEM] + [VMEM] * 2)(flags, own0, own1)
    done, even0 = lax.optimization_barrier((done, even0))
    even1 = swap_blocks(even0)
    tiles_early, done, even_part0, even_part1 = call(
        functools.partial(early_kernel, True), (tiles(4),) + 3 * (sum_shape,), 10**4, 10**4
    )(in_specs=[SMEM] + [VMEM] * 4)(flags, own0, even0, even1, done)
    done, odd0, before = lax.optimization_barrier((done, odd0, before))
    far_flags = flags_of_far(before, base)
    tiles_late, out_odd, own_part0, own_part1, even_part0, even_part1 = call(
        functools.partial(late_kernel, True), (tiles(8),) + 5 * (sum_shape,), 10**9, 10**6
    )(in_specs=[SMEM] * 2 + [VMEM] * 9)(
        flags, far_flags, odd0, own0, own1, even0, even1, own_part0, own_part1, even_part0, even_part1
    )
    *known, from_odd = spread(done, own_part0, own_part1, out_odd, even_part0, even_part1)
    partial = call(sum_kernel, sum_shape, 10**4, 10**4)(in_specs=[VMEM] * 4)(*known)
    odd_partial, odd_ours = to_odd(partial), out_odd
    sketch, pair0 = call(total_kernel, (sum_shape, shape((2, 128, HALF), bf16)), 10**4, 10**4)(
        in_specs=[VMEM] * 2
    )(partial, from_odd)
    even0 = to_even(pair0)
    gram_shape = shape((32, 128))
    first_gram = call(functools.partial(gram_kernel, scale), gram_shape, 10**4, 10**4)(
        in_specs=[VMEM]
    )(sketch)
    odd0 = call(pair_kernel, shape((2, 128, HALF), bf16), 10**4, 10**4)(in_specs=[VMEM] * 2)(
        odd_partial, odd_ours
    )
    pair1, odd0 = lax.optimization_barrier((swap(pair0), odd0))
    done, own_part0, own_part1 = call(
        functools.partial(local_kernel, False), 3 * (sum_shape,), 10**11, 10**4
    )(in_specs=[SMEM] + [VMEM] * 3)(flags, tiles_own, pair0, pair1)
    done, even0 = lax.optimization_barrier((done, even0))
    even1 = swap_blocks(even0)
    done, even_part0, even_part1 = call(
        functools.partial(early_kernel, False), 3 * (sum_shape,), 10**4, 10**4
    )(in_specs=[SMEM] + [VMEM] * 5)(flags, tiles_early, pair0, even0, even1, done)
    out_odd, own_part0, own_part1, even_part0, even_part1 = call(
        functools.partial(late_kernel, False), 5 * (sum_shape,), 10**9, 10**6
    )(in_specs=[SMEM] * 2 + [VMEM] * 10)(
        flags, far_flags, tiles_late, odd0, pair0, pair1, even0, even1,
        own_part0, own_part1, even_part0, even_part1,
    )
    image = call(sum_kernel, sum_shape, 10**6, 2 * 10**6)(in_specs=[VMEM] * 5)(
        *spread(done, own_part0, own_part1, out_odd, even_part0, even_part1)
    )
    keep, gram_give, half = call(
        functools.partial(second_gram_kernel, scale),
        (gram_shape, gram_shape, shape((64, HALF))),
        10**8, 10**6,
    )(in_specs=[SMEM, VMEM, VMEM])(core_ref, first_gram, image)
    got = swap(half)
    mine = sum_over_chips(keep, swap(gram_give))
    other = swap(mine)
    basis, factor = call(finish_kernel, (shape((64, BLK)), shape((64, 64))), 10**8, 10**6)(
        in_specs=[SMEM] + [VMEM] * 4
    )(core_ref, mine, other, image, got)
    return basis.T, factor


def solution(mesh):
    in_specs = (P("rows", None), P("rows", None), P(("rows", "cols"), None))
    out_specs = (P(("rows", "cols"), None), P())
    return jax.shard_map(local, mesh=mesh, in_specs=in_specs, out_specs=out_specs, check_vma=False)
```

```python
import functools

import jax
import jax.numpy as jnp
from jax import lax
from jax.experimental import pallas as pl
from jax.experimental.pallas import tpu as pltpu
from jax.sharding import PartitionSpec as P

BLK = 1024
HALF = 512
SHARPNESS = 6.0
EPSILON = 1e-06
LOG2E = 1.4426950408889634
HIGHEST = lax.Precision.HIGHEST
VMEM = pl.BlockSpec(memory_space=pltpu.VMEM)
HBM = pl.BlockSpec(memory_space=pltpu.HBM)
SMEM = pl.BlockSpec(memory_space=pltpu.SMEM)
NT = (((1,), (1,)), ((), ()))
NN = (((1,), (0,)), ((), ()))
ACROSS, PLANES, RING = 4, 8, 4


def call(kernel, outs, flops, moved, exps=0, room=16):
    return functools.partial(
        pl.pallas_call,
        kernel,
        out_shape=outs,
        out_specs=jax.tree.map(lambda _: VMEM, outs),
        compiler_params=pltpu.CompilerParams(vmem_limit_bytes=room * 1024 * 1024),
        cost_estimate=pl.CostEstimate(flops=flops, bytes_accessed=moved, transcendentals=exps),
    )


def shape(dims, dtype=jnp.float32):
    return jax.ShapeDtypeStruct(dims, dtype)


def dot(left, right, dims, precision=None):
    return lax.dot_general(
        left, right, dims, precision=precision, preferred_element_type=jnp.float32
    )


def packet_kernel(relative, core_ref, rows_ref, columns_ref, packet_ref, raw_ref, vec_ref, sems):
    side = core_ref[0] if relative == 0 else 1 - core_ref[0]
    copies = []
    for block in range(2):
        start = pl.multiple_of(block * BLK + side * HALF, HALF)
        copies.append((
            pltpu.make_async_copy(rows_ref.at[pl.ds(start, HALF), :], raw_ref.at[block], sems.at[block]),
            pltpu.make_async_copy(
                columns_ref.at[:, pl.ds(start, HALF)], vec_ref.at[block], sems.at[2 + block]
            ),
        ))
        for copy in copies[-1]:
            copy.start()
    for block in range(2):
        for copy in copies[block]:
            copy.wait()
        widened = raw_ref[block].astype(jnp.float32)
        inverse = lax.rsqrt(jnp.sum(widened * widened, axis=1, keepdims=True) + EPSILON)
        unit = (widened * inverse).astype(jnp.bfloat16)
        for tile in range(3):
            packet_ref[block, HALF * tile : HALF * (tile + 1)] = unit[:, 128 * tile : 128 * (tile + 1)]
        for tile in range(4):
            packet_ref[block, 1536 + 64 * tile : 1600 + 64 * tile] = vec_ref[
                block, :, 128 * tile : 128 * (tile + 1)
            ]


def unit_rows(packet, start, count):
    return jnp.concatenate(
        [packet[HALF * tile + start : HALF * tile + start + count] for tile in range(3)], axis=1
    )


def vectors(packet):
    return jnp.concatenate([packet[1536 + 64 * tile : 1600 + 64 * tile] for tile in range(4)], axis=1)


def affinity_tile(left, right):
    scores = dot(left, right, NT)
    return jnp.exp2((SHARPNESS * LOG2E) * scores - (SHARPNESS * LOG2E)).astype(jnp.bfloat16)


def fold(product):
    if product.shape[0] == 128:
        return product[:64] + product[64:]
    return product


def make_tiles(left, rights, tile_ref, slot):
    for side in range(2):
        for at in range(0, HALF, 256):
            right = unit_rows(rights[side], at, 256)
            for row in range(0, HALF, 256):
                tile_ref[slot, side, row : row + 256, at : at + 256] = affinity_tile(
                    unit_rows(left, row, 256), right
                )


def use_tiles(tile_ref, slot, rights, left, done_ref, done_at, part_refs, part_at, partial):
    total = fold(dot(rights[0], tile_ref[slot, 0], NT)) + fold(dot(rights[1], tile_ref[slot, 1], NT))
    done_ref[done_at] += total

    def put_part():
        for side in range(2):
            part_refs[side][part_at] += fold(dot(left, tile_ref[slot, side], NN))

    if partial is None:
        put_part()
    else:
        pl.when(partial)(put_part)


def one_pair(make, tile_ref, slot, left, rights, done_ref, done_at, part_refs, part_at, partial=None):
    take = vectors if make else (lambda ref: ref[...])
    if make:
        make_tiles(left, rights, tile_ref, slot)
    use_tiles(
        tile_ref, slot, (take(rights[0]), take(rights[1])), take(left),
        done_ref, done_at, part_refs, part_at, partial,
    )


def local_kernel(make, flags_ref, *refs):
    if make:
        own0, own1, tile_ref, done_ref, part0, part1 = refs
    else:
        tile_ref, own0, own1, done_ref, part0, part1 = refs
    for ref in (done_ref, part0, part1):
        ref[...] = jnp.zeros_like(ref)

    @pl.loop(0, 3)
    def _(slot):
        first, second = slot // 2, (slot + 1) // 2

        @pl.when(flags_ref[slot] > 0)
        def _():
            one_pair(
                make, tile_ref, slot, own0.at[first], (own0.at[second], own1.at[second]),
                done_ref, first, (part0, part1), second, slot == 1,
            )


def early_kernel(make, flags_ref, *refs):
    if make:
        own0, even0, even1, started, tile_ref, done_ref, part0, part1 = refs
    else:
        tile_ref, own0, even0, even1, started, done_ref, part0, part1 = refs
    done_ref[...] = started[...]
    for ref in (part0, part1):
        ref[...] = jnp.zeros_like(ref)

    @pl.loop(0, 4)
    def _(slot):
        left, right = slot // 2, slot % 2

        @pl.when(flags_ref[3 + slot] > 0)
        def _():
            one_pair(
                make, tile_ref, slot, own0.at[left], (even0.at[right], even1.at[right]),
                done_ref, left, (part0, part1), right,
            )


def late_kernel(make, flags_ref, far_ref, *refs):
    if make:
        odd0, own0, own1, even0, even1, *ins = refs[:9]
        tile_ref, done_ref, *parts = refs[9:]
    else:
        tile_ref, odd0, own0, own1, even0, even1, *ins = refs[:10]
        done_ref, *parts = refs[10:]
    done_ref[...] = jnp.zeros_like(done_ref)
    for ref, value in zip(parts, ins):
        ref[...] = value[...]
    for kind in range(2):
        rights = ((own0, own1), (even0, even1))[kind]
        part_refs = (parts[:2], parts[2:])[kind]
        flag_ref, flag_at = ((flags_ref, 7), (far_ref, 0))[kind]

        @pl.loop(0, 4)
        def _(index):
            left, right = index // 2, index % 2

            @pl.when(flag_ref[flag_at + index] > 0)
            def _():
                one_pair(
                    make, tile_ref, kind * 4 + index, odd0.at[left],
                    (rights[0].at[right], rights[1].at[right]), done_ref, left, part_refs, right,
                )


def total_kernel(done, part_mine, part_other, from_odd, from_even, sum_ref, pair_ref=None):
    for block in range(2):
        value = (
            done[block] + part_mine[block] + part_other[block] + from_odd[block] + from_even[block]
        )
        sum_ref[block] = value
        if pair_ref is not None:
            high = value.astype(jnp.bfloat16)
            pair_ref[block, :64] = high
            pair_ref[block, 64:] = (value - high.astype(jnp.float32)).astype(jnp.bfloat16)


def gram_of(value_ref, scale):
    gram = dot(value_ref[0], value_ref[0], NT, HIGHEST) + dot(value_ref[1], value_ref[1], NT, HIGHEST)
    gram = gram * scale
    return jnp.concatenate([gram[:32], gram[32:]], axis=1)


def gram_kernel(scale, value_ref, gram_ref):
    gram_ref[...] = gram_of(value_ref, scale)


def second_gram_kernel(scale, core_ref, first_ref, value_ref, keep_ref, give_ref, swap_ref):
    second = gram_of(value_ref, scale)
    first = first_ref[...]
    lead = core_ref[0] == 0
    keep_ref[...] = jnp.where(lead, first, second)
    give_ref[...] = jnp.where(lead, second, first)
    swap_ref[...] = value_ref[1 - core_ref[0]]


def eliminate(packed):
    lanes = lax.broadcasted_iota(jnp.int32, (8, 64), 1)
    subs = lax.broadcasted_iota(jnp.int32, (8, 64), 0)
    deep = lax.broadcasted_iota(jnp.int32, (8, 128), 0)
    states = []
    for matrix in packed:
        whole = jnp.concatenate([matrix[:, :64], matrix[:, 64:]], axis=0)
        states.append([
            jnp.concatenate(
                [whole[8 * b : 8 * b + 8], (lanes == subs + 8 * b).astype(jnp.float32)], axis=1
            )
            for b in range(8)
        ])
    scales = [[] for _ in states]
    for at in range(8):
        spreads = [
            {
                b: [jnp.broadcast_to(state[b][:, k : k + 1], (8, 128)) for k in range(8 * at, 8 * at + 8)]
                for b in range(at, 8)
            }
            for state in states
        ]
        pivots = [jnp.zeros((8, 128), jnp.float32) for _ in states]
        for sub in range(8):
            for n, (state, spread_of) in enumerate(zip(states, spreads)):
                pivot = spread_of[at][sub][sub : sub + 1, :]
                inverse = 1.0 / pivot
                pivots[n] = jnp.where(deep == sub, pivot, pivots[n])
                row = state[at][sub : sub + 1, :] * inverse
                ahead = {j: spread_of[at][j][sub : sub + 1, :] * inverse for j in range(sub + 1, 8)}
                for b in range(at, 8):
                    column = spread_of[b][sub]
                    if b == at:
                        column = jnp.where(deep > sub, column, 0.0)
                    for j, value in ahead.items():
                        spread_of[b][j] = spread_of[b][j] - column * value
                    state[b] = state[b] - column * row
        for n, pivot in enumerate(pivots):
            scales[n].append(lax.rsqrt(pivot))
    uppers, inverses = [], []
    for state, scale in zip(states, scales):
        whole = jnp.concatenate([rows * by for rows, by in zip(state, scale)], axis=0)
        uppers.append(whole[:, :64])
        inverses.append(whole[:, 64:])
    return uppers, inverses


def copies_kernel(*refs):
    *value_refs, copies_ref = refs
    total = None
    for ref in value_refs:
        value = ref[...] if len(ref.shape) == 2 else jnp.sum(ref[...], axis=0)
        total = value if total is None else total + value
    for at in range(copies_ref.shape[0]):
        copies_ref[at] = total


def finish_kernel(core_ref, mine_ref, other_ref, value_ref, got_ref, basis_ref, factor_ref):
    core = core_ref[0]
    lead = core == 0
    mine, other = mine_ref[...], other_ref[...]
    first, second = jnp.where(lead, mine, other), jnp.where(lead, other, mine)
    uppers, inverses = eliminate([first, second])
    factor = dot(uppers[1], inverses[0], NT, HIGHEST)
    wide = lax.broadcasted_iota(jnp.int32, (64, 64), 1)
    tall = lax.broadcasted_iota(jnp.int32, (64, 64), 0)
    factor_ref[...] = jnp.where(wide >= tall, factor, 0.0)
    low = jnp.where(wide <= tall, inverses[1], 0.0)
    here = pl.multiple_of(core * HALF, HALF)
    there = pl.multiple_of((1 - core) * HALF, HALF)
    basis_ref[:, pl.ds(here, HALF)] = dot(low, value_ref[core], NN, HIGHEST)
    basis_ref[:, pl.ds(there, HALF)] = dot(low, got_ref[...], NN, HIGHEST)


def exchange(value, start):
    links = []
    for r in range(start, lax.axis_size("rows") - 1, 2):
        links += [(r, r + 1), (r + 1, r)]
    return lax.ppermute(value, "rows", links)


def to_even(value):
    return exchange(value, 0)


def to_odd(value):
    return exchange(value, 1)


def swap(value):
    return lax.ppermute(value, "cols", [(0, 1), (1, 0)])


def swap_blocks(value):
    return jnp.stack([swap(value[block]) for block in range(2)])


def live_flags(pairs, base, even_codes, odd_codes):
    none = (100, 100)

    def table(entries):
        return jnp.array([64 * i + j for i, j in (none if e is None else e for e in entries)], jnp.int32)

    even_row = lax.axis_index("rows") % 2 == 0
    wanted = jnp.where(even_row, table(even_codes), table(odd_codes))
    codes = (pairs[:, 0] - base) * 64 + (pairs[:, 1] - base)
    hit = (codes[None, :] == wanted[:, None]) & (pairs[None, :, 0] >= 0)
    return jnp.any(hit, axis=1).astype(jnp.int32)


SLOTS = [(0, 0), (0, 1), (1, 0), (1, 1)]


def own_flags_and_list(pair_list, base):
    own = jnp.concatenate([pair_list, swap(pair_list)], axis=0)
    before = lax.ppermute(own, "rows", [(r, r + 1) for r in range(lax.axis_size("rows") - 1)])
    within, idle = [(0, 0), (0, 1), (1, 1)], [None] * 4
    flags = live_flags(
        own, base,
        within + [(left, 2 + right) for left, right in SLOTS] + idle,
        within + idle + [(right, 2 + left) for left, right in SLOTS],
    )
    return flags, before


def flags_of_far(before, base):
    return live_flags(
        before, base,
        [(left - 2, 2 + right) for left, right in SLOTS],
        [(right - 2, 2 + left) for left, right in SLOTS],
    )


def spread(done, own0, own1, out_odd, even0, even1):
    from_odd = to_odd(out_odd)
    from_even = to_even(even0 + swap(even1))
    return done, own0, swap(own1), from_odd, from_even


def sum_over_chips(*values):
    planes = [[(x * PLANES + z) * RING + y for x in range(ACROSS) for y in range(RING)] for z in range(PLANES)]
    lines = [[(x * PLANES + z) * RING + y for z in range(PLANES)] for x in range(ACROSS) for y in range(RING)]
    for groups in (planes, lines):
        copies = call(copies_kernel, shape((len(groups[0]), 32, 128)), 10**5, 10**5)(
            in_specs=[VMEM] * len(values)
        )(*values)
        values = [
            lax.all_to_all(copies, "rows", 0, 0, axis_index_groups=groups, tiled=True)
        ]
    return values[0].sum(0)


def local(embeddings, test_matrix, pair_list):
    rows_dev = embeddings.shape[0]
    columns = test_matrix.shape[1]
    bf16, f32 = jnp.bfloat16, jnp.float32
    core = lax.axis_index("cols").astype(jnp.int32)
    core_ref = core.reshape(1)
    base = (lax.axis_index("rows") * 2).astype(jnp.int32)
    scale = 1.0 / (rows_dev * lax.axis_size("rows"))

    test_columns = pltpu.with_memory_space_constraint(test_matrix.T, pltpu.HBM)
    embeddings = pltpu.with_memory_space_constraint(embeddings, pltpu.HBM)

    def packet(relative):
        return call(
            functools.partial(packet_kernel, relative), shape((2, 1792, 128), bf16), 10**4, 10**4,
        )(
            in_specs=[SMEM, HBM, HBM],
            scratch_shapes=[
                pltpu.VMEM((2, HALF, 384), bf16),
                pltpu.VMEM((2, columns, HALF), bf16),
                pltpu.SemaphoreType.DMA((4,)),
            ],
        )(core_ref, embeddings, test_columns)

    own0 = packet(0)
    even0 = to_even(own0)
    odd0 = to_odd(own0)
    own1, pair_list = lax.optimization_barrier((packet(1), pair_list))
    flags, before = own_flags_and_list(pair_list, base)

    sum_shape = shape((2, 64, HALF))

    def tiles(count):
        return shape((count, 2, HALF, HALF), bf16)

    tiles_own, done, own_part0, own_part1 = call(
        functools.partial(local_kernel, True), (tiles(3),) + 3 * (sum_shape,), 10**4, 10**4
    )(in_specs=[SMEM] + [VMEM] * 2)(flags, own0, own1)
    done, even0 = lax.optimization_barrier((done, even0))
    even1 = swap_blocks(even0)
    tiles_early, done, even_part0, even_part1 = call(
        functools.partial(early_kernel, True), (tiles(4),) + 3 * (sum_shape,), 10**4, 10**4
    )(in_specs=[SMEM] + [VMEM] * 4)(flags, own0, even0, even1, done)
    done, odd0, before = lax.optimization_barrier((done, odd0, before))
    far_flags = flags_of_far(before, base)
    tiles_late, out_odd, own_part0, own_part1, even_part0, even_part1 = call(
        functools.partial(late_kernel, True), (tiles(8),) + 5 * (sum_shape,), 10**9, 10**6
    )(in_specs=[SMEM] * 2 + [VMEM] * 9)(
        flags, far_flags, odd0, own0, own1, even0, even1, own_part0, own_part1, even_part0, even_part1
    )
    sketch, pair0 = call(total_kernel, (sum_shape, shape((2, 128, HALF), bf16)), 10**6, 2 * 10**6)(
        in_specs=[VMEM] * 5
    )(*spread(done, own_part0, own_part1, out_odd, even_part0, even_part1))

    even0 = to_even(pair0)
    odd0 = to_odd(pair0)
    gram_shape = shape((32, 128))
    first_gram = call(functools.partial(gram_kernel, scale), gram_shape, 10**4, 10**4)(
        in_specs=[VMEM]
    )(sketch)
    pair1 = swap(pair0)
    done, own_part0, own_part1 = call(
        functools.partial(local_kernel, False), 3 * (sum_shape,), 10**4, 10**4
    )(in_specs=[SMEM] + [VMEM] * 3)(flags, tiles_own, pair0, pair1)
    even1 = swap_blocks(even0)
    done, even_part0, even_part1 = call(
        functools.partial(early_kernel, False), 3 * (sum_shape,), 10**4, 10**4
    )(in_specs=[SMEM] + [VMEM] * 5)(flags, tiles_early, pair0, even0, even1, done)
    done, odd0 = lax.optimization_barrier((done, odd0))
    out_odd, own_part0, own_part1, even_part0, even_part1 = call(
        functools.partial(late_kernel, False), 5 * (sum_shape,), 10**9, 10**6
    )(in_specs=[SMEM] * 2 + [VMEM] * 10)(
        flags, far_flags, tiles_late, odd0, pair0, pair1, even0, even1,
        own_part0, own_part1, even_part0, even_part1,
    )
    image = call(total_kernel, sum_shape, 10**6, 2 * 10**6)(in_specs=[VMEM] * 5)(
        *spread(done, own_part0, own_part1, out_odd, even_part0, even_part1)
    )
    keep, give, half = call(
        functools.partial(second_gram_kernel, scale),
        (gram_shape, gram_shape, shape((64, HALF))),
        10**8, 10**6,
    )(in_specs=[SMEM, VMEM, VMEM])(core_ref, first_gram, image)
    got = swap(half)
    mine = sum_over_chips(keep, swap(give))
    other = swap(mine)
    basis, factor = call(finish_kernel, (shape((64, BLK)), shape((64, 64))), 10**8, 10**6)(
        in_specs=[SMEM] + [VMEM] * 4
    )(core_ref, mine, other, image, got)
    return basis.T, factor


def solution(mesh):
    in_specs = (P("rows", None), P("rows", None), P(("rows", "cols"), None))
    out_specs = (P(("rows", "cols"), None), P())
    return jax.shard_map(local, mesh=mesh, in_specs=in_specs, out_specs=out_specs, check_vma=False)
```

```python
import functools

import jax
import jax.numpy as jnp
from jax import lax
from jax.experimental import pallas as pl
from jax.experimental.pallas import tpu as pltpu
from jax.sharding import PartitionSpec as P

BLK = 1024
HALF = 512
SHARPNESS = 6.0
EPSILON = 1e-06
LOG2E = 1.4426950408889634
HIGHEST = lax.Precision.HIGHEST
VMEM = pl.BlockSpec(memory_space=pltpu.VMEM)
HBM = pl.BlockSpec(memory_space=pltpu.HBM)
SMEM = pl.BlockSpec(memory_space=pltpu.SMEM)
NT = (((1,), (1,)), ((), ()))
NN = (((1,), (0,)), ((), ()))
ACROSS, PLANES, RING = 4, 8, 4


def call(kernel, outs, flops, moved, exps=0, room=16):
    return functools.partial(
        pl.pallas_call,
        kernel,
        out_shape=outs,
        out_specs=jax.tree.map(lambda _: VMEM, outs),
        compiler_params=pltpu.CompilerParams(vmem_limit_bytes=room * 1024 * 1024),
        cost_estimate=pl.CostEstimate(flops=flops, bytes_accessed=moved, transcendentals=exps),
    )


def shape(dims, dtype=jnp.float32):
    return jax.ShapeDtypeStruct(dims, dtype)


def dot(left, right, dims, precision=None):
    return lax.dot_general(
        left, right, dims, precision=precision, preferred_element_type=jnp.float32
    )


def packet_kernel(relative, core_ref, rows_ref, columns_ref, packet_ref, raw_ref, vec_ref, sems):
    side = core_ref[0] if relative == 0 else 1 - core_ref[0]
    copies = []
    for block in range(2):
        start = pl.multiple_of(block * BLK + side * HALF, HALF)
        copies.append((
            pltpu.make_async_copy(rows_ref.at[pl.ds(start, HALF), :], raw_ref.at[block], sems.at[block]),
            pltpu.make_async_copy(
                columns_ref.at[:, pl.ds(start, HALF)], vec_ref.at[block], sems.at[2 + block]
            ),
        ))
        for copy in copies[-1]:
            copy.start()
    for block in range(2):
        for copy in copies[block]:
            copy.wait()
        widened = raw_ref[block].astype(jnp.float32)
        inverse = lax.rsqrt(jnp.sum(widened * widened, axis=1, keepdims=True) + EPSILON)
        unit = (widened * inverse).astype(jnp.bfloat16)
        for tile in range(3):
            packet_ref[block, HALF * tile : HALF * (tile + 1)] = unit[:, 128 * tile : 128 * (tile + 1)]
        for tile in range(4):
            packet_ref[block, 1536 + 64 * tile : 1600 + 64 * tile] = vec_ref[
                block, :, 128 * tile : 128 * (tile + 1)
            ]


def unit_rows(packet, start, count):
    return jnp.concatenate(
        [packet[HALF * tile + start : HALF * tile + start + count] for tile in range(3)], axis=1
    )


def vectors(packet):
    return jnp.concatenate([packet[1536 + 64 * tile : 1600 + 64 * tile] for tile in range(4)], axis=1)


def affinity_tile(left, right):
    scores = dot(left, right, NT)
    return jnp.exp2((SHARPNESS * LOG2E) * scores - (SHARPNESS * LOG2E)).astype(jnp.bfloat16)


def fold(product):
    if product.shape[0] == 128:
        return product[:64] + product[64:]
    return product


def make_tiles(left, rights, tile_ref, slot):
    for side in range(2):
        for at in range(0, HALF, 256):
            right = unit_rows(rights[side], at, 256)
            for row in range(0, HALF, 256):
                tile_ref[slot, side, row : row + 256, at : at + 256] = affinity_tile(
                    unit_rows(left, row, 256), right
                )


def use_tiles(tile_ref, slot, rights, left, done_ref, done_at, part_refs, part_at, partial):
    total = fold(dot(rights[0], tile_ref[slot, 0], NT)) + fold(dot(rights[1], tile_ref[slot, 1], NT))
    done_ref[done_at] += total

    def put_part():
        for side in range(2):
            part_refs[side][part_at] += fold(dot(left, tile_ref[slot, side], NN))

    if partial is None:
        put_part()
    else:
        pl.when(partial)(put_part)


def one_pair(make, tile_ref, slot, left, rights, done_ref, done_at, part_refs, part_at, partial=None):
    take = vectors if make else (lambda ref: ref[...])
    if make:
        make_tiles(left, rights, tile_ref, slot)
    use_tiles(
        tile_ref, slot, (take(rights[0]), take(rights[1])), take(left),
        done_ref, done_at, part_refs, part_at, partial,
    )


def local_kernel(make, flags_ref, *refs):
    if make:
        own0, own1, tile_ref, done_ref, part0, part1 = refs
    else:
        tile_ref, own0, own1, done_ref, part0, part1 = refs
    for ref in (done_ref, part0, part1):
        ref[...] = jnp.zeros_like(ref)

    @pl.loop(0, 3)
    def _(slot):
        first, second = slot // 2, (slot + 1) // 2

        @pl.when(flags_ref[slot] > 0)
        def _():
            one_pair(
                make, tile_ref, slot, own0.at[first], (own0.at[second], own1.at[second]),
                done_ref, first, (part0, part1), second, slot == 1,
            )


def early_kernel(make, flags_ref, *refs):
    if make:
        own0, even0, even1, started, tile_ref, done_ref, part0, part1 = refs
    else:
        tile_ref, own0, even0, even1, started, done_ref, part0, part1 = refs
    done_ref[...] = started[...]
    for ref in (part0, part1):
        ref[...] = jnp.zeros_like(ref)

    @pl.loop(0, 4)
    def _(slot):
        left, right = slot // 2, slot % 2

        @pl.when(flags_ref[3 + slot] > 0)
        def _():
            one_pair(
                make, tile_ref, slot, own0.at[left], (even0.at[right], even1.at[right]),
                done_ref, left, (part0, part1), right,
            )


def late_kernel(make, flags_ref, far_ref, *refs):
    if make:
        odd0, own0, own1, even0, even1, *ins = refs[:9]
        tile_ref, done_ref, *parts = refs[9:]
    else:
        tile_ref, odd0, own0, own1, even0, even1, *ins = refs[:10]
        done_ref, *parts = refs[10:]
    done_ref[...] = jnp.zeros_like(done_ref)
    for ref, value in zip(parts, ins):
        ref[...] = value[...]
    for kind in range(2):
        rights = ((own0, own1), (even0, even1))[kind]
        part_refs = (parts[:2], parts[2:])[kind]
        flag_ref, flag_at = ((flags_ref, 7), (far_ref, 0))[kind]

        @pl.loop(0, 4)
        def _(index):
            left, right = index // 2, index % 2

            @pl.when(flag_ref[flag_at + index] > 0)
            def _():
                one_pair(
                    make, tile_ref, kind * 4 + index, odd0.at[left],
                    (rights[0].at[right], rights[1].at[right]), done_ref, left, part_refs, right,
                )


def total_kernel(done, part_mine, part_other, from_odd, from_even, sum_ref, pair_ref=None):
    for block in range(2):
        value = (
            done[block] + part_mine[block] + part_other[block] + from_odd[block] + from_even[block]
        )
        sum_ref[block] = value
        if pair_ref is not None:
            high = value.astype(jnp.bfloat16)
            pair_ref[block, :64] = high
            pair_ref[block, 64:] = (value - high.astype(jnp.float32)).astype(jnp.bfloat16)


def gram_of(value_ref, scale):
    gram = dot(value_ref[0], value_ref[0], NT, HIGHEST) + dot(value_ref[1], value_ref[1], NT, HIGHEST)
    gram = gram * scale
    return jnp.concatenate([gram[:32], gram[32:]], axis=1)


def gram_kernel(scale, value_ref, gram_ref):
    gram_ref[...] = gram_of(value_ref, scale)


def second_gram_kernel(scale, core_ref, first_ref, value_ref, keep_ref, give_ref, swap_ref):
    second = gram_of(value_ref, scale)
    first = first_ref[...]
    lead = core_ref[0] == 0
    keep_ref[...] = jnp.where(lead, first, second)
    give_ref[...] = jnp.where(lead, second, first)
    swap_ref[...] = value_ref[1 - core_ref[0]]


def eliminate(packed):
    lanes = lax.broadcasted_iota(jnp.int32, (8, 64), 1)
    subs = lax.broadcasted_iota(jnp.int32, (8, 64), 0)
    deep = lax.broadcasted_iota(jnp.int32, (8, 128), 0)
    states = []
    for matrix in packed:
        whole = jnp.concatenate([matrix[:, :64], matrix[:, 64:]], axis=0)
        states.append([
            jnp.concatenate(
                [whole[8 * b : 8 * b + 8], (lanes == subs + 8 * b).astype(jnp.float32)], axis=1
            )
            for b in range(8)
        ])
    scales = [[] for _ in states]
    for at in range(8):
        spreads = [
            {
                b: [jnp.broadcast_to(state[b][:, k : k + 1], (8, 128)) for k in range(8 * at, 8 * at + 8)]
                for b in range(at, 8)
            }
            for state in states
        ]
        pivots = [jnp.zeros((8, 128), jnp.float32) for _ in states]
        for sub in range(8):
            for n, (state, spread_of) in enumerate(zip(states, spreads)):
                pivot = spread_of[at][sub][sub : sub + 1, :]
                inverse = 1.0 / pivot
                pivots[n] = jnp.where(deep == sub, pivot, pivots[n])
                row = state[at][sub : sub + 1, :] * inverse
                ahead = {j: spread_of[at][j][sub : sub + 1, :] * inverse for j in range(sub + 1, 8)}
                for b in range(at, 8):
                    column = spread_of[b][sub]
                    if b == at:
                        column = jnp.where(deep > sub, column, 0.0)
                    for j, value in ahead.items():
                        spread_of[b][j] = spread_of[b][j] - column * value
                    state[b] = state[b] - column * row
        for n, pivot in enumerate(pivots):
            scales[n].append(lax.rsqrt(pivot))
    uppers, inverses = [], []
    for state, scale in zip(states, scales):
        whole = jnp.concatenate([rows * by for rows, by in zip(state, scale)], axis=0)
        uppers.append(whole[:, :64])
        inverses.append(whole[:, 64:])
    return uppers, inverses


def copies_kernel(*refs):
    *value_refs, copies_ref = refs
    total = None
    for ref in value_refs:
        value = ref[...] if len(ref.shape) == 2 else jnp.sum(ref[...], axis=0)
        total = value if total is None else total + value
    for at in range(copies_ref.shape[0]):
        copies_ref[at] = total


def finish_kernel(core_ref, mine_ref, other_ref, value_ref, got_ref, basis_ref, factor_ref):
    core = core_ref[0]
    lead = core == 0
    mine, other = mine_ref[...], other_ref[...]
    first, second = jnp.where(lead, mine, other), jnp.where(lead, other, mine)
    uppers, inverses = eliminate([first, second])
    factor = dot(uppers[1], inverses[0], NT, HIGHEST)
    wide = lax.broadcasted_iota(jnp.int32, (64, 64), 1)
    tall = lax.broadcasted_iota(jnp.int32, (64, 64), 0)
    factor_ref[...] = jnp.where(wide >= tall, factor, 0.0)
    low = jnp.where(wide <= tall, inverses[1], 0.0)
    here = pl.multiple_of(core * HALF, HALF)
    there = pl.multiple_of((1 - core) * HALF, HALF)
    basis_ref[:, pl.ds(here, HALF)] = dot(low, value_ref[core], NN, HIGHEST)
    basis_ref[:, pl.ds(there, HALF)] = dot(low, got_ref[...], NN, HIGHEST)


def exchange(value, start):
    links = []
    for r in range(start, lax.axis_size("rows") - 1, 2):
        links += [(r, r + 1), (r + 1, r)]
    return lax.ppermute(value, "rows", links)


def to_even(value):
    return exchange(value, 0)


def to_odd(value):
    return exchange(value, 1)


def swap(value):
    return lax.ppermute(value, "cols", [(0, 1), (1, 0)])


def swap_blocks(value):
    return jnp.stack([swap(value[block]) for block in range(2)])


def live_flags(pairs, base, even_codes, odd_codes):
    none = (100, 100)

    def table(entries):
        return jnp.array([64 * i + j for i, j in (none if e is None else e for e in entries)], jnp.int32)

    even_row = lax.axis_index("rows") % 2 == 0
    wanted = jnp.where(even_row, table(even_codes), table(odd_codes))
    codes = (pairs[:, 0] - base) * 64 + (pairs[:, 1] - base)
    hit = (codes[None, :] == wanted[:, None]) & (pairs[None, :, 0] >= 0)
    return jnp.any(hit, axis=1).astype(jnp.int32)


SLOTS = [(0, 0), (0, 1), (1, 0), (1, 1)]


def own_flags_and_list(pair_list, base):
    own = jnp.concatenate([pair_list, swap(pair_list)], axis=0)
    before = lax.ppermute(own, "rows", [(r, r + 1) for r in range(lax.axis_size("rows") - 1)])
    within, idle = [(0, 0), (0, 1), (1, 1)], [None] * 4
    flags = live_flags(
        own, base,
        within + [(left, 2 + right) for left, right in SLOTS] + idle,
        within + idle + [(right, 2 + left) for left, right in SLOTS],
    )
    return flags, before


def flags_of_far(before, base):
    return live_flags(
        before, base,
        [(left - 2, 2 + right) for left, right in SLOTS],
        [(right - 2, 2 + left) for left, right in SLOTS],
    )


def spread(done, own0, own1, out_odd, even0, even1):
    from_odd = to_odd(out_odd)
    from_even = to_even(even0 + swap(even1))
    return done, own0, swap(own1), from_odd, from_even


def sum_over_chips(*values):
    planes = [[(x * PLANES + z) * RING + y for x in range(ACROSS) for y in range(RING)] for z in range(PLANES)]
    lines = [[(x * PLANES + z) * RING + y for z in range(PLANES)] for x in range(ACROSS) for y in range(RING)]
    for groups in (lines, planes):
        copies = call(copies_kernel, shape((len(groups[0]), 32, 128)), 10**5, 10**5)(
            in_specs=[VMEM] * len(values)
        )(*values)
        values = [
            lax.all_to_all(copies, "rows", 0, 0, axis_index_groups=groups, tiled=True)
        ]
    return values[0].sum(0)


def local(embeddings, test_matrix, pair_list):
    rows_dev = embeddings.shape[0]
    columns = test_matrix.shape[1]
    bf16, f32 = jnp.bfloat16, jnp.float32
    core = lax.axis_index("cols").astype(jnp.int32)
    core_ref = core.reshape(1)
    base = (lax.axis_index("rows") * 2).astype(jnp.int32)
    scale = 1.0 / (rows_dev * lax.axis_size("rows"))

    test_columns = pltpu.with_memory_space_constraint(test_matrix.T, pltpu.HBM)
    embeddings = pltpu.with_memory_space_constraint(embeddings, pltpu.HBM)

    def packet(relative):
        return call(
            functools.partial(packet_kernel, relative), shape((2, 1792, 128), bf16), 10**4, 10**4,
        )(
            in_specs=[SMEM, HBM, HBM],
            scratch_shapes=[
                pltpu.VMEM((2, HALF, 384), bf16),
                pltpu.VMEM((2, columns, HALF), bf16),
                pltpu.SemaphoreType.DMA((4,)),
            ],
        )(core_ref, embeddings, test_columns)

    own0 = packet(0)
    even0 = to_even(own0)
    odd0 = to_odd(own0)
    own1, pair_list = lax.optimization_barrier((packet(1), pair_list))
    flags, before = own_flags_and_list(pair_list, base)

    sum_shape = shape((2, 64, HALF))

    def tiles(count):
        return shape((count, 2, HALF, HALF), bf16)

    tiles_own, done, own_part0, own_part1 = call(
        functools.partial(local_kernel, True), (tiles(3),) + 3 * (sum_shape,), 10**4, 10**4
    )(in_specs=[SMEM] + [VMEM] * 2)(flags, own0, own1)
    done, even0 = lax.optimization_barrier((done, even0))
    even1 = swap_blocks(even0)
    tiles_early, done, even_part0, even_part1 = call(
        functools.partial(early_kernel, True), (tiles(4),) + 3 * (sum_shape,), 10**4, 10**4
    )(in_specs=[SMEM] + [VMEM] * 4)(flags, own0, even0, even1, done)
    done, odd0, before = lax.optimization_barrier((done, odd0, before))
    far_flags = flags_of_far(before, base)
    tiles_late, out_odd, own_part0, own_part1, even_part0, even_part1 = call(
        functools.partial(late_kernel, True), (tiles(8),) + 5 * (sum_shape,), 10**9, 10**6
    )(in_specs=[SMEM] * 2 + [VMEM] * 9)(
        flags, far_flags, odd0, own0, own1, even0, even1, own_part0, own_part1, even_part0, even_part1
    )
    sketch, pair0 = call(total_kernel, (sum_shape, shape((2, 128, HALF), bf16)), 10**6, 2 * 10**6)(
        in_specs=[VMEM] * 5
    )(*spread(done, own_part0, own_part1, out_odd, even_part0, even_part1))

    even0 = to_even(pair0)
    odd0 = to_odd(pair0)
    gram_shape = shape((32, 128))
    first_gram = call(functools.partial(gram_kernel, scale), gram_shape, 10**4, 10**4)(
        in_specs=[VMEM]
    )(sketch)
    pair1 = swap(pair0)
    done, own_part0, own_part1 = call(
        functools.partial(local_kernel, False), 3 * (sum_shape,), 10**4, 10**4
    )(in_specs=[SMEM] + [VMEM] * 3)(flags, tiles_own, pair0, pair1)
    even1 = swap_blocks(even0)
    done, even_part0, even_part1 = call(
        functools.partial(early_kernel, False), 3 * (sum_shape,), 10**4, 10**4
    )(in_specs=[SMEM] + [VMEM] * 5)(flags, tiles_early, pair0, even0, even1, done)
    done, odd0 = lax.optimization_barrier((done, odd0))
    out_odd, own_part0, own_part1, even_part0, even_part1 = call(
        functools.partial(late_kernel, False), 5 * (sum_shape,), 10**9, 10**6
    )(in_specs=[SMEM] * 2 + [VMEM] * 10)(
        flags, far_flags, tiles_late, odd0, pair0, pair1, even0, even1,
        own_part0, own_part1, even_part0, even_part1,
    )
    image = call(total_kernel, sum_shape, 10**6, 2 * 10**6)(in_specs=[VMEM] * 5)(
        *spread(done, own_part0, own_part1, out_odd, even_part0, even_part1)
    )
    keep, give, half = call(
        functools.partial(second_gram_kernel, scale),
        (gram_shape, gram_shape, shape((64, HALF))),
        10**8, 10**6,
    )(in_specs=[SMEM, VMEM, VMEM])(core_ref, first_gram, image)
    got = swap(half)
    mine = sum_over_chips(keep, swap(give))
    other = swap(mine)
    basis, factor = call(finish_kernel, (shape((64, BLK)), shape((64, 64))), 10**8, 10**6)(
        in_specs=[SMEM] + [VMEM] * 4
    )(core_ref, mine, other, image, got)
    return basis.T, factor


def solution(mesh):
    in_specs = (P("rows", None), P("rows", None), P(("rows", "cols"), None))
    out_specs = (P(("rows", "cols"), None), P())
    return jax.shard_map(local, mesh=mesh, in_specs=in_specs, out_specs=out_specs, check_vma=False)
```
